256 devices in a mesh: dp: 4 (over x), space: 16 (over z_lo, y), tm: 4 (over z_hi, core).
Axes of the slice: x: 4, y: 4, z: 8 (z_hi: 2, z_lo: 4; z = z_hi * 4 + z_lo), core: 2. Of those that a mesh axis runs over, the one named last changes fastest.
Arguments:
- inputs: bfloat16 [4, 32, 64, 4096], P('dp', 'tm', None, 'space'), may hold values from -6 to 6
- grad_out: bfloat16 [4, 32, 64, 4096], P('dp', 'tm', None, 'space'), may hold values from -6 to 6
- conv_w: bfloat16 [2, 128, 64], replicated, may hold values from -0.5 to 0.5
- conv_b: float32 [128], replicated, may hold values from -3 to 3
- mix_w: bfloat16 [3, 64, 64], replicated, may hold values from -0.4375 to 0.4375
- mix_b: float32 [64], replicated, may hold values from -3 to 3
- adj_tiles: bfloat16 [32, 8, 128, 128], P('space'), may hold values from -0.1875 to 0.1875
- tile_cols: int32 [32, 8], P('space'), may hold values from 0 to 9, as said below
- send_rows: int32 [16, 16, 64], P('space'), may hold values from 0 to 255
- counts: int32 [16, 16], P('space'), may hold values from 0 to 64, as said below
Outputs:
- outputs: bfloat16 [4, 32, 64, 4096], P('dp', 'tm', None, 'space')
- grad_inputs: bfloat16 [4, 32, 64, 4096], P('dp', 'tm', None, 'space')
- grad_conv_w: float32 [2, 128, 64], replicated
- grad_conv_b: float32 [128], replicated
- grad_mix_w: float32 [3, 64, 64], replicated
- grad_mix_b: float32 [64], replicated
The draws below stay inside these ranges and needn't reach their ends.
Inputs may be any that keep to these rules, and one draw needn't show every extreme that they name: counts[s, s] = 0; counts[0, 1] = 64. `tile_cols`: column blocks below 2 are the part's own sensor blocks, 2 + i the i-th block of 128 received slots in order of source part and slot; in each row block the first 4 ids are below 2, the others are not.
All inputs are finite; a program needn't handle non-finite values.
Results may differ from the reference program's by a relative error of at most 0.0058.
Values may be sent and summed in bfloat16 or wider, within the bound.
A program may use at most 64 MiB of HBM per device.

```python
import math
import jax
import jax.numpy as jnp
from jax import lax

CH = 64
TILE = 128
KT = 8
DILATION_SIZE = 2
NS_DEV = 256
BMAX = 64
RB = 2
HALO = 1024
HB = 8
BATCH = 4
TIME = 32
SENSORS = 4096
CELLS = 524288
N_SPACE = 16


def draw_counts(key, part):
    loaded = jax.random.randint(jax.random.fold_in(key, 11), (N_SPACE, N_SPACE), BMAX // 4, BMAX + 1)
    source = lax.broadcasted_iota(jnp.int32, (N_SPACE, N_SPACE), 0)
    target = lax.broadcasted_iota(jnp.int32, (N_SPACE, N_SPACE), 1)
    filled = jnp.where((source == 0) & (target == 1), BMAX, loaded)
    return jnp.where(target == source, 0, filled).astype(jnp.int32)


def draw_tile_cols(key, part):
    half_slots = KT // 2
    row_total = N_SPACE * RB
    own_cols = jax.random.randint(jax.random.fold_in(key, 21), (row_total, half_slots), 0, RB)
    offsets = jax.random.randint(jax.random.fold_in(key, 22), (N_SPACE,), 0, HB)
    row_ids = lax.broadcasted_iota(jnp.int32, (row_total, half_slots), 0)
    slot_ids = lax.broadcasted_iota(jnp.int32, (row_total, half_slots), 1)
    local_row = row_ids % RB
    own_cols = jnp.where(slot_ids == 0, local_row, own_cols)
    remote_cols = RB + (local_row * half_slots + slot_ids + offsets[row_ids // RB]) % HB
    return jnp.concatenate([own_cols, remote_cols], 1).astype(jnp.int32)


def plant(result, key, low, top_value):
    dims = result.shape
    spot = [jax.random.randint(jax.random.fold_in(key, axis), (), 0, dims[axis]) for axis in range(len(dims))]
    result = result.at[tuple(spot)].set(low)
    longest = dims.index(max(dims))
    spot[longest] = (spot[longest] + 1) % dims[longest]
    return result.at[tuple(spot)].set(top_value)


def steps_of(key, shape, split, smallest, high):
    def one(dim, parts):
        draws = jax.random.uniform(jax.random.fold_in(jax.random.fold_in(key, 6), dim), (parts,), jnp.float32, smallest / len(split), high / len(split))
        return jnp.repeat(jnp.exp(draws), shape[dim] // parts).reshape((-1,) + (1,) * (len(shape) - dim - 1))

    level = one(*split[0])
    for cut in split[1:]:
        level = level * one(*cut)
    return level


def centred(own_key, dims, spread, limit, pieces=(), held_as=jnp.bfloat16):
    loudness = steps_of(own_key, dims, pieces, -0.22, 0.18) if pieces else 1.0
    result = jax.random.normal(own_key, dims, jnp.float32) * spread * loudness
    return jnp.minimum(jnp.maximum(result, -limit), limit).astype(held_as)


def setup_inputs(seed: int = 0) -> dict:
    splits = jax.random.split(jax.random.key(seed), 11)
    inputs = centred(splits[0], (BATCH, TIME, CH, SENSORS), 1.0, 6.0, ((0, 4), (1, 4), (3, 16)))
    grad_out = centred(splits[1], (BATCH, TIME, CH, SENSORS), 1.0, 6.0, ((0, 4), (1, 4), (3, 16)))
    conv_w = centred(splits[2], (2, 2 * CH, CH), (2 * CH) ** -0.5, 0.5)
    conv_b = centred(splits[3], (2 * CH,), 0.5, 3.0, (), jnp.float32)
    mix_w = centred(splits[4], (3, CH, CH), (3 * CH) ** -0.5, 0.4375)
    mix_b = centred(splits[5], (CH,), 0.5, 3.0, (), jnp.float32)
    adj_tiles = centred(splits[6], (N_SPACE * RB, KT, TILE, TILE), (KT * TILE) ** -0.5, 0.1875, ((0, 16),))
    tile_cols = draw_tile_cols(jax.random.fold_in(splits[10], 71), 0)
    send_rows = plant(jax.random.randint(splits[8], (N_SPACE, N_SPACE, BMAX), 0, NS_DEV), jax.random.fold_in(splits[8], 1), 0, NS_DEV - 1).astype(jnp.int32)
    counts = draw_counts(jax.random.fold_in(splits[10], 71), 0)
    return dict(inputs=inputs, grad_out=grad_out, conv_w=conv_w, conv_b=conv_b, mix_w=mix_w, mix_b=mix_b, adj_tiles=adj_tiles, tile_cols=tile_cols, send_rows=send_rows, counts=counts)


def boundary_rows(field, send_rows, counts):
    owners = jnp.arange(N_SPACE, dtype=jnp.int32)
    global_idx = owners[:, None, None] * NS_DEV + send_rows
    slots = jnp.arange(BMAX, dtype=jnp.int32)
    live_slots = (slots[None, None, :] < counts[:, :, None]).astype(field.dtype)
    return field[:, :, global_idx] * live_slots

def diffuse(field, adj_tiles, tile_cols, send_rows, counts):
    timestep_count, chan_count = (field.shape[0], field.shape[1])
    gathered = boundary_rows(field, send_rows, counts)

    def per_part(part):
        local_rows = lax.dynamic_slice_in_dim(field, part * NS_DEV, NS_DEV, 2)
        halo_rows = jnp.take(gathered, part, axis=3).reshape(timestep_count, chan_count, HALO)
        extended = jnp.concatenate([local_rows, halo_rows], axis=2)
        blocks = extended.reshape(timestep_count, chan_count, RB + HB, TILE)
        part_cols = lax.dynamic_slice_in_dim(tile_cols, part * RB, RB, 0)
        part_tiles = lax.dynamic_slice_in_dim(adj_tiles, part * RB, RB, 0).astype(jnp.float32)
        picked = blocks[:, :, part_cols].astype(jnp.float32)
        product = jnp.einsum('tcrkj,rkij->tcri', picked, part_tiles)
        return product.reshape(timestep_count, chan_count, NS_DEV).astype(jnp.bfloat16)
    results = lax.map(per_part, jnp.arange(N_SPACE, dtype=jnp.int32))
    return jnp.transpose(results, (1, 2, 0, 3)).reshape(field.shape)

def diffuse_back(grad, adj_tiles, tile_cols, send_rows, counts):
    timestep_count, chan_count = (grad.shape[0], grad.shape[1])

    def per_part(part):
        local_rows = lax.dynamic_slice_in_dim(grad, part * NS_DEV, NS_DEV, 2)
        blocks = local_rows.reshape(timestep_count, chan_count, RB, TILE).astype(jnp.float32)
        part_cols = lax.dynamic_slice_in_dim(tile_cols, part * RB, RB, 0)
        part_tiles = lax.dynamic_slice_in_dim(adj_tiles, part * RB, RB, 0).astype(jnp.float32)
        product = jnp.einsum('tcri,rkij->tcrkj', blocks, part_tiles)
        extended = jnp.zeros((timestep_count, chan_count, RB + HB, TILE), jnp.float32)
        extended = extended.at[:, :, part_cols].add(product)
        extended = extended.reshape(timestep_count, chan_count, NS_DEV + HALO)
        return (extended[:, :, :NS_DEV], extended[:, :, NS_DEV:].astype(jnp.bfloat16))
    local_parts, halo_parts = lax.map(per_part, jnp.arange(N_SPACE, dtype=jnp.int32))
    total = jnp.transpose(local_parts, (1, 2, 0, 3)).reshape(grad.shape)
    halo_parts = halo_parts.reshape(N_SPACE, timestep_count, chan_count, N_SPACE, BMAX)
    halo_parts = jnp.transpose(halo_parts, (1, 2, 3, 0, 4)).astype(jnp.float32)
    owners = jnp.arange(N_SPACE, dtype=jnp.int32)
    global_idx = owners[:, None, None] * NS_DEV + send_rows
    slots = jnp.arange(BMAX, dtype=jnp.int32)
    live_slots = (slots[None, None, :] < counts[:, :, None]).astype(jnp.float32)
    return total.at[:, :, global_idx].add(halo_parts * live_slots)

def reference(inputs, grad_out, conv_w, conv_b, mix_w, mix_b, adj_tiles, tile_cols, send_rows, counts):
    conv_f = conv_w.astype(jnp.float32)
    mix_f = mix_w.astype(jnp.float32)

    def per_sample(pair):
        sample_input, sample_grad = pair
        timestep_count = sample_input.shape[0]
        zero_border_slice = jnp.zeros((DILATION_SIZE,) + sample_input.shape[1:], jnp.bfloat16)
        preceding_window = jnp.concatenate([zero_border_slice, sample_input[:timestep_count - DILATION_SIZE]], 0)
        input_f = sample_input.astype(jnp.float32)
        previous_f = preceding_window.astype(jnp.float32)
        preact = jnp.einsum('oc,tcn->ton', conv_f[1], input_f) + jnp.einsum('oc,tcn->ton', conv_f[0], previous_f)
        preact = preact + conv_b[None, :, None]
        filtered = jnp.tanh(preact[:, :CH])
        gating = jax.nn.sigmoid(preact[:, CH:])
        hidden = (filtered * gating).astype(jnp.bfloat16)
        hop_one = diffuse(hidden, adj_tiles, tile_cols, send_rows, counts)
        hop_two = diffuse(hop_one, adj_tiles, tile_cols, send_rows, counts)
        fields = (hidden, hop_one, hop_two)
        mixed = mix_b[None, :, None] + input_f
        for index in range(3):
            mixed = mixed + jnp.einsum('oc,tcn->ton', mix_f[index], fields[index].astype(jnp.float32))
        outputs = mixed.astype(jnp.bfloat16)
        grad_f = sample_grad.astype(jnp.float32)
        back_two = jnp.einsum('oc,ton->tcn', mix_f[2], grad_f).astype(jnp.bfloat16)
        back_one = jnp.einsum('oc,ton->tcn', mix_f[1], grad_f) + diffuse_back(back_two, adj_tiles, tile_cols, send_rows, counts)
        back_one = back_one.astype(jnp.bfloat16)
        back_hidden = jnp.einsum('oc,ton->tcn', mix_f[0], grad_f) + diffuse_back(back_one, adj_tiles, tile_cols, send_rows, counts)
        grad_filter = back_hidden * (1.0 - filtered * filtered) * gating
        grad_gate = back_hidden * filtered * gating * (1.0 - gating)
        backward_preactivation = jnp.concatenate([grad_filter, grad_gate], 1).astype(jnp.bfloat16).astype(jnp.float32)
        following_window = jnp.concatenate([backward_preactivation[DILATION_SIZE:], jnp.zeros((DILATION_SIZE,) + backward_preactivation.shape[1:], jnp.float32)], 0)
        grad_inputs = grad_f + jnp.einsum('oc,ton->tcn', conv_f[1], backward_preactivation) + jnp.einsum('oc,ton->tcn', conv_f[0], following_window)
        grad_inputs = grad_inputs.astype(jnp.bfloat16)
        grad_conv_w = jnp.stack([jnp.einsum('ton,tcn->oc', backward_preactivation, previous_f), jnp.einsum('ton,tcn->oc', backward_preactivation, input_f)])
        grad_conv_b = lax.optimization_barrier(jnp.sum(backward_preactivation, axis=(0, 2)))
        grad_mix_w = jnp.stack([jnp.einsum('ton,tcn->oc', grad_f, item.astype(jnp.float32)) for item in fields])
        grad_mix_b = lax.optimization_barrier(jnp.sum(grad_f, axis=(0, 2)))
        return (outputs, grad_inputs, grad_conv_w, grad_conv_b, grad_mix_w, grad_mix_b)
    results = lax.map(per_sample, (inputs, grad_out))
    scale = 1.0 / math.sqrt(CELLS)
    return (results[0], results[1], lax.optimization_barrier(jnp.sum(results[2], 0)) * scale, lax.optimization_barrier(jnp.sum(results[3], 0)) * scale, lax.optimization_barrier(jnp.sum(results[4], 0)) * scale, lax.optimization_barrier(jnp.sum(results[5], 0)) * scale)
```

```python
import functools
import math

import jax
import jax.numpy as jnp
from jax import lax
from jax.experimental import pallas as pl
from jax.experimental.pallas import tpu as pltpu
from jax.sharding import PartitionSpec as P

MESH = pl.DeviceIdType.MESH
F32 = jnp.float32
BF16 = jnp.bfloat16


def nn(a, b):
    return jnp.dot(a, b, preferred_element_type=F32)


def nt(a, b):
    return lax.dot_general(a, b, (((1,), (1,)), ((), ())), preferred_element_type=F32)


def kernel(
    dims,
    x_ref, g_ref, convw_ref, convb_ref, mixw_ref, mixb_ref, adj_ref, cols_ref, idx_ref,
    out_ref, gin_ref, gcw_ref, gcb_ref, gmw_ref, gmb_ref,
    xb, bpb, xt, gt, wt, wtt, mcat, gm, gmt, dm, dmt,
    b2, b1, b1base, b0base, filt, gate, hid, hop1, hop2, bp,
    sq1, sf1, sq2, sf2, rq1, rf1, rq2, rf2,
    pay_c, pay_m, ra_c, ra_m, rb_c, rb_m, fin_c, fin_m, sum_c, sum_m,
    ssem, rsem, assem, arsem, nsem,
):
    n_space, n_dp, n_tm, scale = dims
    me = lax.axis_index("space")
    tm = lax.axis_index("tm")
    dp = lax.axis_index("dp")
    grp = dp * n_tm + tm
    n_grp = n_dp * n_tm

    def space_dev(k):
        return {"space": k}

    def grp_dev(k):
        return {"dp": lax.div(k, n_tm), "tm": lax.rem(k, n_tm)}

    barrier = pltpu.get_barrier_semaphore()

    @pl.loop(1, n_space)
    def _(off):
        pl.semaphore_signal(
            barrier, inc=1, device_id=space_dev(lax.rem(me + off, n_space)), device_id_type=MESH
        )

    @pl.loop(1, n_grp)
    def _(off):
        pl.semaphore_signal(
            barrier, inc=1, device_id=grp_dev(lax.rem(grp + off, n_grp)), device_id_type=MESH
        )

    def exchange(mine, count, dev, src, dst, ss, rs):
        def copy(tgt, frm):
            return pltpu.make_async_remote_copy(
                src_ref=src(tgt), dst_ref=dst(frm), send_sem=ss.at[tgt], recv_sem=rs.at[frm],
                device_id=dev(tgt), device_id_type=MESH,
            )

        def start():
            @pl.loop(1, count)
            def _(off):
                copy(lax.rem(mine + off, count), mine).start()

        def wait_recv():
            @pl.loop(1, count)
            def _(off):
                copy(lax.rem(mine + off, count), lax.rem(mine + (count - off), count)).wait_recv()

        def wait_send():
            @pl.loop(1, count)
            def _(off):
                copy(lax.rem(mine + off, count), mine).wait_send()

        return start, wait_recv, wait_send

    slots = 64

    def rows(ref, size):
        def at(k):
            return ref.at[pl.ds(pl.multiple_of(k * size, size), size), :]

        return at

    def halo(i, send, recv):
        return exchange(
            me, n_space, space_dev, rows(send, slots), rows(recv, slots), ssem.at[i], rsem.at[i]
        )

    q1_start, q1_recv, q1_sent = halo(0, sq1, rq1)
    f1_start, f1_recv, f1_sent = halo(1, sf1, rf1)
    q2_start, q2_recv, q2_sent = halo(2, sq2, rq2)
    f2_start, f2_recv, f2_sent = halo(3, sf2, rf2)

    def next_copy():
        return pltpu.make_async_remote_copy(
            src_ref=x_ref.at[pl.ds(384, 128), :], dst_ref=xb, send_sem=nsem.at[0], recv_sem=nsem.at[1],
            device_id={"tm": lax.rem(tm + 1, n_tm)}, device_id_type=MESH,
        )

    def back_copy():
        return pltpu.make_async_remote_copy(
            src_ref=bp.at[:, pl.ds(0, 256)], dst_ref=bpb, send_sem=nsem.at[2], recv_sem=nsem.at[3],
            device_id={"tm": lax.rem(tm + n_tm - 1, n_tm)}, device_id_type=MESH,
        )

    pl.semaphore_wait(barrier, n_space - 1 + n_grp - 1)

    @pl.when(tm < n_tm - 1)
    def _():
        next_copy().start()

    @pl.when(tm == 0)
    def _():
        xb[...] = jnp.zeros_like(xb)

    @pl.when(tm == n_tm - 1)
    def _():
        bpb[...] = jnp.zeros_like(bpb)

    own_slots = pl.ds(pl.multiple_of(me * slots, slots), slots)
    for ref in (rq1, rf1, rq2, rf2):
        ref[own_slots, :] = jnp.zeros((slots, 512), BF16)

    zero = jnp.zeros((64, 64), F32)

    def pair(w):
        w = w.astype(F32)
        top = jnp.concatenate([w, zero], 1)
        low = jnp.concatenate([zero, w], 1)
        return jnp.concatenate([top, low], 0)

    for k in range(3):
        mcat[:, 128 * k : 128 * (k + 1)] = pair(mixw_ref[k]).astype(BF16)
    for half in range(2):
        for tap in range(2):
            block = pair(convw_ref[tap, 64 * half : 64 * (half + 1), :])
            wt[128 * half : 128 * (half + 1), 128 * tap : 128 * (tap + 1)] = block.astype(BF16)
            wtt[128 * tap : 128 * (tap + 1), 128 * half : 128 * (half + 1)] = block.T.astype(BF16)

    for r in range(2):
        for b in range(10):
            total = None
            for k in range(4):
                slot = k if b < 2 else 4 + k
                hit = (cols_ref[r, slot] == b).astype(F32)
                term = adj_ref[r, slot].astype(F32) * hit
                total = term if total is None else total + term
            dm[128 * r : 128 * (r + 1), 128 * b : 128 * (b + 1)] = total.astype(BF16)
            dmt[128 * b : 128 * (b + 1), 128 * r : 128 * (r + 1)] = total.T.astype(BF16)

    for p in range(4):
        lanes = slice(128 * p, 128 * (p + 1))
        gt[:, lanes] = g_ref[lanes, :].T
        terms = nn(gt[:, lanes], mcat[...])
        b0base[:, lanes] = terms[:, :128]
        b1base[:, lanes] = terms[:, 128:256]
        b2[:, lanes] = terms[:, 256:].astype(BF16)

    def halo_sums(src, dst):
        @pl.loop(0, 4)
        def _(m):
            at = pl.multiple_of(m * 256, 256)
            dst[pl.ds(at, 256), :] = nn(dmt[pl.ds(at + 256, 256), :], src[...]).astype(BF16)

    def pack(src, dst):
        @pl.loop(0, 4)
        def _(m):
            at = pl.multiple_of(m * 256, 256)
            dst[pl.ds(at, 256), :] = nn(gmt[pl.ds(at, 256), :], src[...]).astype(BF16)

    halo_sums(b2, sq1)
    q1_start()

    for m in range(4):
        lanes = slice(256 * m, 256 * (m + 1))
        sensor = lax.broadcasted_iota(jnp.int32, (256, 256), 0)
        block = (sensor == idx_ref[0:1, lanes]).astype(F32)
        gm[:, lanes] = block.astype(BF16)
        gmt[lanes, :] = block.T.astype(BF16)

    for p in range(4):
        xt[:, 128 * (p + 1) : 128 * (p + 2)] = x_ref[128 * p : 128 * (p + 1), :].T

    @pl.when(tm > 0)
    def _():
        next_copy().wait_recv()

    xt[:, 0:128] = xb[...].T
    b = convb_ref[...]
    bias = jnp.concatenate([b[:, :64], b[:, :64], b[:, 64:], b[:, 64:]], 1)
    for p in range(4):
        lanes = slice(128 * p, 128 * (p + 1))
        pre = nt(xt[:, 128 * p : 128 * p + 256], wt[...]) + bias
        f = jnp.tanh(pre[:, :128])
        s = jax.nn.sigmoid(pre[:, 128:])
        filt[:, lanes] = f
        gate[:, lanes] = s
        hid[:, lanes] = (f * s).astype(BF16)
    pack(hid, sf1)
    f1_start()

    q1_recv()
    for m in range(2):
        at = slice(128 * m, 128 * (m + 1))
        b1[at, :] = (b1base[at, :] + nn(dmt[at, :], b2[...]) + nn(gm[at, :], rq1[...])).astype(BF16)
    halo_sums(b1, sq2)
    q2_start()

    f1_recv()
    for m in range(2):
        at = slice(128 * m, 128 * (m + 1))
        hop1[at, :] = (nn(dm[at, :256], hid[...]) + nn(dm[at, 256:], rf1[...])).astype(BF16)
    pack(hop1, sf2)
    f2_start()

    acc0 = acc1 = None
    for p in range(4):
        lanes = slice(128 * p, 128 * (p + 1))
        a0 = nn(g_ref[lanes, :], hid[:, lanes])
        a1 = nn(g_ref[lanes, :], hop1[:, lanes])
        acc0 = a0 if acc0 is None else acc0 + a0
        acc1 = a1 if acc1 is None else acc1 + a1
    low_lanes = lax.broadcasted_iota(jnp.int32, (64, 128), 1) < 64

    def diag_low(a):
        return a[:64] + pltpu.roll(a[64:], 64, 1)

    def diag_high(a):
        return pltpu.roll(a[:64], 64, 1) + a[64:]

    pay_m[0:64, :] = jnp.where(low_lanes, diag_low(acc0), diag_high(acc1))
    gsum = jnp.zeros((1, 128), F32)
    for p in range(4):
        gsum = gsum + jnp.sum(gt[:, 128 * p : 128 * (p + 1)].astype(F32), axis=0, keepdims=True)

    q2_recv()
    bsum = jnp.zeros((1, 256), F32)
    for p in range(4):
        lanes = slice(128 * p, 128 * (p + 1))
        bh = b0base[:, lanes] + nn(dmt[:256, :], b1[:, lanes]) + nn(gm[...], rq2[:, lanes])
        f = filt[:, lanes]
        s = gate[:, lanes]
        gf = (bh * (1.0 - f * f) * s).astype(BF16)
        gg = (bh * f * s * (1.0 - s)).astype(BF16)
        bp[:, 256 * p : 256 * p + 128] = gf
        bp[:, 256 * p + 128 : 256 * (p + 1)] = gg
        if p == 0:
            @pl.when(tm > 0)
            def _():
                back_copy().start()
        bsum = bsum + jnp.concatenate(
            [
                jnp.sum(gf.astype(F32), axis=0, keepdims=True),
                jnp.sum(gg.astype(F32), axis=0, keepdims=True),
            ],
            1,
        )
    acc_prev = nn(xb[...], bp[:, :256])
    acc_cur = nn(x_ref[0:128, :], bp[:, :256])
    for p in range(1, 4):
        lanes = slice(128 * p, 128 * (p + 1))
        wide = slice(256 * p, 256 * (p + 1))
        acc_prev = acc_prev + nn(x_ref[128 * (p - 1) : 128 * p, :], bp[:, wide])
        acc_cur = acc_cur + nn(x_ref[lanes, :], bp[:, wide])
    for tap, acc in ((0, acc_prev), (1, acc_cur)):
        pay_c[64 * tap : 64 * (tap + 1), :] = jnp.where(
            low_lanes, diag_low(acc[:, :128]), diag_high(acc[:, 128:])
        )

    def reduce_calls(i, pay, ra, rb, fin, part):
        chunk = 8
        s1 = exchange(
            me, n_space, space_dev, rows(pay, chunk), rows(ra, chunk), assem.at[3 * i], arsem.at[3 * i]
        )
        s2 = exchange(
            grp, n_grp, grp_dev, lambda k: part.at[0:8, :], rows(rb, chunk),
            assem.at[3 * i + 1], arsem.at[3 * i + 1],
        )
        s3 = exchange(
            me, n_space, space_dev, lambda k: part.at[8:16, :], rows(fin, chunk),
            assem.at[3 * i + 2], arsem.at[3 * i + 2],
        )
        mine = pl.ds(pl.multiple_of(me * chunk, chunk), chunk)
        ours = pl.ds(pl.multiple_of(grp * chunk, chunk), chunk)

        def first():
            ra[mine, :] = pay[mine, :]
            s1[0]()

        def second():
            s1[1]()
            total = ra[0:8, :]
            for k in range(1, n_space):
                total = total + ra[8 * k : 8 * k + 8, :]
            part[0:8, :] = total
            rb[ours, :] = total
            s2[0]()

        def third():
            s2[1]()
            total = rb[0:8, :]
            for k in range(1, n_grp):
                total = total + rb[8 * k : 8 * k + 8, :]
            total = total * scale
            part[8:16, :] = total
            fin[mine, :] = total
            s3[0]()

        def last():
            s3[1]()

        def sent():
            for s in (s1, s2, s3):
                s[2]()

        return first, second, third, last, sent

    c_first, c_second, c_third, c_last, c_sent = reduce_calls(0, pay_c, ra_c, rb_c, fin_c, sum_c)
    m_first, m_second, m_third, m_last, m_sent = reduce_calls(1, pay_m, ra_m, rb_m, fin_m, sum_m)
    c_first()

    def grad_in(p, nxt):
        lanes = slice(128 * p, 128 * (p + 1))
        here = nt(wtt[128:, :], bp[:, 256 * p : 256 * (p + 1)])
        gin_ref[lanes, :] = (g_ref[lanes, :].astype(F32) + here + nt(wtt[:128, :], nxt)).astype(BF16)

    for p in range(3):
        grad_in(p, bp[:, 256 * (p + 1) : 256 * (p + 2)])

    @pl.when(tm < n_tm - 1)
    def _():
        back_copy().wait_recv()

    grad_in(3, bpb[...])
    c_second()

    f2_recv()
    acc2 = None
    for m in range(2):
        at = slice(128 * m, 128 * (m + 1))
        hop2[at, :] = (nn(dm[at, :256], hop1[...]) + nn(dm[at, 256:], rf2[...])).astype(BF16)
    for p in range(4):
        lanes = slice(128 * p, 128 * (p + 1))
        a2 = nn(g_ref[lanes, :], hop2[:, lanes])
        acc2 = a2 if acc2 is None else acc2 + a2
    row = lax.broadcasted_iota(jnp.int32, (64, 128), 0)
    f_sum = bsum[:, :128]
    g_sum = bsum[:, 128:]
    f_sum = f_sum + pltpu.roll(f_sum, 64, 1)
    g_sum = g_sum + pltpu.roll(g_sum, 64, 1)
    o_sum = gsum + pltpu.roll(gsum, 64, 1)
    extra = jnp.where(row == 0, f_sum, jnp.where(row == 1, g_sum, jnp.where(row == 2, o_sum, 0.0)))
    pay_m[64:128, :] = jnp.where(low_lanes, diag_low(acc2), extra)
    m_first()
    c_third()

    mb = mixb_ref[...]
    mb = jnp.concatenate([mb, mb], 1)
    mb = jnp.broadcast_to(mb, (128, 128)).T
    mb = jnp.concatenate([mb, mb], 1)

    def mixed(p):
        lanes = slice(128 * p, 128 * (p + 1))
        total = x_ref[lanes, :].astype(F32) + mb
        for k, field in enumerate((hid, hop1, hop2)):
            total = total + nt(mcat[:, 128 * k : 128 * (k + 1)], field[:, lanes])
        out_ref[lanes, :] = total.astype(BF16)

    mixed(0)
    mixed(1)
    m_second()
    mixed(2)
    mixed(3)
    c_last()
    for tap in range(2):
        gcw_ref[tap] = fin_c[64 * tap : 64 * (tap + 1), :].T
    m_third()
    for s in (q1_sent, f1_sent, q2_sent, f2_sent, c_sent):
        s()

    @pl.when(tm < n_tm - 1)
    def _():
        next_copy().wait_send()

    @pl.when(tm > 0)
    def _():
        back_copy().wait_send()

    m_last()
    gmw_ref[0] = fin_m[0:64, 0:64]
    gmw_ref[1] = pltpu.roll(fin_m[0:64, :], 64, 1)[:, 0:64]
    gmw_ref[2] = fin_m[64:128, 0:64]
    tail = fin_m[64:72, :]
    gcb_ref[...] = jnp.where(low_lanes[0:1], pltpu.roll(tail[0:1], 64, 1), tail[1:2])
    gmb_ref[...] = pltpu.roll(tail[2:3], 64, 1)[:, 0:64]
    m_sent()


def body(dims, inputs, grad_out, conv_w, conv_b, mix_w, mix_b, adj_tiles, tile_cols, send_rows, counts):
    x = inputs.reshape(512, 256)
    g = grad_out.reshape(512, 256)
    slot = lax.broadcasted_iota(jnp.int32, send_rows.shape[1:], 1)
    idx = jnp.where(slot < counts[0][:, None], send_rows[0], -1).reshape(1, -1)
    vmem = pl.BlockSpec(memory_space=pltpu.VMEM)
    smem = pl.BlockSpec(memory_space=pltpu.SMEM)
    n_space = dims[0]
    n_grp = dims[1] * dims[2]

    def bf(*shape):
        return pltpu.VMEM(shape, BF16)

    def fl(*shape):
        return pltpu.VMEM(shape, F32)

    scratch = [
        bf(128, 256), bf(256, 256), bf(256, 640), bf(256, 512), bf(256, 256), bf(256, 256), bf(128, 384),
        bf(256, 1024), bf(1024, 256), bf(256, 1280), bf(1280, 256),
        bf(256, 512), bf(256, 512), fl(256, 512), fl(256, 512), fl(256, 512), fl(256, 512),
        bf(256, 512), bf(256, 512), bf(256, 512), bf(256, 1024),
    ]
    scratch += [bf(1024, 512)] * 8
    scratch += [fl(128, 128)] * 8 + [fl(16, 128)] * 2
    scratch += [
        pltpu.SemaphoreType.DMA((4, n_space)), pltpu.SemaphoreType.DMA((4, n_space)),
        pltpu.SemaphoreType.DMA((6, n_grp)), pltpu.SemaphoreType.DMA((6, n_grp)),
        pltpu.SemaphoreType.DMA((4,)),
    ]
    outs = pl.pallas_call(
        functools.partial(kernel, dims),
        out_shape=(
            jax.ShapeDtypeStruct((512, 256), BF16),
            jax.ShapeDtypeStruct((512, 256), BF16),
            jax.ShapeDtypeStruct((2, 128, 64), F32),
            jax.ShapeDtypeStruct((1, 128), F32),
            jax.ShapeDtypeStruct((3, 64, 64), F32),
            jax.ShapeDtypeStruct((1, 64), F32),
        ),
        in_specs=[vmem] * 7 + [smem, vmem],
        out_specs=(vmem,) * 6,
        scratch_shapes=scratch,
        compiler_params=pltpu.CompilerParams(
            collective_id=0, has_side_effects=True, vmem_limit_bytes=48 * 2**20
        ),
    )(x, g, conv_w, conv_b.reshape(1, 128), mix_w, mix_b.reshape(1, 64), adj_tiles, tile_cols, idx)
    out, gin, gcw, gcb, gmw, gmb = outs
    return (
        out.reshape(inputs.shape),
        gin.reshape(inputs.shape),
        gcw,
        gcb.reshape(128),
        gmw,
        gmb.reshape(64),
    )


def solution(mesh):
    in_specs = (
        P("dp", "tm", None, "space"),
        P("dp", "tm", None, "space"),
        P(),
        P(),
        P(),
        P(),
        P("space", None, None, None),
        P("space", None),
        P("space", None, None),
        P("space", None),
    )
    out_specs = (P("dp", "tm", None, "space"), P("dp", "tm", None, "space"), P(), P(), P(), P())
    cells = 512 * 256 // 64 * mesh.shape["dp"] * mesh.shape["space"] * mesh.shape["tm"]
    dims = (mesh.shape["space"], mesh.shape["dp"], mesh.shape["tm"], 1.0 / math.sqrt(cells))
    return jax.shard_map(
        functools.partial(body, dims), mesh=mesh, in_specs=in_specs, out_specs=out_specs, check_vma=False
    )
```

```python
import functools
import math

import jax
import jax.numpy as jnp
from jax import lax
from jax.experimental import pallas as pl
from jax.experimental.pallas import tpu as pltpu
from jax.sharding import PartitionSpec as P

MESH = pl.DeviceIdType.MESH
F32 = jnp.float32
BF16 = jnp.bfloat16
SLOTS = 64
CHUNK = 16


def nn(a, b):
    return jnp.dot(a, b, preferred_element_type=F32)


def nt(a, b):
    return lax.dot_general(a, b, (((1,), (1,)), ((), ())), preferred_element_type=F32)


def exchange(mine, count, dev, src, dst, ss, rs):
    def copy(tgt, frm):
        return pltpu.make_async_remote_copy(
            src_ref=src(tgt), dst_ref=dst(frm), send_sem=ss.at[tgt], recv_sem=rs.at[frm],
            device_id=dev(tgt), device_id_type=MESH,
        )

    def start():
        @pl.loop(1, count)
        def _(off):
            copy(lax.rem(mine + off, count), mine).start()

    def received():
        @pl.loop(1, count)
        def _(off):
            copy(lax.rem(mine + off, count), lax.rem(mine + (count - off), count)).wait_recv()

    def sent():
        @pl.loop(1, count)
        def _(off):
            copy(lax.rem(mine + off, count), mine).wait_send()

    return copy, start, received, sent


def rows(ref, size):
    return lambda k: ref.at[pl.ds(pl.multiple_of(k * size, size), size), :]


def kernel(
    dims,
    x_hbm, g_hbm, adj_hbm, convw_ref, convb_ref, mixw_ref, mixb_ref, cols_ref, idx_ref,
    out_ref, gin_ref, fin,
    x_ref, g_ref, adj_ref, xb, bpb, xt, gt, wt, wtt, mcat, mcatv, gm, gmt, dm, dmt, dlo, dlot,
    qg, qqg, filt, gate, hid, hidn, hop1, hop2, bp, part,
    sq1, sq2, sf1, sf2, rq1, rq2, rf1, rf2,
    pay, ra, rb, sums,
    ssem, rsem, assem, arsem, nsem, lsem,
):
    n_space, n_dp, n_tm, scale = dims
    me = lax.axis_index("space")
    tm = lax.axis_index("tm")
    dp = lax.axis_index("dp")
    grp = dp * n_tm + tm
    n_grp = n_dp * n_tm
    z = lax.div(me, 4)
    y = lax.rem(me, 4)

    def space_dev(k):
        return {"space": k}

    def grp_dev(k):
        return {"dp": lax.div(k, n_tm), "tm": lax.rem(k, n_tm)}

    loads = [
        pltpu.make_async_copy(src, dst, lsem.at[i])
        for i, (src, dst) in enumerate(((g_hbm, g_ref), (adj_hbm, adj_ref), (x_hbm, x_ref)))
    ]
    for load in loads:
        load.start()

    barrier = pltpu.get_barrier_semaphore()

    @pl.loop(1, n_space)
    def _(off):
        pl.semaphore_signal(
            barrier, inc=1, device_id=space_dev(lax.rem(me + off, n_space)), device_id_type=MESH
        )

    @pl.loop(1, n_grp)
    def _(off):
        pl.semaphore_signal(
            barrier, inc=1, device_id=grp_dev(lax.rem(grp + off, n_grp)), device_id_type=MESH
        )

    def halo(i, send, recv):
        return [
            exchange(
                me, n_space, space_dev, rows(send.at[h], SLOTS), rows(recv.at[h], SLOTS),
                ssem.at[2 * i + h], rsem.at[2 * i + h],
            )
            for h in range(2)
        ]

    q1 = halo(0, sq1, rq1)
    q2 = halo(1, sq2, rq2)
    f1 = halo(2, sf1, rf1)
    f2 = halo(3, sf2, rf2)

    def by_distance(step):
        far = 1 - lax.div(step, 2)
        odd = lax.rem(lax.div(step + 1, 2), 2)
        return 2 * lax.rem(lax.div(z, 2) + far, 2) + lax.rem(lax.rem(z, 2) + odd, 2)

    def spread(ex, matrix, field, buf, h, compute=True, send=True):
        copy = ex[h][0]
        lanes = slice(256 * h, 256 * (h + 1))

        @pl.loop(0, 4)
        def _(step):
            zz = by_distance(step)
            if compute:
                at = pl.ds(pl.multiple_of(zz * 256, 256), 256)
                buf[h, at, :] = nn(matrix[at, :], field[:, lanes]).astype(BF16)
            if send:
                @pl.loop(0, 4)
                def _(k):
                    tgt = zz * 4 + lax.rem(y + k, 4)

                    @pl.when(tgt != me)
                    def _():
                        copy(tgt, me).start()

    def next_copy():
        return pltpu.make_async_remote_copy(
            src_ref=x_ref.at[pl.ds(384, 128), :], dst_ref=xb, send_sem=nsem.at[0], recv_sem=nsem.at[1],
            device_id={"tm": lax.rem(tm + 1, n_tm)}, device_id_type=MESH,
        )

    def back_copy():
        return pltpu.make_async_remote_copy(
            src_ref=bp.at[:, pl.ds(0, 256)], dst_ref=bpb, send_sem=nsem.at[2], recv_sem=nsem.at[3],
            device_id={"tm": lax.rem(tm + n_tm - 1, n_tm)}, device_id_type=MESH,
        )

    def tile_sum(r, b):
        total = None
        for k in range(4):
            slot = k if b < 2 else 4 + k
            hit = (cols_ref[r, slot] == b).astype(F32)
            term = adj_ref[r, slot].astype(F32) * hit
            total = term if total is None else total + term
        return total

    loads[0].wait()
    for p in range(4):
        gt[:, 128 * p : 128 * (p + 1)] = g_ref[128 * p : 128 * (p + 1), :].T
    loads[1].wait()
    for b in range(2, 10):
        for r in range(2):
            block = tile_sum(r, b).astype(BF16)
            dm[128 * r : 128 * (r + 1), 128 * b : 128 * (b + 1)] = block
            dmt[128 * (b - 2) : 128 * (b - 1), 128 * r : 128 * (r + 1)] = block.T

    own_slots = pl.ds(pl.multiple_of(me * SLOTS, SLOTS), SLOTS)
    for ref in (rq1, rq2, rf1, rf2):
        for h in range(2):
            ref[h, own_slots, :] = jnp.zeros((SLOTS, 256), BF16)
    loads[2].wait()
    pl.semaphore_wait(barrier, n_space - 1 + n_grp - 1)

    for h in range(2):
        spread(q1, dmt, gt, sq1, h)

    @pl.when(tm < n_tm - 1)
    def _():
        next_copy().start()

    @pl.when(tm == 0)
    def _():
        xb[...] = jnp.zeros_like(xb)

    @pl.when(tm == n_tm - 1)
    def _():
        bpb[...] = jnp.zeros_like(bpb)

    for b in range(2):
        for r in range(2):
            total = tile_sum(r, b)
            high = total.astype(BF16)
            low = (total - high.astype(F32)).astype(BF16)
            here = slice(128 * r, 128 * (r + 1)), slice(128 * b, 128 * (b + 1))
            dm[here] = high
            dlo[here] = low
            dlot[128 * b : 128 * (b + 1), 128 * r : 128 * (r + 1)] = high.T
            dlot[128 * b : 128 * (b + 1), 256 + 128 * r : 256 + 128 * (r + 1)] = low.T

    for m in range(4):
        lanes = slice(256 * m, 256 * (m + 1))
        sensor = lax.broadcasted_iota(jnp.int32, (256, 256), 0)
        block = (sensor == idx_ref[0:1, lanes]).astype(F32).astype(BF16)
        gm[:, lanes] = block
        gmt[lanes, :] = block.T

    zero = jnp.zeros((64, 64), F32)

    def pair(w):
        w = w.astype(F32)
        return jnp.concatenate([jnp.concatenate([w, zero], 1), jnp.concatenate([zero, w], 1)], 0)

    for k in range(3):
        block = pair(mixw_ref[k]).astype(BF16)
        mcat[:, 128 * k : 128 * (k + 1)] = block
        mcatv[128 * k : 128 * (k + 1), :] = block
    for half in range(2):
        for tap in range(2):
            block = pair(convw_ref[tap, 64 * half : 64 * (half + 1), :]).astype(BF16)
            wt[128 * half : 128 * (half + 1), 128 * tap : 128 * (tap + 1)] = block
            wtt[128 * tap : 128 * (tap + 1), 128 * half : 128 * (half + 1)] = block.T

    for p in range(4):
        xt[:, 128 * (p + 1) : 128 * (p + 2)] = x_ref[128 * p : 128 * (p + 1), :].T

    @pl.when(tm > 0)
    def _():
        next_copy().wait_recv()

    xt[:, 0:128] = xb[...].T
    b = convb_ref[...]
    bias = jnp.concatenate([b[:, :64], b[:, :64], b[:, 64:], b[:, 64:]], 1)
    for p in range(4):
        lanes = slice(128 * p, 128 * (p + 1))
        pre = nt(xt[:, 128 * p : 128 * p + 256], wt[...]) + bias
        f = jnp.tanh(pre[:, :128])
        s = jax.nn.sigmoid(pre[:, 128:])
        filt[:, lanes] = f
        gate[:, lanes] = s
        hid[:, lanes] = (f * s).astype(BF16)

    for h in range(2):
        lanes = slice(256 * h, 256 * (h + 1))
        q1[h][2]()
        grad = gt[:, lanes]
        own = nn(dlot[:, :256], grad) + nn(dlot[:, 256:], grad)
        qg[:, lanes] = (own + nn(gm[...], rq1[h])).astype(BF16)
        spread(q2, dmt, qg, sq2, h)

    spread(f1, gmt, hid, sf1, 0)
    spread(f1, gmt, hid, sf1, 1, send=False)
    for p in range(4):
        lanes = slice(128 * p, 128 * (p + 1))
        hidn[lanes, :] = hid[:, lanes].T
    gsum = jnp.zeros((1, 128), F32)
    for p in range(4):
        gsum = gsum + jnp.sum(gt[:, 128 * p : 128 * (p + 1)].astype(F32), axis=0, keepdims=True)

    low_lanes = lax.broadcasted_iota(jnp.int32, (64, 128), 1) < 64

    def diag_low(a):
        return a[:64] + pltpu.roll(a[64:], 64, 1)

    def diag_high(a):
        return pltpu.roll(a[:64], 64, 1) + a[64:]

    bsum = jnp.zeros((1, 256), F32)
    accs = [None] * 5

    def add(i, term):
        accs[i] = term if accs[i] is None else accs[i] + term

    for h in range(2):
        lanes = slice(256 * h, 256 * (h + 1))
        q2[h][2]()
        grad = qg[:, lanes]
        own = nn(dlot[:, :256], grad) + nn(dlot[:, 256:], grad)
        qqg[:, lanes] = (own + nn(gm[...], rq2[h])).astype(BF16)
        for p in (2 * h, 2 * h + 1):
            lanes = slice(128 * p, 128 * (p + 1))
            three = (gt[:, lanes], qg[:, lanes], qqg[:, lanes])
            bh = nn(jnp.concatenate(three, 1), mcatv[...])
            f = filt[:, lanes]
            s = gate[:, lanes]
            gf = (bh * (1.0 - f * f) * s).astype(BF16)
            gg = (bh * f * s * (1.0 - s)).astype(BF16)
            bp[:, 256 * p : 256 * p + 128] = gf
            bp[:, 256 * p + 128 : 256 * (p + 1)] = gg
            if p == 0:
                @pl.when(tm > 0)
                def _():
                    back_copy().start()
            bsum = bsum + jnp.concatenate(
                [
                    jnp.sum(gf.astype(F32), axis=0, keepdims=True),
                    jnp.sum(gg.astype(F32), axis=0, keepdims=True),
                ],
                1,
            )
            for k in range(3):
                add(k, nn(hidn[lanes, :], three[k]))
            wide = bp[:, 256 * p : 256 * (p + 1)]
            add(3, nn(xb[...] if p == 0 else x_ref[128 * (p - 1) : 128 * p, :], wide))
            add(4, nn(x_ref[lanes, :], wide))
    row = lax.broadcasted_iota(jnp.int32, (64, 128), 0)
    f_sum = bsum[:, :128]
    g_sum = bsum[:, 128:]
    f_sum = f_sum + pltpu.roll(f_sum, 64, 1)
    g_sum = g_sum + pltpu.roll(g_sum, 64, 1)
    o_sum = gsum + pltpu.roll(gsum, 64, 1)
    extra = jnp.where(row == 0, f_sum, jnp.where(row == 1, g_sum, jnp.where(row == 2, o_sum, 0.0)))
    pay[0:64, :] = jnp.where(low_lanes, diag_low(accs[0]), diag_high(accs[1]))
    pay[64:128, :] = jnp.where(low_lanes, diag_low(accs[2]), extra)
    for tap in range(2):
        acc = accs[3 + tap]
        pay[128 + 64 * tap : 192 + 64 * tap, :] = jnp.where(
            low_lanes, diag_low(acc[:, :128]), diag_high(acc[:, 128:])
        )

    s1 = exchange(me, n_space, space_dev, rows(pay, CHUNK), rows(ra, CHUNK), assem.at[0], arsem.at[0])
    s2 = exchange(grp, n_grp, grp_dev, lambda k: sums.at[0], rows(rb, CHUNK), assem.at[1], arsem.at[1])
    s3 = exchange(me, n_space, space_dev, lambda k: sums.at[1], rows(fin, CHUNK), assem.at[2], arsem.at[2])
    mine = pl.ds(pl.multiple_of(me * CHUNK, CHUNK), CHUNK)
    ours = pl.ds(pl.multiple_of(grp * CHUNK, CHUNK), CHUNK)

    def total_of(ref, count):
        total = ref[0:CHUNK, :]
        for k in range(1, count):
            total = total + ref[CHUNK * k : CHUNK * (k + 1), :]
        return total

    ra[mine, :] = pay[mine, :]
    s1[1]()
    spread(f1, gmt, hid, sf1, 1, compute=False)

    def grad_in(p, nxt):
        lanes = slice(128 * p, 128 * (p + 1))
        here = nt(wtt[128:, :], bp[:, 256 * p : 256 * (p + 1)])
        gin_ref[lanes, :] = (g_ref[lanes, :].astype(F32) + here + nt(wtt[:128, :], nxt)).astype(BF16)

    mb = mixb_ref[...]
    mb = jnp.broadcast_to(jnp.concatenate([mb, mb], 1), (128, 128)).T
    mb = jnp.concatenate([mb, mb], 1)

    for p in range(3):
        grad_in(p, bp[:, 256 * (p + 1) : 256 * (p + 2)])

    s1[2]()
    total = total_of(ra, n_space)
    sums[0] = total
    rb[ours, :] = total
    s2[1]()

    def hop(dst, src, recv, h):
        lanes = slice(256 * h, 256 * (h + 1))
        field = src[:, lanes]
        own = nn(dm[:, :256], field) + nn(dlo[...], field)
        dst[:, lanes] = (own + nn(dm[:, 256:], recv[h])).astype(BF16)

    def mixed(p, last):
        lanes = slice(128 * p, 128 * (p + 1))
        if last:
            here = nt(mcat[:, 256:], hop2[:, lanes])
            out_ref[lanes, :] = (part[lanes, :] + here).astype(BF16)
        else:
            here = nt(mcat[:, :128], hid[:, lanes]) + nt(mcat[:, 128:256], hop1[:, lanes])
            part[lanes, :] = x_ref[lanes, :].astype(F32) + mb + here

    f1[0][2]()
    hop(hop1, hid, rf1, 0)
    spread(f2, gmt, hop1, sf2, 0)
    mixed(0, False)
    mixed(1, False)
    f1[1][2]()
    hop(hop1, hid, rf1, 1)
    spread(f2, gmt, hop1, sf2, 1, send=False)
    s2[2]()
    total = total_of(rb, n_grp) * scale
    sums[1] = total
    fin[mine, :] = total
    s3[1]()
    spread(f2, gmt, hop1, sf2, 1, compute=False)
    mixed(2, False)
    mixed(3, False)

    @pl.when(tm < n_tm - 1)
    def _():
        back_copy().wait_recv()

    grad_in(3, bpb[...])
    for ex in (q1[0], q1[1], q2[0], q2[1], f1[0], f1[1], s1, s2):
        ex[3]()

    @pl.when(tm < n_tm - 1)
    def _():
        next_copy().wait_send()

    @pl.when(tm > 0)
    def _():
        back_copy().wait_send()

    for h in range(2):
        f2[h][2]()
        hop(hop2, hop1, rf2, h)
        mixed(2 * h, True)
        mixed(2 * h + 1, True)
    s3[2]()
    for ex in (f2[0], f2[1], s3):
        ex[3]()


def finish(out_in, gin_in, fin, out_ref, gin_ref, gcw_ref, gcb_ref, gmw_ref, gmb_ref):
    out_ref[...] = out_in[...]
    gin_ref[...] = gin_in[...]
    two = fin[0:64, :].T
    gmw_ref[0] = two[0:64]
    gmw_ref[1] = two[64:128]
    gmw_ref[2] = fin[64:128, :].T[0:64]
    for tap in range(2):
        gcw_ref[tap] = fin[128 + 64 * tap : 192 + 64 * tap, :].T
    tail = fin[64:72, :]
    low = lax.broadcasted_iota(jnp.int32, (1, 128), 1) < 64
    gcb_ref[...] = jnp.where(low, pltpu.roll(tail[0:1], 64, 1), tail[1:2])
    gmb_ref[...] = pltpu.roll(tail[2:3], 64, 1)[:, 0:64]


def body(dims, inputs, grad_out, conv_w, conv_b, mix_w, mix_b, adj_tiles, tile_cols, send_rows, counts):
    x = inputs.reshape(512, 256)
    g = grad_out.reshape(512, 256)
    slot = lax.broadcasted_iota(jnp.int32, send_rows.shape[1:], 1)
    idx = jnp.where(slot < counts[0][:, None], send_rows[0], -1).reshape(1, -1)
    vmem = pl.BlockSpec(memory_space=pltpu.VMEM)
    smem = pl.BlockSpec(memory_space=pltpu.SMEM)
    hbm = pl.BlockSpec(memory_space=pltpu.HBM)
    n_space = dims[0]
    n_grp = dims[1] * dims[2]

    def bf(*shape):
        return pltpu.VMEM(shape, BF16)

    def fl(*shape):
        return pltpu.VMEM(shape, F32)

    def dma(*shape):
        return pltpu.SemaphoreType.DMA(shape)

    scratch = [
        bf(512, 256), bf(512, 256), bf(2, 8, 128, 128), bf(128, 256), bf(256, 256), bf(256, 640), bf(256, 512),
        bf(256, 256), bf(256, 256), bf(128, 384), bf(384, 128),
        bf(256, 1024), bf(1024, 256), bf(256, 1280), bf(1024, 256), bf(256, 256), bf(256, 512),
        bf(256, 512), bf(256, 512), fl(256, 512), fl(256, 512), bf(256, 512), bf(512, 256),
        bf(256, 512), bf(256, 512), bf(256, 1024), fl(512, 256),
    ]
    scratch += [bf(2, 1024, 256)] * 8
    scratch += [fl(256, 128)] * 3 + [fl(2, CHUNK, 128)]
    scratch += [dma(8, n_space), dma(8, n_space), dma(3, n_grp), dma(3, n_grp), dma(4), dma(3)]
    out, gin, fin = pl.pallas_call(
        functools.partial(kernel, dims),
        out_shape=(
            jax.ShapeDtypeStruct((512, 256), BF16),
            jax.ShapeDtypeStruct((512, 256), BF16),
            jax.ShapeDtypeStruct((256, 128), F32),
        ),
        in_specs=[hbm] * 3 + [vmem] * 4 + [smem, vmem],
        out_specs=(vmem,) * 3,
        scratch_shapes=scratch,
        compiler_params=pltpu.CompilerParams(
            collective_id=0, has_side_effects=True, vmem_limit_bytes=48 * 2**20
        ),
    )(x, g, adj_tiles, conv_w, conv_b.reshape(1, 128), mix_w, mix_b.reshape(1, 64), tile_cols, idx)
    out, gin, gcw, gcb, gmw, gmb = pl.pallas_call(
        finish,
        out_shape=(
            jax.ShapeDtypeStruct((512, 256), BF16),
            jax.ShapeDtypeStruct((512, 256), BF16),
            jax.ShapeDtypeStruct((2, 128, 64), F32),
            jax.ShapeDtypeStruct((1, 128), F32),
            jax.ShapeDtypeStruct((3, 64, 64), F32),
            jax.ShapeDtypeStruct((1, 64), F32),
        ),
        in_specs=[vmem] * 3,
        out_specs=(vmem,) * 6,
    )(out, gin, fin)
    return (
        out.reshape(inputs.shape),
        gin.reshape(inputs.shape),
        gcw,
        gcb.reshape(128),
        gmw,
        gmb.reshape(64),
    )


def solution(mesh):
    in_specs = (
        P("dp", "tm", None, "space"),
        P("dp", "tm", None, "space"),
        P(),
        P(),
        P(),
        P(),
        P("space", None, None, None),
        P("space", None),
        P("space", None, None),
        P("space", None),
    )
    out_specs = (P("dp", "tm", None, "space"), P("dp", "tm", None, "space"), P(), P(), P(), P())
    cells = 8 * 256 * mesh.shape["dp"] * mesh.shape["space"] * mesh.shape["tm"]
    dims = (mesh.shape["space"], mesh.shape["dp"], mesh.shape["tm"], 1.0 / math.sqrt(cells))
    return jax.shard_map(
        functools.partial(body, dims), mesh=mesh, in_specs=in_specs, out_specs=out_specs, check_vma=False
    )
```

```python
import functools
import math

import jax
import jax.numpy as jnp
from jax import lax
from jax.experimental import pallas as pl
from jax.experimental.pallas import tpu as pltpu
from jax.sharding import PartitionSpec as P

MESH = pl.DeviceIdType.MESH
F32 = jnp.float32
BF16 = jnp.bfloat16
SLOTS = 64


def nn(a, b):
    return jnp.dot(a, b, preferred_element_type=F32)


def nt(a, b):
    return lax.dot_general(a, b, (((1,), (1,)), ((), ())), preferred_element_type=F32)


def exchange(mine, count, dev, src, dst, ss, rs):
    def copy(tgt, frm):
        return pltpu.make_async_remote_copy(
            src_ref=src(tgt), dst_ref=dst(frm), send_sem=ss.at[tgt], recv_sem=rs.at[frm],
            device_id=dev(tgt), device_id_type=MESH,
        )

    def start():
        @pl.loop(1, count)
        def _(off):
            copy(lax.rem(mine + off, count), mine).start()

    def received():
        @pl.loop(1, count)
        def _(off):
            copy(lax.rem(mine + off, count), lax.rem(mine + (count - off), count)).wait_recv()

    def sent():
        @pl.loop(1, count)
        def _(off):
            copy(lax.rem(mine + off, count), mine).wait_send()

    return copy, start, received, sent


def rows(ref, size):
    return lambda k: ref.at[pl.ds(pl.multiple_of(k * size, size), size), :]


def kernel(
    dims,
    x_hbm, g_hbm, adj_hbm, convw_hbm, convb_hbm, mixw_hbm, mixb_hbm, send_hbm, cols_ref, counts_ref,
    out_ref, gin_ref, fin,
    x_ref, g_ref, adj_ref, convw_ref, convb_ref, mixw_ref, mixb_ref, send_ref, xb, bpb, xt, gt, wt, wtt, mcat, mcatv, gm, gmt, dm, dmt, dlo, dlot,
    qg, qqg, filt, gate, hid, hidn, hop1, hop2, bp, part,
    sq1, sq2, sf1, sf2, rq1, rq2, rf1, rf2,
    pay, ra, rb, rc, rd, sum_a, sum_b, sum_c,
    ssem, rsem, assem, arsem, nsem, lsem,
):
    n_space, n_dp, n_tm, scale = dims
    me = lax.axis_index("space")
    tm = lax.axis_index("tm")
    dp = lax.axis_index("dp")
    z = lax.div(me, 4)
    y = lax.rem(me, 4)
    z_hi = lax.div(tm, 2)
    core = lax.rem(tm, 2)
    e = dp * 2 + core
    n_e = n_dp * 2
    q = z_hi * 4 + z

    def space_dev(k):
        return {"space": k}

    def e_dev(k):
        return {"dp": lax.div(k, 2), "tm": z_hi * 2 + lax.rem(k, 2)}

    def y_dev(k):
        return {"space": z * 4 + k}

    def q_dev(k):
        return {"space": lax.rem(k, 4) * 4 + y, "tm": lax.div(k, 4) * 2 + core}

    def signal(dev):
        pl.semaphore_signal(barrier, inc=1, device_id=dev, device_id_type=MESH)

    loads = [
        pltpu.make_async_copy(src, dst, lsem.at[i])
        for i, (src, dst) in enumerate(
            (
                (g_hbm, g_ref), (adj_hbm, adj_ref), (x_hbm, x_ref), (send_hbm, send_ref),
                (convw_hbm, convw_ref), (convb_hbm, convb_ref), (mixw_hbm, mixw_ref), (mixb_hbm, mixb_ref),
            )
        )
    ]
    for load in loads:
        load.start()

    barrier = pltpu.get_barrier_semaphore()

    @pl.loop(1, n_space)
    def _(off):
        signal(space_dev(lax.rem(me + off, n_space)))

    @pl.loop(1, n_e)
    def _(off):
        signal(e_dev(lax.rem(e + off, n_e)))

    @pl.loop(0, 4)
    def _(k):
        signal(q_dev((1 - z_hi) * 4 + k))

    signal({"tm": 3 - tm})

    def halo(i, send, recv):
        return [
            exchange(
                me, n_space, space_dev, rows(send.at[h], SLOTS), rows(recv.at[h], SLOTS),
                ssem.at[2 * i + h], rsem.at[2 * i + h],
            )
            for h in range(2)
        ]

    q1 = halo(0, sq1, rq1)
    q2 = halo(1, sq2, rq2)
    f1 = halo(2, sf1, rf1)
    f2 = halo(3, sf2, rf2)

    def by_distance(step):
        far = 1 - lax.div(step, 2)
        odd = lax.rem(lax.div(step + 1, 2), 2)
        return 2 * lax.rem(lax.div(z, 2) + far, 2) + lax.rem(lax.rem(z, 2) + odd, 2)

    def spread(ex, matrix, field, buf, h, compute=True, send=True):
        copy = ex[h][0]
        lanes = slice(256 * h, 256 * (h + 1))

        @pl.loop(0, 4)
        def _(step):
            zz = by_distance(step)
            if compute:
                at = pl.ds(pl.multiple_of(zz * 256, 256), 256)
                buf[h, at, :] = nn(matrix[at, :], field[:, lanes]).astype(BF16)
            if send:
                @pl.loop(0, 4)
                def _(k):
                    tgt = zz * 4 + lax.rem(y + k, 4)

                    @pl.when(tgt != me)
                    def _():
                        copy(tgt, me).start()

    def next_copy():
        return pltpu.make_async_remote_copy(
            src_ref=x_ref.at[pl.ds(384, 128), :], dst_ref=xb, send_sem=nsem.at[0], recv_sem=nsem.at[1],
            device_id={"tm": lax.rem(tm + 1, n_tm)}, device_id_type=MESH,
        )

    def back_copy():
        return pltpu.make_async_remote_copy(
            src_ref=bp.at[:, pl.ds(0, 256)], dst_ref=bpb, send_sem=nsem.at[2], recv_sem=nsem.at[3],
            device_id={"tm": lax.rem(tm + n_tm - 1, n_tm)}, device_id_type=MESH,
        )

    def tile_sum(r, b):
        total = None
        for k in range(4):
            slot = k if b < 2 else 4 + k
            hit = (cols_ref[r, slot] == b).astype(F32)
            term = adj_ref[r, slot].astype(F32) * hit
            total = term if total is None else total + term
        return total

    loads[0].wait()
    for p in range(4):
        gt[:, 128 * p : 128 * (p + 1)] = g_ref[128 * p : 128 * (p + 1), :].T
    loads[1].wait()
    for b in range(2, 10):
        for r in range(2):
            block = tile_sum(r, b).astype(BF16)
            dm[128 * r : 128 * (r + 1), 128 * b : 128 * (b + 1)] = block
            dmt[128 * (b - 2) : 128 * (b - 1), 128 * r : 128 * (r + 1)] = block.T

    own_slots = pl.ds(pl.multiple_of(me * SLOTS, SLOTS), SLOTS)
    for ref in (rq1, rq2, rf1, rf2):
        for h in range(2):
            ref[h, own_slots, :] = jnp.zeros((SLOTS, 256), BF16)
    for load in loads[2:]:
        load.wait()
    pl.semaphore_wait(barrier, n_space - 1 + n_e - 1 + 4 + 1)

    for h in range(2):
        spread(q1, dmt, gt, sq1, h)

    @pl.when(tm < n_tm - 1)
    def _():
        next_copy().start()

    @pl.when(tm == 0)
    def _():
        xb[...] = jnp.zeros_like(xb)

    @pl.when(tm == n_tm - 1)
    def _():
        bpb[...] = jnp.zeros_like(bpb)

    for b in range(2):
        for r in range(2):
            total = tile_sum(r, b)
            high = total.astype(BF16)
            low = (total - high.astype(F32)).astype(BF16)
            here = slice(128 * r, 128 * (r + 1)), slice(128 * b, 128 * (b + 1))
            dm[here] = high
            dlo[here] = low
            dlot[128 * b : 128 * (b + 1), 128 * r : 128 * (r + 1)] = high.T
            dlot[128 * b : 128 * (b + 1), 256 + 128 * r : 256 + 128 * (r + 1)] = low.T

    slot = lax.broadcasted_iota(jnp.int32, (1, SLOTS), 1)
    sensor = lax.broadcasted_iota(jnp.int32, (256, 128), 0)
    for m in range(8):
        picks = [
            jnp.where(slot < counts_ref[0, d], send_ref[d : d + 1, :], -1) for d in (2 * m, 2 * m + 1)
        ]
        block = (sensor == jnp.concatenate(picks, 1)).astype(F32).astype(BF16)
        gm[:, 128 * m : 128 * (m + 1)] = block
        gmt[128 * m : 128 * (m + 1), :] = block.T

    zero = jnp.zeros((64, 64), F32)

    def pair(w):
        w = w.astype(F32)
        return jnp.concatenate([jnp.concatenate([w, zero], 1), jnp.concatenate([zero, w], 1)], 0)

    for k in range(3):
        block = pair(mixw_ref[k]).astype(BF16)
        mcat[:, 128 * k : 128 * (k + 1)] = block
        mcatv[128 * k : 128 * (k + 1), :] = block
    for half in range(2):
        for tap in range(2):
            block = pair(convw_ref[tap].astype(F32)[:, 64 * half : 64 * (half + 1)]).astype(BF16)
            wtt[128 * tap : 128 * (tap + 1), 128 * half : 128 * (half + 1)] = block
            wt[128 * half : 128 * (half + 1), 128 * tap : 128 * (tap + 1)] = block.T

    for p in range(4):
        xt[:, 128 * (p + 1) : 128 * (p + 2)] = x_ref[128 * p : 128 * (p + 1), :].T

    @pl.when(tm > 0)
    def _():
        next_copy().wait_recv()

    xt[:, 0:128] = xb[...].T
    b = convb_ref[...]
    bias = jnp.concatenate([b[:, :64], b[:, :64], b[:, 64:], b[:, 64:]], 1)
    for p in range(4):
        lanes = slice(128 * p, 128 * (p + 1))
        pre = nt(xt[:, 128 * p : 128 * p + 256], wt[...]) + bias
        f = jnp.tanh(pre[:, :128])
        s = jax.nn.sigmoid(pre[:, 128:])
        filt[:, lanes] = f
        gate[:, lanes] = s
        hid[:, lanes] = (f * s).astype(BF16)

    for h in range(2):
        lanes = slice(256 * h, 256 * (h + 1))
        q1[h][2]()
        grad = gt[:, lanes]
        own = nn(dlot[:, :256], grad) + nn(dlot[:, 256:], grad)
        qg[:, lanes] = (own + nn(gm[...], rq1[h])).astype(BF16)
        spread(q2, dmt, qg, sq2, h)

    spread(f1, gmt, hid, sf1, 0)
    spread(f1, gmt, hid, sf1, 1)
    for p in range(4):
        lanes = slice(128 * p, 128 * (p + 1))
        hidn[lanes, :] = hid[:, lanes].T
    gsum = jnp.zeros((1, 128), F32)
    for p in range(4):
        gsum = gsum + jnp.sum(gt[:, 128 * p : 128 * (p + 1)].astype(F32), axis=0, keepdims=True)

    low_lanes = lax.broadcasted_iota(jnp.int32, (64, 128), 1) < 64

    def diag_low(a):
        return a[:64] + pltpu.roll(a[64:], 64, 1)

    def diag_high(a):
        return pltpu.roll(a[:64], 64, 1) + a[64:]

    bsum = jnp.zeros((1, 256), F32)
    accs = [None] * 5

    def add(i, term):
        accs[i] = term if accs[i] is None else accs[i] + term

    for h in range(2):
        lanes = slice(256 * h, 256 * (h + 1))
        q2[h][2]()
        grad = qg[:, lanes]
        own = nn(dlot[:, :256], grad) + nn(dlot[:, 256:], grad)
        qqg[:, lanes] = (own + nn(gm[...], rq2[h])).astype(BF16)
        for p in (2 * h, 2 * h + 1):
            lanes = slice(128 * p, 128 * (p + 1))
            three = (gt[:, lanes], qg[:, lanes], qqg[:, lanes])
            bh = nn(jnp.concatenate(three, 1), mcatv[...])
            f = filt[:, lanes]
            s = gate[:, lanes]
            gf = (bh * (1.0 - f * f) * s).astype(BF16)
            gg = (bh * f * s * (1.0 - s)).astype(BF16)
            bp[:, 256 * p : 256 * p + 128] = gf
            bp[:, 256 * p + 128 : 256 * (p + 1)] = gg
            if p == 0:
                @pl.when(tm > 0)
                def _():
                    back_copy().start()
            bsum = bsum + jnp.concatenate(
                [
                    jnp.sum(gf.astype(F32), axis=0, keepdims=True),
                    jnp.sum(gg.astype(F32), axis=0, keepdims=True),
                ],
                1,
            )
            for k in range(3):
                add(k, nn(hidn[lanes, :], three[k]))
            wide = bp[:, 256 * p : 256 * (p + 1)]
            add(3, nn(xb[...] if p == 0 else x_ref[128 * (p - 1) : 128 * p, :], wide))
            add(4, nn(x_ref[lanes, :], wide))
    row = lax.broadcasted_iota(jnp.int32, (64, 128), 0)
    f_sum = bsum[:, :128]
    g_sum = bsum[:, 128:]
    f_sum = f_sum + pltpu.roll(f_sum, 64, 1)
    g_sum = g_sum + pltpu.roll(g_sum, 64, 1)
    o_sum = gsum + pltpu.roll(gsum, 64, 1)
    extra = jnp.where(row == 0, f_sum, jnp.where(row == 1, g_sum, jnp.where(row == 2, o_sum, 0.0)))
    pay[0:64, :] = jnp.where(low_lanes, diag_low(accs[0]), diag_high(accs[1]))
    pay[64:128, :] = jnp.where(low_lanes, diag_low(accs[2]), extra)
    for tap in range(2):
        acc = accs[3 + tap]
        pay[128 + 64 * tap : 192 + 64 * tap, :] = jnp.where(
            low_lanes, diag_low(acc[:, :128]), diag_high(acc[:, 128:])
        )

    s1 = exchange(e, n_e, e_dev, rows(pay, 32), rows(ra, 32), assem.at[0], arsem.at[0])
    s2 = exchange(y, 4, y_dev, rows(sum_a, 8), rows(rb, 8), assem.at[1], arsem.at[1])
    s3 = exchange(q, 8, q_dev, lambda k: sum_b, rows(rc, 8), assem.at[2], arsem.at[2])
    s4 = exchange(y, 4, y_dev, lambda k: sum_c, rows(rd, 8), assem.at[3], arsem.at[3])
    s5 = exchange(e, n_e, e_dev, lambda k: rd, rows(fin, 32), assem.at[4], arsem.at[4])

    def total_of(ref, count, size):
        total = ref[0:size, :]
        for k in range(1, count):
            total = total + ref[size * k : size * (k + 1), :]
        return total

    def place(k, size):
        return pl.ds(pl.multiple_of(k * size, size), size)

    ra[place(e, 32), :] = pay[place(e, 32), :]
    s1[1]()

    def grad_in(p, nxt):
        lanes = slice(128 * p, 128 * (p + 1))
        here = nt(wtt[128:, :], bp[:, 256 * p : 256 * (p + 1)])
        gin_ref[lanes, :] = (g_ref[lanes, :].astype(F32) + here + nt(wtt[:128, :], nxt)).astype(BF16)

    mb = mixb_ref[...]
    mb = jnp.broadcast_to(jnp.concatenate([mb, mb], 1), (128, 128)).T
    mb = jnp.concatenate([mb, mb], 1)

    for p in range(3):
        grad_in(p, bp[:, 256 * (p + 1) : 256 * (p + 2)])

    s1[2]()
    sum_a[...] = total_of(ra, n_e, 32)
    rb[place(y, 8), :] = sum_a[place(y, 8), :]
    s2[1]()
    s2[2]()
    total = total_of(rb, 4, 8)
    sum_b[...] = total
    rc[place(q, 8), :] = total
    s3[1]()

    def hop(dst, src, recv, h):
        lanes = slice(256 * h, 256 * (h + 1))
        field = src[:, lanes]
        own = nn(dm[:, :256], field) + nn(dlo[...], field)
        dst[:, lanes] = (own + nn(dm[:, 256:], recv[h])).astype(BF16)

    def mixed(p, last):
        lanes = slice(128 * p, 128 * (p + 1))
        if last:
            here = nt(mcat[:, 256:], hop2[:, lanes])
            out_ref[lanes, :] = (part[lanes, :] + here).astype(BF16)
        else:
            here = nt(mcat[:, :128], hid[:, lanes]) + nt(mcat[:, 128:256], hop1[:, lanes])
            part[lanes, :] = x_ref[lanes, :].astype(F32) + mb + here

    f1[0][2]()
    hop(hop1, hid, rf1, 0)
    spread(f2, gmt, hop1, sf2, 0)
    mixed(0, False)
    mixed(1, False)
    f1[1][2]()
    hop(hop1, hid, rf1, 1)
    spread(f2, gmt, hop1, sf2, 1)
    s3[2]()
    total = total_of(rc, 8, 8) * scale
    sum_c[...] = total
    rd[place(y, 8), :] = total
    s4[1]()
    mixed(2, False)
    mixed(3, False)
    s4[2]()
    fin[place(e, 32), :] = rd[...]
    s5[1]()

    @pl.when(tm < n_tm - 1)
    def _():
        back_copy().wait_recv()

    grad_in(3, bpb[...])
    for ex in (q1[0], q1[1], q2[0], q2[1], f1[0], f1[1], s1, s2, s3, s4):
        ex[3]()

    @pl.when(tm < n_tm - 1)
    def _():
        next_copy().wait_send()

    @pl.when(tm > 0)
    def _():
        back_copy().wait_send()

    for h in range(2):
        f2[h][2]()
        hop(hop2, hop1, rf2, h)
        mixed(2 * h, True)
        mixed(2 * h + 1, True)
    s5[2]()
    for ex in (f2[0], f2[1], s5):
        ex[3]()


def finish(out_in, gin_in, fin, out_ref, gin_ref, gcw_ref, gcb_ref, gmw_ref, gmb_ref):
    out_ref[...] = out_in[...]
    gin_ref[...] = gin_in[...]
    two = fin[0:64, :].T
    gmw_ref[0] = two[0:64]
    gmw_ref[1] = two[64:128]
    gmw_ref[2] = fin[64:128, :].T[0:64]
    for tap in range(2):
        gcw_ref[tap] = fin[128 + 64 * tap : 192 + 64 * tap, :]
    tail = fin[64:72, :]
    low = lax.broadcasted_iota(jnp.int32, (1, 128), 1) < 64
    gcb_ref[...] = jnp.where(low, pltpu.roll(tail[0:1], 64, 1), tail[1:2])
    gmb_ref[...] = pltpu.roll(tail[2:3], 64, 1)[:, 0:64]


def body(dims, inputs, grad_out, conv_w, conv_b, mix_w, mix_b, adj_tiles, tile_cols, send_rows, counts):
    x = inputs.reshape(512, 256)
    g = grad_out.reshape(512, 256)
    vmem = pl.BlockSpec(memory_space=pltpu.VMEM)
    smem = pl.BlockSpec(memory_space=pltpu.SMEM)
    hbm = pl.BlockSpec(memory_space=pltpu.HBM)
    n_space = dims[0]
    n_e = dims[1] * 2

    def bf(*shape):
        return pltpu.VMEM(shape, BF16)

    def fl(*shape):
        return pltpu.VMEM(shape, F32)

    def dma(*shape):
        return pltpu.SemaphoreType.DMA(shape)

    scratch = [
        bf(512, 256), bf(512, 256), bf(2, 8, 128, 128), bf(2, 64, 128), fl(1, 128), bf(3, 64, 64), fl(1, 64),
        pltpu.VMEM((16, SLOTS), jnp.int32), bf(128, 256), bf(256, 256), bf(256, 640), bf(256, 512),
        bf(256, 256), bf(256, 256), bf(128, 384), bf(384, 128),
        bf(256, 1024), bf(1024, 256), bf(256, 1280), bf(1024, 256), bf(256, 256), bf(256, 512),
        bf(256, 512), bf(256, 512), fl(256, 512), fl(256, 512), bf(256, 512), bf(512, 256),
        bf(256, 512), bf(256, 512), bf(256, 1024), fl(512, 256),
    ]
    scratch += [bf(2, 1024, 256)] * 8
    scratch += [fl(256, 128), fl(256, 128), fl(32, 128), fl(64, 128), fl(32, 128), fl(32, 128), fl(8, 128), fl(8, 128)]
    scratch += [dma(8, n_space), dma(8, n_space), dma(5, n_e), dma(5, n_e), dma(4), dma(8)]
    out, gin, fin = pl.pallas_call(
        functools.partial(kernel, dims),
        out_shape=(
            jax.ShapeDtypeStruct((512, 256), BF16),
            jax.ShapeDtypeStruct((512, 256), BF16),
            jax.ShapeDtypeStruct((256, 128), F32),
        ),
        in_specs=[hbm] * 8 + [smem] * 2,
        out_specs=(vmem,) * 3,
        scratch_shapes=scratch,
        compiler_params=pltpu.CompilerParams(
            collective_id=0, has_side_effects=True, vmem_limit_bytes=60 * 2**20
        ),
    )(
        x, g, adj_tiles, jnp.swapaxes(conv_w, 1, 2), conv_b.reshape(1, 128), mix_w, mix_b.reshape(1, 64),
        send_rows[0], tile_cols, counts,
    )
    out, gin, gcw, gcb, gmw, gmb = pl.pallas_call(
        finish,
        out_shape=(
            jax.ShapeDtypeStruct((512, 256), BF16),
            jax.ShapeDtypeStruct((512, 256), BF16),
            jax.ShapeDtypeStruct((2, 64, 128), F32),
            jax.ShapeDtypeStruct((1, 128), F32),
            jax.ShapeDtypeStruct((3, 64, 64), F32),
            jax.ShapeDtypeStruct((1, 64), F32),
        ),
        in_specs=[vmem] * 3,
        out_specs=(vmem,) * 6,
    )(out, gin, fin)
    return (
        out.reshape(inputs.shape),
        gin.reshape(inputs.shape),
        jnp.swapaxes(gcw, 1, 2),
        gcb.reshape(128),
        gmw,
        gmb.reshape(64),
    )


def solution(mesh):
    in_specs = (
        P("dp", "tm", None, "space"),
        P("dp", "tm", None, "space"),
        P(),
        P(),
        P(),
        P(),
        P("space", None, None, None),
        P("space", None),
        P("space", None, None),
        P("space", None),
    )
    out_specs = (P("dp", "tm", None, "space"), P("dp", "tm", None, "space"), P(), P(), P(), P())
    cells = 8 * 256 * mesh.shape["dp"] * mesh.shape["space"] * mesh.shape["tm"]
    dims = (mesh.shape["space"], mesh.shape["dp"], mesh.shape["tm"], 1.0 / math.sqrt(cells))
    return jax.shard_map(
        functools.partial(body, dims), mesh=mesh, in_specs=in_specs, out_specs=out_specs, check_vma=False
    )
```

```python
import functools
import math

import jax
import jax.numpy as jnp
from jax import lax
from jax.experimental import pallas as pl
from jax.experimental.pallas import tpu as pltpu
from jax.sharding import PartitionSpec as P

MESH = pl.DeviceIdType.MESH
F32 = jnp.float32
BF16 = jnp.bfloat16
SLOTS = 64


def nn(a, b):
    return jnp.dot(a, b, preferred_element_type=F32)


def nt(a, b):
    return lax.dot_general(a, b, (((1,), (1,)), ((), ())), preferred_element_type=F32)


def exchange(mine, count, dev, src, dst, ss, rs):
    def copy(tgt, frm):
        return pltpu.make_async_remote_copy(
            src_ref=src(tgt), dst_ref=dst(frm), send_sem=ss.at[tgt], recv_sem=rs.at[frm],
            device_id=dev(tgt), device_id_type=MESH,
        )

    def start():
        @pl.loop(1, count)
        def _(off):
            copy(lax.rem(mine + off, count), mine).start()

    def received():
        @pl.loop(1, count)
        def _(off):
            copy(lax.rem(mine + off, count), lax.rem(mine + (count - off), count)).wait_recv()

    def sent():
        @pl.loop(1, count)
        def _(off):
            copy(lax.rem(mine + off, count), mine).wait_send()

    return copy, start, received, sent


def rows(ref, size):
    return lambda k: ref.at[pl.ds(pl.multiple_of(k * size, size), size), :]


def kernel(
    dims,
    x_hbm, g_hbm, adj_hbm, convw_hbm, convb_hbm, mixw_hbm, mixb_hbm, send_hbm, cols_ref, counts_ref,
    out_ref, gin_ref, fin,
    x_ref, g_ref, adj_ref, convw_ref, convb_ref, mixw_ref, mixb_ref, send_ref, xb, bpb, xt, gt, wt, wtt, mcat, mcatv, gm, gmt, dm, dmt, dlo, dlot,
    qg, qqg, filt, gate, hid, hidn, hop1, hop2, bp, part,
    sq1, sq2, sf1, sf2, rq1, rq2, rf1, rf2,
    pay, ra, rb, rc, rd, sum_a, sum_b, sum_c,
    meta, metax, gx, gxt, far, pick, rx1, rx2, tsend, tback,
    ssem, rsem, assem, arsem, nsem, lsem, fsem, psem, xsem,
):
    n_space, n_dp, n_tm, scale = dims
    me = lax.axis_index("space")
    tm = lax.axis_index("tm")
    dp = lax.axis_index("dp")
    z = lax.div(me, 4)
    y = lax.rem(me, 4)
    z_hi = lax.div(tm, 2)
    core = lax.rem(tm, 2)
    e = dp * 2 + core
    n_e = n_dp * 2
    q = z_hi * 4 + z
    side = lax.div(z, 2)
    end_z = 3 * side
    far_z = 3 - end_z
    is_end = z == end_z
    far_me = far_z * 4 + y
    row_in_side = lax.rem(z, 2) * 4 + y

    def space_dev(k):
        return {"space": k}

    def e_dev(k):
        return {"dp": lax.div(k, 2), "tm": z_hi * 2 + lax.rem(k, 2)}

    def y_dev(k):
        return {"space": z * 4 + k}

    def q_dev(k):
        return {"space": lax.rem(k, 4) * 4 + y, "tm": lax.div(k, 4) * 2 + core}

    def signal(dev):
        pl.semaphore_signal(barrier, inc=1, device_id=dev, device_id_type=MESH)

    loads = [
        pltpu.make_async_copy(src, dst, lsem.at[i])
        for i, (src, dst) in enumerate(
            (
                (g_hbm, g_ref), (adj_hbm, adj_ref), (x_hbm, x_ref), (send_hbm, send_ref),
                (convw_hbm, convw_ref), (convb_hbm, convb_ref), (mixw_hbm, mixw_ref), (mixb_hbm, mixb_ref),
            )
        )
    ]
    for load in loads:
        load.start()

    barrier = pltpu.get_barrier_semaphore()

    @pl.loop(1, n_space)
    def _(off):
        signal(space_dev(lax.rem(me + off, n_space)))

    @pl.loop(1, n_e)
    def _(off):
        signal(e_dev(lax.rem(e + off, n_e)))

    @pl.loop(0, 4)
    def _(k):
        signal(q_dev((1 - z_hi) * 4 + k))

    signal({"tm": 3 - tm})

    def halo(i, send, recv):
        return [
            exchange(
                me, n_space, space_dev, rows(send.at[h], SLOTS), rows(recv.at[h], SLOTS),
                ssem.at[2 * i + h], rsem.at[2 * i + h],
            )
            for h in range(2)
        ]

    q1 = halo(0, sq1, rq1)
    q2 = halo(1, sq2, rq2)
    f1 = halo(2, sf1, rf1)
    f2 = halo(3, sf2, rf2)

    def by_distance(step):
        far = 1 - lax.div(step, 2)
        odd = lax.rem(lax.div(step + 1, 2), 2)
        return 2 * lax.rem(lax.div(z, 2) + far, 2) + lax.rem(lax.rem(z, 2) + odd, 2)

    def slot_block(ref, h, k):
        return ref.at[h, pl.ds(pl.multiple_of(k * SLOTS, SLOTS), SLOTS), :]

    def across(part):
        return is_end & (lax.div(part, 8) != side)

    def f_spread(ex, field, buf, h):
        copy = ex[h][0]
        lanes = slice(256 * h, 256 * (h + 1))

        @pl.loop(0, 4)
        def _(step):
            zz = by_distance(step)

            @pl.when(jnp.logical_not(across(zz * 4)))
            def _():
                at = pl.ds(pl.multiple_of(zz * 256, 256), 256)
                buf[h, at, :] = nn(gmt[at, :], field[:, lanes]).astype(BF16)

                @pl.loop(0, 4)
                def _(k):
                    tgt = zz * 4 + lax.rem(y + k, 4)

                    @pl.when(tgt != me)
                    def _():
                        copy(tgt, me).start()

    def swap(i, h, field):
        return pltpu.make_async_remote_copy(
            src_ref=field.at[:, pl.ds(256 * h, 256)], dst_ref=far.at[2 * i + h],
            send_sem=fsem.at[0, 2 * i + h], recv_sem=fsem.at[1, 2 * i + h],
            device_id=space_dev(far_me), device_id_type=MESH,
        )

    def f_swap(i, h, field):
        @pl.when(is_end)
        def _():
            swap(i, h, field).start()

    def proxy_copy(i, h, recv, k, tgt):
        return pltpu.make_async_remote_copy(
            src_ref=slot_block(pick, 2 * i + h, k), dst_ref=slot_block(recv, h, far_me),
            send_sem=psem.at[2 * i + h, k], recv_sem=rsem.at[4 + 2 * i + h, far_me],
            device_id=space_dev(tgt), device_id_type=MESH,
        )

    def f_proxy(i, h, field, recv):
        @pl.when(is_end)
        def _():
            swap(i, h, field).wait_recv()

            @pl.loop(0, 2)
            def _(step):
                zz = lax.rem(lax.rem(z, 2) + 1 + step, 2)
                at = pl.ds(pl.multiple_of(zz * 256, 256), 256)
                pick[2 * i + h, at, :] = nn(gxt[at, :], far[2 * i + h]).astype(BF16)

                @pl.loop(0, 4)
                def _(j):
                    k = zz * 4 + lax.rem(y + j, 4)
                    tgt = side * 8 + k

                    @pl.when(tgt != me)
                    def _():
                        proxy_copy(i, h, recv, k, tgt).start()

            slot_block(recv, h, far_me)[...] = slot_block(pick, 2 * i + h, row_in_side)[...]

    def f_received(i, h, ex):
        copy = ex[h][0]

        @pl.loop(1, n_space)
        def _(off):
            frm = lax.rem(me + (n_space - off), n_space)

            @pl.when(jnp.logical_not(is_end & (frm == far_me)))
            def _():
                copy(lax.rem(me + off, n_space), frm).wait_recv()

    def f_sent(i, h, ex, field, recv):
        copy = ex[h][0]

        @pl.loop(1, n_space)
        def _(off):
            tgt = lax.rem(me + off, n_space)

            @pl.when(jnp.logical_not(across(tgt)))
            def _():
                copy(tgt, me).wait_send()

        @pl.when(is_end)
        def _():
            swap(i, h, field).wait_send()

            @pl.loop(0, 8)
            def _(k):
                @pl.when(k != row_in_side)
                def _():
                    proxy_copy(i, h, recv, k, side * 8 + k).wait_send()

    def collect_copy(i, h, send, rx, s, k):
        return pltpu.make_async_remote_copy(
            src_ref=slot_block(send, h, s), dst_ref=slot_block(rx, h, k),
            send_sem=ssem.at[2 * i + h, s], recv_sem=xsem.at[2 * i + h, k],
            device_id=space_dev(end_z * 4 + lax.rem(s, 4)), device_id_type=MESH,
        )

    def q_spread(i, ex, field, buf, rx, h):
        copy = ex[h][0]
        lanes = slice(256 * h, 256 * (h + 1))

        @pl.loop(0, 4)
        def _(step):
            zz = by_distance(step)
            at = pl.ds(pl.multiple_of(zz * 256, 256), 256)
            buf[h, at, :] = nn(dmt[at, :], field[:, lanes]).astype(BF16)

            @pl.loop(0, 4)
            def _(k):
                tgt = zz * 4 + lax.rem(y + k, 4)

                @pl.when((zz != far_z) & (tgt != me))
                def _():
                    copy(tgt, me).start()

                @pl.when((zz == far_z) & (jnp.logical_not(is_end) | (tgt != far_me)))
                def _():
                    collect_copy(i, h, buf, rx, tgt, row_in_side).start()

        @pl.when(is_end)
        def _():
            slot_block(rx, h, row_in_side)[...] = slot_block(buf, h, far_me)[...]

    def back_field(i, h):
        return pltpu.make_async_remote_copy(
            src_ref=tsend.at[2 * i + h], dst_ref=tback.at[2 * i + h],
            send_sem=fsem.at[2, 2 * i + h], recv_sem=fsem.at[3, 2 * i + h],
            device_id=space_dev(far_me), device_id_type=MESH,
        )

    def q_received(i, h, ex, buf, rx):
        copy = ex[h][0]

        @pl.when(is_end)
        def _():
            @pl.loop(0, 8)
            def _(k):
                @pl.when(k != row_in_side)
                def _():
                    collect_copy(i, h, buf, rx, far_me, k).wait_recv()

            tsend[2 * i + h] = nn(gx[...], rx[h]).astype(BF16)
            back_field(i, h).start()

        @pl.loop(1, n_space)
        def _(off):
            frm = lax.rem(me + (n_space - off), n_space)

            @pl.when(jnp.logical_not(across(frm)))
            def _():
                copy(lax.rem(me + off, n_space), frm).wait_recv()

        @pl.when(is_end)
        def _():
            back_field(i, h).wait_recv()

    def q_sent(i, h, ex, buf, rx):
        copy = ex[h][0]

        @pl.loop(1, n_space)
        def _(off):
            tgt = lax.rem(me + off, n_space)
            zz = lax.div(tgt, 4)

            @pl.when(zz != far_z)
            def _():
                copy(tgt, me).wait_send()

            @pl.when((zz == far_z) & (jnp.logical_not(is_end) | (tgt != far_me)))
            def _():
                collect_copy(i, h, buf, rx, tgt, row_in_side).wait_send()

        @pl.when(is_end)
        def _():
            back_field(i, h).wait_send()

    def meta_copy():
        return pltpu.make_async_remote_copy(
            src_ref=meta, dst_ref=metax, send_sem=nsem.at[4], recv_sem=nsem.at[5],
            device_id=space_dev(far_me), device_id_type=MESH,
        )

    def next_copy():
        return pltpu.make_async_remote_copy(
            src_ref=x_ref.at[pl.ds(384, 128), :], dst_ref=xb, send_sem=nsem.at[0], recv_sem=nsem.at[1],
            device_id={"tm": lax.rem(tm + 1, n_tm)}, device_id_type=MESH,
        )

    def back_copy():
        return pltpu.make_async_remote_copy(
            src_ref=bp.at[:, pl.ds(0, 256)], dst_ref=bpb, send_sem=nsem.at[2], recv_sem=nsem.at[3],
            device_id={"tm": lax.rem(tm + n_tm - 1, n_tm)}, device_id_type=MESH,
        )

    def tile_sum(r, b):
        total = None
        for k in range(4):
            slot = k if b < 2 else 4 + k
            hit = (cols_ref[r, slot] == b).astype(F32)
            term = adj_ref[r, slot].astype(F32) * hit
            total = term if total is None else total + term
        return total

    loads[0].wait()
    for p in range(4):
        gt[:, 128 * p : 128 * (p + 1)] = g_ref[128 * p : 128 * (p + 1), :].T
    loads[1].wait()
    for b in range(2, 10):
        for r in range(2):
            block = tile_sum(r, b).astype(BF16)
            dm[128 * r : 128 * (r + 1), 128 * b : 128 * (b + 1)] = block
            dmt[128 * (b - 2) : 128 * (b - 1), 128 * r : 128 * (r + 1)] = block.T

    own_slots = pl.ds(pl.multiple_of(me * SLOTS, SLOTS), SLOTS)
    for ref in (rq1, rq2, rf1, rf2):
        for h in range(2):
            ref[h, own_slots, :] = jnp.zeros((SLOTS, 256), BF16)
    @pl.when(is_end)
    def _():
        for ref in (rq1, rq2):
            for h in range(2):
                ref[h, pl.ds(pl.multiple_of((1 - side) * 512, 512), 512), :] = jnp.zeros((512, 256), BF16)

    @pl.when(jnp.logical_not(is_end))
    def _():
        tback[...] = jnp.zeros_like(tback)

    for load in loads[2:]:
        load.wait()
    slot = lax.broadcasted_iota(jnp.int32, (1, SLOTS), 1)
    for d in range(16):
        picks = jnp.where(slot < counts_ref[0, d], send_ref[d : d + 1, :], -1)
        meta[d : d + 1, :] = jnp.concatenate([picks, picks], 1)
    pl.semaphore_wait(barrier, n_space - 1 + n_e - 1 + 4 + 1)

    @pl.when(is_end)
    def _():
        meta_copy().start()

    for h in range(2):
        q_spread(0, q1, gt, sq1, rx1, h)

    @pl.when(tm < n_tm - 1)
    def _():
        next_copy().start()

    @pl.when(tm == 0)
    def _():
        xb[...] = jnp.zeros_like(xb)

    @pl.when(tm == n_tm - 1)
    def _():
        bpb[...] = jnp.zeros_like(bpb)

    for b in range(2):
        for r in range(2):
            total = tile_sum(r, b)
            high = total.astype(BF16)
            low = (total - high.astype(F32)).astype(BF16)
            here = slice(128 * r, 128 * (r + 1)), slice(128 * b, 128 * (b + 1))
            dm[here] = high
            dlo[here] = low
            dlot[128 * b : 128 * (b + 1), 128 * r : 128 * (r + 1)] = high.T
            dlot[128 * b : 128 * (b + 1), 256 + 128 * r : 256 + 128 * (r + 1)] = low.T

    sensor = lax.broadcasted_iota(jnp.int32, (256, 128), 0)
    low_row = lax.broadcasted_iota(jnp.int32, (1, 128), 1) < 64

    def select(first, second):
        return (sensor == jnp.where(low_row, first, second)).astype(F32).astype(BF16)

    for m in range(8):
        sel = select(meta[2 * m : 2 * m + 1, :], meta[2 * m + 1 : 2 * m + 2, :])
        gm[:, 128 * m : 128 * (m + 1)] = sel
        gmt[128 * m : 128 * (m + 1), :] = sel.T

    zero = jnp.zeros((64, 64), F32)

    def pair(w):
        w = w.astype(F32)
        return jnp.concatenate([jnp.concatenate([w, zero], 1), jnp.concatenate([zero, w], 1)], 0)

    for k in range(3):
        block = pair(mixw_ref[k]).astype(BF16)
        mcat[:, 128 * k : 128 * (k + 1)] = block
        mcatv[128 * k : 128 * (k + 1), :] = block
    for half in range(2):
        for tap in range(2):
            block = pair(convw_ref[tap].astype(F32)[:, 64 * half : 64 * (half + 1)]).astype(BF16)
            wtt[128 * tap : 128 * (tap + 1), 128 * half : 128 * (half + 1)] = block
            wt[128 * half : 128 * (half + 1), 128 * tap : 128 * (tap + 1)] = block.T

    for p in range(4):
        xt[:, 128 * (p + 1) : 128 * (p + 2)] = x_ref[128 * p : 128 * (p + 1), :].T

    @pl.when(tm > 0)
    def _():
        next_copy().wait_recv()

    xt[:, 0:128] = xb[...].T
    b = convb_ref[...]
    bias = jnp.concatenate([b[:, :64], b[:, :64], b[:, 64:], b[:, 64:]], 1)
    for p in range(4):
        lanes = slice(128 * p, 128 * (p + 1))
        pre = nt(xt[:, 128 * p : 128 * p + 256], wt[...]) + bias
        f = jnp.tanh(pre[:, :128])
        s = jax.nn.sigmoid(pre[:, 128:])
        filt[:, lanes] = f
        gate[:, lanes] = s
        hid[:, lanes] = (f * s).astype(BF16)

    for h in range(2):
        f_swap(0, h, hid)

    @pl.when(is_end)
    def _():
        meta_copy().wait_recv()
        for m in range(4):
            d = side * 8 + 2 * m
            sel = select(metax[pl.ds(d, 1), :], metax[pl.ds(d + 1, 1), :])
            gx[:, 128 * m : 128 * (m + 1)] = sel
            gxt[128 * m : 128 * (m + 1), :] = sel.T

    for h in range(2):
        lanes = slice(256 * h, 256 * (h + 1))
        q_received(0, h, q1, sq1, rx1)
        grad = gt[:, lanes]
        own = nn(dlot[:, :256], grad) + nn(dlot[:, 256:], grad)
        own = own + tback[h].astype(F32)
        qg[:, lanes] = (own + nn(gm[...], rq1[h])).astype(BF16)
        q_spread(1, q2, qg, sq2, rx2, h)

    for h in range(2):
        f_spread(f1, hid, sf1, h)
        f_proxy(0, h, hid, rf1)
    for p in range(4):
        lanes = slice(128 * p, 128 * (p + 1))
        hidn[lanes, :] = hid[:, lanes].T
    gsum = jnp.zeros((1, 128), F32)
    for p in range(4):
        gsum = gsum + jnp.sum(gt[:, 128 * p : 128 * (p + 1)].astype(F32), axis=0, keepdims=True)

    low_lanes = lax.broadcasted_iota(jnp.int32, (64, 128), 1) < 64

    def diag_low(a):
        return a[:64] + pltpu.roll(a[64:], 64, 1)

    def diag_high(a):
        return pltpu.roll(a[:64], 64, 1) + a[64:]

    bsum = jnp.zeros((1, 256), F32)
    accs = [None] * 5

    def add(i, term):
        accs[i] = term if accs[i] is None else accs[i] + term

    for h in range(2):
        lanes = slice(256 * h, 256 * (h + 1))
        q_received(1, h, q2, sq2, rx2)
        grad = qg[:, lanes]
        own = nn(dlot[:, :256], grad) + nn(dlot[:, 256:], grad)
        own = own + tback[2 + h].astype(F32)
        qqg[:, lanes] = (own + nn(gm[...], rq2[h])).astype(BF16)
        for p in (2 * h, 2 * h + 1):
            lanes = slice(128 * p, 128 * (p + 1))
            three = (gt[:, lanes], qg[:, lanes], qqg[:, lanes])
            bh = nn(jnp.concatenate(three, 1), mcatv[...])
            f = filt[:, lanes]
            s = gate[:, lanes]
            gf = (bh * (1.0 - f * f) * s).astype(BF16)
            gg = (bh * f * s * (1.0 - s)).astype(BF16)
            bp[:, 256 * p : 256 * p + 128] = gf
            bp[:, 256 * p + 128 : 256 * (p + 1)] = gg
            if p == 0:
                @pl.when(tm > 0)
                def _():
                    back_copy().start()
            bsum = bsum + jnp.concatenate(
                [
                    jnp.sum(gf.astype(F32), axis=0, keepdims=True),
                    jnp.sum(gg.astype(F32), axis=0, keepdims=True),
                ],
                1,
            )
            for k in range(3):
                add(k, nn(hidn[lanes, :], three[k]))
            wide = bp[:, 256 * p : 256 * (p + 1)]
            add(3, nn(xb[...] if p == 0 else x_ref[128 * (p - 1) : 128 * p, :], wide))
            add(4, nn(x_ref[lanes, :], wide))
    row = lax.broadcasted_iota(jnp.int32, (64, 128), 0)
    f_sum = bsum[:, :128]
    g_sum = bsum[:, 128:]
    f_sum = f_sum + pltpu.roll(f_sum, 64, 1)
    g_sum = g_sum + pltpu.roll(g_sum, 64, 1)
    o_sum = gsum + pltpu.roll(gsum, 64, 1)
    extra = jnp.where(row == 0, f_sum, jnp.where(row == 1, g_sum, jnp.where(row == 2, o_sum, 0.0)))
    pay[0:64, :] = jnp.where(low_lanes, diag_low(accs[0]), diag_high(accs[1]))
    pay[64:128, :] = jnp.where(low_lanes, diag_low(accs[2]), extra)
    for tap in range(2):
        acc = accs[3 + tap]
        pay[128 + 64 * tap : 192 + 64 * tap, :] = jnp.where(
            low_lanes, diag_low(acc[:, :128]), diag_high(acc[:, 128:])
        )

    s1 = exchange(e, n_e, e_dev, rows(pay, 32), rows(ra, 32), assem.at[0], arsem.at[0])
    s2 = exchange(y, 4, y_dev, rows(sum_a, 8), rows(rb, 8), assem.at[1], arsem.at[1])
    s3 = exchange(q, 8, q_dev, lambda k: sum_b, rows(rc, 8), assem.at[2], arsem.at[2])
    s4 = exchange(y, 4, y_dev, lambda k: sum_c, rows(rd, 8), assem.at[3], arsem.at[3])
    s5 = exchange(e, n_e, e_dev, lambda k: rd, rows(fin, 32), assem.at[4], arsem.at[4])

    def total_of(ref, count, size):
        total = ref[0:size, :]
        for k in range(1, count):
            total = total + ref[size * k : size * (k + 1), :]
        return total

    def place(k, size):
        return pl.ds(pl.multiple_of(k * size, size), size)

    ra[place(e, 32), :] = pay[place(e, 32), :]
    s1[1]()

    def grad_in(p, nxt):
        lanes = slice(128 * p, 128 * (p + 1))
        here = nt(wtt[128:, :], bp[:, 256 * p : 256 * (p + 1)])
        gin_ref[lanes, :] = (g_ref[lanes, :].astype(F32) + here + nt(wtt[:128, :], nxt)).astype(BF16)

    mb = mixb_ref[...]
    mb = jnp.broadcast_to(jnp.concatenate([mb, mb], 1), (128, 128)).T
    mb = jnp.concatenate([mb, mb], 1)

    for p in range(3):
        grad_in(p, bp[:, 256 * (p + 1) : 256 * (p + 2)])

    s1[2]()
    sum_a[...] = total_of(ra, n_e, 32)
    rb[place(y, 8), :] = sum_a[place(y, 8), :]
    s2[1]()
    s2[2]()
    total = total_of(rb, 4, 8)
    sum_b[...] = total
    rc[place(q, 8), :] = total
    s3[1]()

    def hop(dst, src, recv, h):
        lanes = slice(256 * h, 256 * (h + 1))
        field = src[:, lanes]
        own = nn(dm[:, :256], field) + nn(dlo[...], field)
        dst[:, lanes] = (own + nn(dm[:, 256:], recv[h])).astype(BF16)

    def mixed(p, last):
        lanes = slice(128 * p, 128 * (p + 1))
        if last:
            here = nt(mcat[:, 256:], hop2[:, lanes])
            out_ref[lanes, :] = (part[lanes, :] + here).astype(BF16)
        else:
            here = nt(mcat[:, :128], hid[:, lanes]) + nt(mcat[:, 128:256], hop1[:, lanes])
            part[lanes, :] = x_ref[lanes, :].astype(F32) + mb + here

    for h in range(2):
        f_received(0, h, f1)
        hop(hop1, hid, rf1, h)
        f_swap(1, h, hop1)
        f_spread(f2, hop1, sf2, h)
    f_proxy(1, 0, hop1, rf2)
    s3[2]()
    total = total_of(rc, 8, 8) * scale
    sum_c[...] = total
    rd[place(y, 8), :] = total
    s4[1]()
    f_proxy(1, 1, hop1, rf2)
    s4[2]()
    fin[place(e, 32), :] = rd[...]
    s5[1]()
    for p in range(4):
        mixed(p, False)

    @pl.when(tm < n_tm - 1)
    def _():
        back_copy().wait_recv()

    grad_in(3, bpb[...])
    for h in range(2):
        q_sent(0, h, q1, sq1, rx1)
        q_sent(1, h, q2, sq2, rx2)
        f_sent(0, h, f1, hid, rf1)
    for ex in (s1, s2, s3, s4):
        ex[3]()

    @pl.when(is_end)
    def _():
        meta_copy().wait_send()

    @pl.when(tm < n_tm - 1)
    def _():
        next_copy().wait_send()

    @pl.when(tm > 0)
    def _():
        back_copy().wait_send()

    for h in range(2):
        f_received(1, h, f2)
        hop(hop2, hop1, rf2, h)
        mixed(2 * h, True)
        mixed(2 * h + 1, True)
    s5[2]()
    s5[3]()
    for h in range(2):
        f_sent(1, h, f2, hop1, rf2)


def finish(out_in, gin_in, fin, out_ref, gin_ref, gcw_ref, gcb_ref, gmw_ref, gmb_ref):
    out_ref[...] = out_in[...]
    gin_ref[...] = gin_in[...]
    two = fin[0:64, :].T
    gmw_ref[0] = two[0:64]
    gmw_ref[1] = two[64:128]
    gmw_ref[2] = fin[64:128, :].T[0:64]
    for tap in range(2):
        gcw_ref[tap] = fin[128 + 64 * tap : 192 + 64 * tap, :]
    tail = fin[64:72, :]
    low = lax.broadcasted_iota(jnp.int32, (1, 128), 1) < 64
    gcb_ref[...] = jnp.where(low, pltpu.roll(tail[0:1], 64, 1), tail[1:2])
    gmb_ref[...] = pltpu.roll(tail[2:3], 64, 1)[:, 0:64]


def body(dims, inputs, grad_out, conv_w, conv_b, mix_w, mix_b, adj_tiles, tile_cols, send_rows, counts):
    x = inputs.reshape(512, 256)
    g = grad_out.reshape(512, 256)
    vmem = pl.BlockSpec(memory_space=pltpu.VMEM)
    smem = pl.BlockSpec(memory_space=pltpu.SMEM)
    hbm = pl.BlockSpec(memory_space=pltpu.HBM)
    n_space = dims[0]
    n_e = dims[1] * 2

    def bf(*shape):
        return pltpu.VMEM(shape, BF16)

    def fl(*shape):
        return pltpu.VMEM(shape, F32)

    def dma(*shape):
        return pltpu.SemaphoreType.DMA(shape)

    scratch = [
        bf(512, 256), bf(512, 256), bf(2, 8, 128, 128), bf(2, 64, 128), fl(1, 128), bf(3, 64, 64), fl(1, 64),
        pltpu.VMEM((16, SLOTS), jnp.int32), bf(128, 256), bf(256, 256), bf(256, 640), bf(256, 512),
        bf(256, 256), bf(256, 256), bf(128, 384), bf(384, 128),
        bf(256, 1024), bf(1024, 256), bf(256, 1280), bf(1024, 256), bf(256, 256), bf(256, 512),
        bf(256, 512), bf(256, 512), fl(256, 512), fl(256, 512), bf(256, 512), bf(512, 256),
        bf(256, 512), bf(256, 512), bf(256, 1024), fl(512, 256),
    ]
    scratch += [bf(2, 1024, 256)] * 8
    scratch += [fl(256, 128), fl(256, 128), fl(32, 128), fl(64, 128), fl(32, 128), fl(32, 128), fl(8, 128), fl(8, 128)]
    ints = pltpu.VMEM((16, 128), jnp.int32)
    scratch += [ints, ints, bf(256, 512), bf(512, 256), bf(4, 256, 256), bf(4, 512, 256), bf(2, 512, 256), bf(2, 512, 256)]
    scratch += [bf(4, 256, 256), bf(4, 256, 256)]
    scratch += [dma(8, n_space), dma(8, n_space), dma(5, n_e), dma(5, n_e), dma(6), dma(8)]
    scratch += [dma(4, 4), dma(4, 8), dma(4, 8)]
    out, gin, fin = pl.pallas_call(
        functools.partial(kernel, dims),
        out_shape=(
            jax.ShapeDtypeStruct((512, 256), BF16),
            jax.ShapeDtypeStruct((512, 256), BF16),
            jax.ShapeDtypeStruct((256, 128), F32),
        ),
        in_specs=[hbm] * 8 + [smem] * 2,
        out_specs=(vmem,) * 3,
        scratch_shapes=scratch,
        compiler_params=pltpu.CompilerParams(
            collective_id=0, has_side_effects=True, vmem_limit_bytes=60 * 2**20
        ),
    )(
        x, g, adj_tiles, jnp.swapaxes(conv_w, 1, 2), conv_b.reshape(1, 128), mix_w, mix_b.reshape(1, 64),
        send_rows[0], tile_cols, counts,
    )
    out, gin, gcw, gcb, gmw, gmb = pl.pallas_call(
        finish,
        out_shape=(
            jax.ShapeDtypeStruct((512, 256), BF16),
            jax.ShapeDtypeStruct((512, 256), BF16),
            jax.ShapeDtypeStruct((2, 64, 128), F32),
            jax.ShapeDtypeStruct((1, 128), F32),
            jax.ShapeDtypeStruct((3, 64, 64), F32),
            jax.ShapeDtypeStruct((1, 64), F32),
        ),
        in_specs=[vmem] * 3,
        out_specs=(vmem,) * 6,
    )(out, gin, fin)
    return (
        out.reshape(inputs.shape),
        gin.reshape(inputs.shape),
        jnp.swapaxes(gcw, 1, 2),
        gcb.reshape(128),
        gmw,
        gmb.reshape(64),
    )


def solution(mesh):
    in_specs = (
        P("dp", "tm", None, "space"),
        P("dp", "tm", None, "space"),
        P(),
        P(),
        P(),
        P(),
        P("space", None, None, None),
        P("space", None),
        P("space", None, None),
        P("space", None),
    )
    out_specs = (P("dp", "tm", None, "space"), P("dp", "tm", None, "space"), P(), P(), P(), P())
    cells = 8 * 256 * mesh.shape["dp"] * mesh.shape["space"] * mesh.shape["tm"]
    dims = (mesh.shape["space"], mesh.shape["dp"], mesh.shape["tm"], 1.0 / math.sqrt(cells))
    return jax.shard_map(
        functools.partial(body, dims), mesh=mesh, in_specs=in_specs, out_specs=out_specs, check_vma=False
    )
```

```python
import functools
import math

import jax
import jax.numpy as jnp
from jax import lax
from jax.experimental import pallas as pl
from jax.experimental.pallas import tpu as pltpu
from jax.sharding import PartitionSpec as P

MESH = pl.DeviceIdType.MESH
F32 = jnp.float32
BF16 = jnp.bfloat16
SLOTS = 64


def nn(a, b):
    return jnp.dot(a, b, preferred_element_type=F32)


def nt(a, b):
    return lax.dot_general(a, b, (((1,), (1,)), ((), ())), preferred_element_type=F32)


def exchange(mine, count, dev, src, dst, ss, rs):
    def copy(tgt, frm):
        return pltpu.make_async_remote_copy(
            src_ref=src(tgt), dst_ref=dst(frm), send_sem=ss.at[tgt], recv_sem=rs.at[frm],
            device_id=dev(tgt), device_id_type=MESH,
        )

    def start():
        @pl.loop(1, count)
        def _(off):
            copy(lax.rem(mine + off, count), mine).start()

    def received():
        @pl.loop(1, count)
        def _(off):
            copy(lax.rem(mine + off, count), lax.rem(mine + (count - off), count)).wait_recv()

    def sent():
        @pl.loop(1, count)
        def _(off):
            copy(lax.rem(mine + off, count), mine).wait_send()

    return copy, start, received, sent


def rows(ref, size):
    return lambda k: ref.at[pl.ds(pl.multiple_of(k * size, size), size), :]


def kernel(
    dims,
    x_hbm, g_hbm, adj_hbm, convw_hbm, convb_hbm, mixw_hbm, mixb_hbm, send_hbm, cols_ref, counts_ref,
    out_ref, gin_ref, fin,
    xall, g_ref, adj_ref, convw_ref, convb_ref, mixw_ref, mixb_ref, send_ref, bpb, xt, gt, wt, wtt, mcat, mcatv, gm, gmt, dm, dmt, dlo, dlot,
    qg, qqg, filt, gate, hid, hidn, hop1, hop2, bp, part,
    sq1, sq2, sf1, sf2, rq1, rq2, rf1, rf2,
    pay, ra, rc, sum_b, sum_c,
    meta, metax, gx, gxt, far, pick, rx1, rx2, tsend, tback,
    ssem, rsem, assem, arsem, nsem, lsem, fsem, psem, xsem,
):
    n_space, n_dp, n_tm, scale = dims
    me = lax.axis_index("space")
    tm = lax.axis_index("tm")
    dp = lax.axis_index("dp")
    x_ref = xall.at[pl.ds(128, 512), :]
    xb = xall.at[pl.ds(0, 128), :]
    z = lax.div(me, 4)
    y = lax.rem(me, 4)
    z_hi = lax.div(tm, 2)
    core = lax.rem(tm, 2)
    e = dp * 2 + core
    n_e = n_dp * 2
    q = z_hi * 4 + z
    side = lax.div(z, 2)
    end_z = 3 * side
    far_z = 3 - end_z
    is_end = z == end_z
    far_me = far_z * 4 + y
    row_in_side = lax.rem(z, 2) * 4 + y

    def space_dev(k):
        return {"space": k}

    w = e * 4 + y
    n_w = n_e * 4

    def w_dev(k):
        ek = lax.div(k, 4)
        return {"dp": lax.div(ek, 2), "space": z * 4 + lax.rem(k, 4), "tm": z_hi * 2 + lax.rem(ek, 2)}

    def q_dev(k):
        return {"space": lax.rem(k, 4) * 4 + y, "tm": lax.div(k, 4) * 2 + core}

    def signal(dev):
        pl.semaphore_signal(barrier, inc=1, device_id=dev, device_id_type=MESH)

    loads = [
        pltpu.make_async_copy(src, dst, lsem.at[i])
        for i, (src, dst) in enumerate(
            (
                (g_hbm, g_ref), (adj_hbm, adj_ref), (x_hbm, x_ref), (send_hbm, send_ref),
                (convw_hbm, convw_ref), (convb_hbm, convb_ref), (mixw_hbm, mixw_ref), (mixb_hbm, mixb_ref),
            )
        )
    ]
    for load in loads:
        load.start()

    barrier = pltpu.get_barrier_semaphore()

    @pl.loop(1, n_space)
    def _(off):
        signal(space_dev(lax.rem(me + off, n_space)))

    @pl.loop(1, n_w)
    def _(off):
        signal(w_dev(lax.rem(w + off, n_w)))

    @pl.loop(0, 4)
    def _(k):
        signal(q_dev((1 - z_hi) * 4 + k))

    signal({"tm": 3 - tm})

    def halo(i, send, recv):
        return [
            exchange(
                me, n_space, space_dev, rows(send.at[h], SLOTS), rows(recv.at[h], SLOTS),
                ssem.at[2 * i + h], rsem.at[2 * i + h],
            )
            for h in range(2)
        ]

    q1 = halo(0, sq1, rq1)
    q2 = halo(1, sq2, rq2)
    f1 = halo(2, sf1, rf1)
    f2 = halo(3, sf2, rf2)

    def part_of(step, k):
        sd = lax.rem(side + 1 + step, 2)
        first = jnp.where(step == 0, 1 - side, 1 - lax.rem(z, 2))
        return sd * 8 + lax.rem(first + lax.div(k, 4), 2) * 4 + lax.rem(y + k, 4)

    def side_rows(step):
        return pl.ds(pl.multiple_of(lax.rem(side + 1 + step, 2) * 512, 512), 512)

    def slot_block(ref, h, k):
        return ref.at[h, pl.ds(pl.multiple_of(k * SLOTS, SLOTS), SLOTS), :]

    def across(part):
        return is_end & (part // 8 != side)

    def f_spread(ex, field, buf, h):
        copy = ex[h][0]
        lanes = slice(256 * h, 256 * (h + 1))

        @pl.loop(0, 2)
        def _(step):
            @pl.when(jnp.logical_not(is_end & (step == 0)))
            def _():
                at = side_rows(step)
                buf[h, at, :] = nn(gmt[at, :], field[:, lanes]).astype(BF16)

                @pl.loop(0, 8)
                def _(k):
                    tgt = part_of(step, k)

                    @pl.when(tgt != me)
                    def _():
                        copy(tgt, me).start()

    def swap(i, h, field):
        return pltpu.make_async_remote_copy(
            src_ref=field.at[:, pl.ds(256 * h, 256)], dst_ref=far.at[2 * i + h],
            send_sem=fsem.at[0, 2 * i + h], recv_sem=fsem.at[1, 2 * i + h],
            device_id=space_dev(far_me), device_id_type=MESH,
        )

    def f_swap(i, h, field):
        @pl.when(is_end)
        def _():
            swap(i, h, field).start()

    def proxy_copy(i, h, recv, k, tgt):
        return pltpu.make_async_remote_copy(
            src_ref=slot_block(pick, 2 * i + h, k), dst_ref=slot_block(recv, h, far_me),
            send_sem=psem.at[2 * i + h, k], recv_sem=rsem.at[4 + 2 * i + h, far_me],
            device_id=space_dev(tgt), device_id_type=MESH,
        )

    def f_proxy(i, h, field, recv):
        @pl.when(is_end)
        def _():
            swap(i, h, field).wait_recv()

            pick[2 * i + h] = nn(gxt[...], far[2 * i + h]).astype(BF16)

            @pl.loop(0, 8)
            def _(j):
                tgt = part_of(1, j)

                @pl.when(tgt != me)
                def _():
                    proxy_copy(i, h, recv, tgt - side * 8, tgt).start()

            slot_block(recv, h, far_me)[...] = slot_block(pick, 2 * i + h, row_in_side)[...]

    def f_received(i, h, ex, recv, total):
        copy = ex[h][0]
        for half in range(2):
            for k in range(8):
                frm = 8 * half + k

                @pl.when((frm != me) & jnp.logical_not(is_end & (frm == far_me)))
                def _():
                    copy(lax.rem(me + 1, n_space), frm).wait_recv()

            at = slice(512 * half, 512 * (half + 1))
            total = total + nn(dm[:, 256 + 512 * half : 768 + 512 * half], recv[h, at, :])
        return total

    def f_sent(i, h, ex, field, recv):
        copy = ex[h][0]

        @pl.loop(1, n_space)
        def _(off):
            tgt = lax.rem(me + off, n_space)

            @pl.when(jnp.logical_not(across(tgt)))
            def _():
                copy(tgt, me).wait_send()

        @pl.when(is_end)
        def _():
            swap(i, h, field).wait_send()

            @pl.loop(0, 8)
            def _(k):
                @pl.when(k != row_in_side)
                def _():
                    proxy_copy(i, h, recv, k, side * 8 + k).wait_send()

    def collect_copy(i, h, send, rx, s, k):
        return pltpu.make_async_remote_copy(
            src_ref=slot_block(send, h, s), dst_ref=slot_block(rx, h, k),
            send_sem=ssem.at[2 * i + h, s], recv_sem=xsem.at[2 * i + h, k],
            device_id=space_dev(end_z * 4 + lax.rem(s, 4)), device_id_type=MESH,
        )

    def q_spread(i, ex, field, buf, rx, h, build=None):
        copy = ex[h][0]
        lanes = slice(256 * h, 256 * (h + 1))

        @pl.loop(0, 2)
        def _(step):
            if build is not None:
                build(lax.rem(side + 1 + step, 2))
            at = side_rows(step)
            buf[h, at, :] = nn(dmt[at, :], field[:, lanes]).astype(BF16)

            @pl.loop(0, 8)
            def _(k):
                tgt = part_of(step, k)
                to_far = lax.div(tgt, 4) == far_z

                @pl.when(jnp.logical_not(to_far) & (tgt != me))
                def _():
                    copy(tgt, me).start()

                @pl.when(to_far & (jnp.logical_not(is_end) | (tgt != far_me)))
                def _():
                    collect_copy(i, h, buf, rx, tgt, row_in_side).start()

        @pl.when(is_end)
        def _():
            slot_block(rx, h, row_in_side)[...] = slot_block(buf, h, far_me)[...]

    def back_field(i, h):
        return pltpu.make_async_remote_copy(
            src_ref=tsend.at[2 * i + h], dst_ref=tback.at[2 * i + h],
            send_sem=fsem.at[2, 2 * i + h], recv_sem=fsem.at[3, 2 * i + h],
            device_id=space_dev(far_me), device_id_type=MESH,
        )

    def q_collect(i, h, buf, rx):
        @pl.when(is_end)
        def _():
            @pl.loop(0, 8)
            def _(k):
                @pl.when(k != row_in_side)
                def _():
                    collect_copy(i, h, buf, rx, far_me, k).wait_recv()

            tsend[2 * i + h] = nn(gx[...], rx[h]).astype(BF16)
            back_field(i, h).start()

    def q_received(i, h, ex, recv, total):
        copy = ex[h][0]
        for half in range(2):
            for k in range(8):
                frm = 8 * half + k

                @pl.when((frm != me) & jnp.logical_not(across(frm)))
                def _():
                    copy(lax.rem(me + 1, n_space), frm).wait_recv()

            at = slice(512 * half, 512 * (half + 1))
            total = total + nn(gm[:, at], recv[h, at, :])

        @pl.when(is_end)
        def _():
            back_field(i, h).wait_recv()

        return total + tback[2 * i + h].astype(F32)

    def q_sent(i, h, ex, buf, rx):
        copy = ex[h][0]

        @pl.loop(1, n_space)
        def _(off):
            tgt = lax.rem(me + off, n_space)
            zz = lax.div(tgt, 4)

            @pl.when(zz != far_z)
            def _():
                copy(tgt, me).wait_send()

            @pl.when((zz == far_z) & (jnp.logical_not(is_end) | (tgt != far_me)))
            def _():
                collect_copy(i, h, buf, rx, tgt, row_in_side).wait_send()

        @pl.when(is_end)
        def _():
            back_field(i, h).wait_send()

    def meta_copy():
        return pltpu.make_async_remote_copy(
            src_ref=meta, dst_ref=metax, send_sem=nsem.at[4], recv_sem=nsem.at[5],
            device_id=space_dev(far_me), device_id_type=MESH,
        )

    def next_copy():
        return pltpu.make_async_remote_copy(
            src_ref=xall.at[pl.ds(512, 128), :], dst_ref=xb, send_sem=nsem.at[0], recv_sem=nsem.at[1],
            device_id={"tm": lax.rem(tm + 1, n_tm)}, device_id_type=MESH,
        )

    def back_copy():
        return pltpu.make_async_remote_copy(
            src_ref=bp.at[:, pl.ds(0, 256)], dst_ref=bpb, send_sem=nsem.at[2], recv_sem=nsem.at[3],
            device_id={"tm": lax.rem(tm + n_tm - 1, n_tm)}, device_id_type=MESH,
        )

    def tile_sum(r, b, own=False):
        total = None
        for k in range(4):
            slot = k if own else 4 + k
            hit = (cols_ref[r, slot] == b).astype(F32)
            term = adj_ref[r, slot].astype(F32) * hit
            total = term if total is None else total + term
        return total

    loads[0].wait()
    for p in range(4):
        gt[:, 128 * p : 128 * (p + 1)] = g_ref[128 * p : 128 * (p + 1), :].T
    loads[1].wait()

    def build(sd):
        for k in range(4):
            b = 4 * sd + k
            at = pl.ds(pl.multiple_of(b * 128, 128), 128)
            for r in range(2):
                tile = tile_sum(r, b + 2).astype(BF16)
                dm[128 * r : 128 * (r + 1), pl.ds(pl.multiple_of(256 + b * 128, 128), 128)] = tile
                dmt[at, 128 * r : 128 * (r + 1)] = tile.T

    loads[2].wait()
    pl.semaphore_wait(barrier, n_space - 1 + n_w - 1 + 4 + 1)

    @pl.when(tm < n_tm - 1)
    def _():
        next_copy().start()

    q_spread(0, q1, gt, sq1, rx1, 0, build)

    own_slots = pl.ds(pl.multiple_of(me * SLOTS, SLOTS), SLOTS)
    for ref in (rq1, rq2, rf1, rf2):
        for h in range(2):
            ref[h, own_slots, :] = jnp.zeros((SLOTS, 256), BF16)
    @pl.when(is_end)
    def _():
        for ref in (rq1, rq2):
            for h in range(2):
                ref[h, pl.ds(pl.multiple_of((1 - side) * 512, 512), 512), :] = jnp.zeros((512, 256), BF16)

    @pl.when(jnp.logical_not(is_end))
    def _():
        tback[...] = jnp.zeros_like(tback)

    for load in loads[3:]:
        load.wait()

    @pl.when(tm == 0)
    def _():
        xb[...] = jnp.zeros((128, 256), BF16)

    @pl.when(tm == n_tm - 1)
    def _():
        bpb[...] = jnp.zeros_like(bpb)

    zero = jnp.zeros((64, 64), F32)

    def pair(w):
        w = w.astype(F32)
        return jnp.concatenate([jnp.concatenate([w, zero], 1), jnp.concatenate([zero, w], 1)], 0)

    for k in range(3):
        block = pair(mixw_ref[k]).astype(BF16)
        mcat[:, 128 * k : 128 * (k + 1)] = block
        mcatv[128 * k : 128 * (k + 1), :] = block
    for half in range(2):
        for tap in range(2):
            block = pair(convw_ref[tap].astype(F32)[:, 64 * half : 64 * (half + 1)]).astype(BF16)
            wtt[128 * tap : 128 * (tap + 1), 128 * half : 128 * (half + 1)] = block
            wt[128 * half : 128 * (half + 1), 128 * tap : 128 * (tap + 1)] = block.T

    for p in range(4):
        xt[:, 128 * (p + 1) : 128 * (p + 2)] = x_ref[128 * p : 128 * (p + 1), :].T

    b = convb_ref[...]
    bias = jnp.concatenate([b[:, :64], b[:, :64], b[:, 64:], b[:, 64:]], 1)

    def conv(p):
        lanes = slice(128 * p, 128 * (p + 1))
        pre = nt(xt[:, 128 * p : 128 * p + 256], wt[...]) + bias
        f = jnp.tanh(pre[:, :128])
        s = jax.nn.sigmoid(pre[:, 128:])
        filt[:, lanes] = f
        gate[:, lanes] = s
        hid[:, lanes] = (f * s).astype(BF16)

    for p in (2, 3):
        conv(p)
    f_swap(0, 1, hid)
    slot = lax.broadcasted_iota(jnp.int32, (1, SLOTS), 1)
    for d in range(16):
        picks = jnp.where(slot < counts_ref[0, d], send_ref[d : d + 1, :], -1)
        meta[d : d + 1, :] = jnp.concatenate([picks, picks], 1)

    @pl.when(is_end)
    def _():
        meta_copy().start()

    q_spread(0, q1, gt, sq1, rx1, 1)
    conv(1)

    sensor = lax.broadcasted_iota(jnp.int32, (256, 128), 0)
    low_row = lax.broadcasted_iota(jnp.int32, (1, 128), 1) < 64

    def select(first, second):
        return (sensor == jnp.where(low_row, first, second)).astype(F32).astype(BF16)

    for m in range(8):
        sel = select(meta[2 * m : 2 * m + 1, :], meta[2 * m + 1 : 2 * m + 2, :])
        gm[:, 128 * m : 128 * (m + 1)] = sel
        gmt[128 * m : 128 * (m + 1), :] = sel.T

    f_spread(f1, hid, sf1, 1)

    @pl.when(tm > 0)
    def _():
        next_copy().wait_recv()

    xt[:, 0:128] = xb[...].T
    conv(0)
    f_swap(0, 0, hid)

    for b in range(2):
        for r in range(2):
            total = tile_sum(r, b, True)
            high = total.astype(BF16)
            low = (total - high.astype(F32)).astype(BF16)
            here = slice(128 * r, 128 * (r + 1)), slice(128 * b, 128 * (b + 1))
            dm[here] = high
            dlo[here] = low
            dlot[128 * b : 128 * (b + 1), 128 * r : 128 * (r + 1)] = high.T
            dlot[128 * b : 128 * (b + 1), 256 + 128 * r : 256 + 128 * (r + 1)] = low.T

    @pl.when(is_end)
    def _():
        meta_copy().wait_recv()
        for m in range(4):
            d = side * 8 + 2 * m
            sel = select(metax[pl.ds(d, 1), :], metax[pl.ds(d + 1, 1), :])
            gx[:, 128 * m : 128 * (m + 1)] = sel
            gxt[128 * m : 128 * (m + 1), :] = sel.T

    def own_back(field, h):
        grad = field[:, 256 * h : 256 * (h + 1)]
        return nn(dlot[:, :256], grad) + nn(dlot[:, 256:], grad)

    q_collect(0, 0, sq1, rx1)
    f_proxy(0, 1, hid, rf1)
    q_collect(0, 1, sq1, rx1)
    for h in range(2):
        own = own_back(gt, h)
        qg[:, 256 * h : 256 * (h + 1)] = q_received(0, h, q1, rq1, own).astype(BF16)
        q_spread(1, q2, qg, sq2, rx2, h)

    def hop(i, h, ex, src, dst, recv):
        lanes = slice(256 * h, 256 * (h + 1))
        field = src[:, lanes]
        own = nn(dm[:, :256], field) + nn(dlo[...], field)
        dst[:, lanes] = f_received(i, h, ex, recv, own).astype(BF16)

    f_spread(f1, hid, sf1, 0)
    f_proxy(0, 0, hid, rf1)
    for p in range(4):
        lanes = slice(128 * p, 128 * (p + 1))
        hidn[lanes, :] = hid[:, lanes].T
    gsum = jnp.zeros((1, 128), F32)
    for p in range(4):
        gsum = gsum + jnp.sum(gt[:, 128 * p : 128 * (p + 1)].astype(F32), axis=0, keepdims=True)
    hop(0, 1, f1, hid, hop1, rf1)
    f_swap(1, 1, hop1)
    f_spread(f2, hop1, sf2, 1)
    for h in range(2):
        q_collect(1, h, sq2, rx2)

    low_lanes = lax.broadcasted_iota(jnp.int32, (64, 128), 1) < 64

    def diag_low(a):
        return a[:64] + pltpu.roll(a[64:], 64, 1)

    def diag_high(a):
        return pltpu.roll(a[:64], 64, 1) + a[64:]

    bsum = jnp.zeros((1, 256), F32)
    accs = [None] * 2

    def add(i, term):
        accs[i] = term if accs[i] is None else accs[i] + term

    for h in range(2):
        own = own_back(qg, h)
        qqg[:, 256 * h : 256 * (h + 1)] = q_received(1, h, q2, rq2, own).astype(BF16)
        for p in (2 * h, 2 * h + 1):
            lanes = slice(128 * p, 128 * (p + 1))
            three = jnp.concatenate([gt[:, lanes], qg[:, lanes], qqg[:, lanes]], 1)
            bh = nn(three, mcatv[...])
            f = filt[:, lanes]
            s = gate[:, lanes]
            gf = (bh * (1.0 - f * f) * s).astype(BF16)
            gg = (bh * f * s * (1.0 - s)).astype(BF16)
            bp[:, 256 * p : 256 * p + 128] = gf
            bp[:, 256 * p + 128 : 256 * (p + 1)] = gg
            if p == 0:
                @pl.when(tm > 0)
                def _():
                    back_copy().start()
            bsum = bsum + jnp.concatenate(
                [
                    jnp.sum(gf.astype(F32), axis=0, keepdims=True),
                    jnp.sum(gg.astype(F32), axis=0, keepdims=True),
                ],
                1,
            )
            add(0, nn(hidn[lanes, :], three))
            add(1, nn(xall[128 * p : 128 * p + 256, :], bp[:, 256 * p : 256 * (p + 1)]))
        if h == 0:
            f_proxy(1, 1, hop1, rf2)
    row = lax.broadcasted_iota(jnp.int32, (64, 128), 0)
    f_sum = bsum[:, :128]
    g_sum = bsum[:, 128:]
    f_sum = f_sum + pltpu.roll(f_sum, 64, 1)
    g_sum = g_sum + pltpu.roll(g_sum, 64, 1)
    o_sum = gsum + pltpu.roll(gsum, 64, 1)
    extra = jnp.where(row == 0, f_sum, jnp.where(row == 1, g_sum, jnp.where(row == 2, o_sum, 0.0)))
    pay[0:64, :] = jnp.where(low_lanes, diag_low(accs[0][:, :128]), diag_high(accs[0][:, 128:256]))
    pay[64:128, :] = jnp.where(low_lanes, diag_low(accs[0][:, 256:]), extra)
    for tap in range(2):
        acc = accs[1][128 * tap : 128 * (tap + 1)]
        pay[128 + 64 * tap : 192 + 64 * tap, :] = jnp.where(
            low_lanes, diag_low(acc[:, :128]), diag_high(acc[:, 128:])
        )

    s1 = exchange(w, n_w, w_dev, rows(pay, 8), rows(ra, 8), assem.at[0], arsem.at[0])
    s2 = exchange(q, 8, q_dev, lambda k: sum_b, rows(rc, 8), assem.at[1], arsem.at[1])
    s3 = exchange(w, n_w, w_dev, lambda k: sum_c, rows(fin, 8), assem.at[2], arsem.at[2])

    def total_of(ref, count, size):
        total = ref[0:size, :]
        for k in range(1, count):
            total = total + ref[size * k : size * (k + 1), :]
        return total

    def place(k, size):
        return pl.ds(pl.multiple_of(k * size, size), size)

    ra[place(w, 8), :] = pay[place(w, 8), :]
    s1[1]()

    def grad_in(p):
        lanes = slice(128 * p, 128 * (p + 1))
        if p < 3:
            here = nt(jnp.concatenate([wtt[128:, :], wtt[:128, :]], 1), bp[:, 256 * p : 256 * p + 512])
        else:
            here = nt(wtt[128:, :], bp[:, 768:]) + nt(wtt[:128, :], bpb[...])
        gin_ref[lanes, :] = (g_ref[lanes, :].astype(F32) + here).astype(BF16)

    mb = mixb_ref[...]
    mb = jnp.broadcast_to(jnp.concatenate([mb, mb], 1), (128, 128)).T
    mb = jnp.concatenate([mb, mb], 1)

    def mixed(p, last):
        lanes = slice(128 * p, 128 * (p + 1))
        if last:
            here = nt(mcat[:, 256:], hop2[:, lanes])
            out_ref[lanes, :] = (part[lanes, :] + here).astype(BF16)
        else:
            here = nt(mcat[:, :256], jnp.concatenate([hid[:, lanes], hop1[:, lanes]], 1))
            part[lanes, :] = x_ref[lanes, :].astype(F32) + mb + here

    hop(0, 0, f1, hid, hop1, rf1)
    f_swap(1, 0, hop1)
    f_spread(f2, hop1, sf2, 0)
    s1[2]()
    total = total_of(ra, n_w, 8)
    sum_b[...] = total
    rc[place(q, 8), :] = total
    s2[1]()
    f_proxy(1, 0, hop1, rf2)
    for p in range(3):
        grad_in(p)
    s2[2]()
    total = total_of(rc, 8, 8) * scale
    sum_c[...] = total
    fin[place(w, 8), :] = total
    s3[1]()
    for p in range(4):
        mixed(p, False)

    @pl.when(tm < n_tm - 1)
    def _():
        back_copy().wait_recv()

    grad_in(3)
    for h in range(2):
        q_sent(0, h, q1, sq1, rx1)
        q_sent(1, h, q2, sq2, rx2)
        f_sent(0, h, f1, hid, rf1)
    s1[3]()
    s2[3]()

    @pl.when(is_end)
    def _():
        meta_copy().wait_send()

    @pl.when(tm < n_tm - 1)
    def _():
        next_copy().wait_send()

    @pl.when(tm > 0)
    def _():
        back_copy().wait_send()

    for h in (1, 0):
        hop(1, h, f2, hop1, hop2, rf2)
        mixed(2 * h, True)
        mixed(2 * h + 1, True)
    s3[2]()
    s3[3]()
    for h in range(2):
        f_sent(1, h, f2, hop1, rf2)


def finish(out_in, gin_in, fin, out_ref, gin_ref, gcw_ref, gcb_ref, gmw_ref, gmb_ref):
    out_ref[...] = out_in[...]
    gin_ref[...] = gin_in[...]
    two = fin[0:64, :].T
    gmw_ref[0] = two[0:64]
    gmw_ref[1] = two[64:128]
    gmw_ref[2] = fin[64:128, :].T[0:64]
    for tap in range(2):
        gcw_ref[tap] = fin[128 + 64 * tap : 192 + 64 * tap, :]
    tail = fin[64:72, :]
    low = lax.broadcasted_iota(jnp.int32, (1, 128), 1) < 64
    gcb_ref[...] = jnp.where(low, pltpu.roll(tail[0:1], 64, 1), tail[1:2])
    gmb_ref[...] = pltpu.roll(tail[2:3], 64, 1)[:, 0:64]


def body(dims, inputs, grad_out, conv_w, conv_b, mix_w, mix_b, adj_tiles, tile_cols, send_rows, counts):
    x = inputs.reshape(512, 256)
    g = grad_out.reshape(512, 256)
    vmem = pl.BlockSpec(memory_space=pltpu.VMEM)
    smem = pl.BlockSpec(memory_space=pltpu.SMEM)
    hbm = pl.BlockSpec(memory_space=pltpu.HBM)
    n_space = dims[0]
    n_e = dims[1] * 2

    def bf(*shape):
        return pltpu.VMEM(shape, BF16)

    def fl(*shape):
        return pltpu.VMEM(shape, F32)

    def dma(*shape):
        return pltpu.SemaphoreType.DMA(shape)

    scratch = [
        bf(640, 256), bf(512, 256), bf(2, 8, 128, 128), bf(2, 64, 128), fl(1, 128), bf(3, 64, 64), fl(1, 64),
        pltpu.VMEM((16, SLOTS), jnp.int32), bf(256, 256), bf(256, 640), bf(256, 512),
        bf(256, 256), bf(256, 256), bf(128, 384), bf(384, 128),
        bf(256, 1024), bf(1024, 256), bf(256, 1280), bf(1024, 256), bf(256, 256), bf(256, 512),
        bf(256, 512), bf(256, 512), fl(256, 512), fl(256, 512), bf(256, 512), bf(512, 256),
        bf(256, 512), bf(256, 512), bf(256, 1024), fl(512, 256),
    ]
    scratch += [bf(2, 1024, 256)] * 8
    scratch += [fl(256, 128), fl(256, 128), fl(64, 128), fl(8, 128), fl(8, 128)]
    ints = pltpu.VMEM((16, 128), jnp.int32)
    scratch += [ints, ints, bf(256, 512), bf(512, 256), bf(4, 256, 256), bf(4, 512, 256), bf(2, 512, 256), bf(2, 512, 256)]
    scratch += [bf(4, 256, 256), bf(4, 256, 256)]
    scratch += [dma(8, n_space), dma(8, n_space), dma(3, 4 * n_e), dma(3, 4 * n_e), dma(6), dma(8)]
    scratch += [dma(4, 4), dma(4, 8), dma(4, 8)]
    out, gin, fin = pl.pallas_call(
        functools.partial(kernel, dims),
        out_shape=(
            jax.ShapeDtypeStruct((512, 256), BF16),
            jax.ShapeDtypeStruct((512, 256), BF16),
            jax.ShapeDtypeStruct((256, 128), F32),
        ),
        in_specs=[hbm] * 8 + [smem] * 2,
        out_specs=(vmem,) * 3,
        scratch_shapes=scratch,
        compiler_params=pltpu.CompilerParams(
            collective_id=0, has_side_effects=True, vmem_limit_bytes=60 * 2**20
        ),
    )(
        x, g, adj_tiles, jnp.swapaxes(conv_w, 1, 2), conv_b.reshape(1, 128), mix_w, mix_b.reshape(1, 64),
        send_rows[0], tile_cols, counts,
    )
    out, gin, gcw, gcb, gmw, gmb = pl.pallas_call(
        finish,
        out_shape=(
            jax.ShapeDtypeStruct((512, 256), BF16),
            jax.ShapeDtypeStruct((512, 256), BF16),
            jax.ShapeDtypeStruct((2, 64, 128), F32),
            jax.ShapeDtypeStruct((1, 128), F32),
            jax.ShapeDtypeStruct((3, 64, 64), F32),
            jax.ShapeDtypeStruct((1, 64), F32),
        ),
        in_specs=[vmem] * 3,
        out_specs=(vmem,) * 6,
    )(out, gin, fin)
    return (
        out.reshape(inputs.shape),
        gin.reshape(inputs.shape),
        jnp.swapaxes(gcw, 1, 2),
        gcb.reshape(128),
        gmw,
        gmb.reshape(64),
    )


def solution(mesh):
    in_specs = (
        P("dp", "tm", None, "space"),
        P("dp", "tm", None, "space"),
        P(),
        P(),
        P(),
        P(),
        P("space", None, None, None),
        P("space", None),
        P("space", None, None),
        P("space", None),
    )
    out_specs = (P("dp", "tm", None, "space"), P("dp", "tm", None, "space"), P(), P(), P(), P())
    cells = 8 * 256 * mesh.shape["dp"] * mesh.shape["space"] * mesh.shape["tm"]
    dims = (mesh.shape["space"], mesh.shape["dp"], mesh.shape["tm"], 1.0 / math.sqrt(cells))
    return jax.shard_map(
        functools.partial(body, dims), mesh=mesh, in_specs=in_specs, out_specs=out_specs, check_vma=False
    )
```

```python
import functools
import math

import jax
import jax.numpy as jnp
from jax import lax
from jax.experimental import pallas as pl
from jax.experimental.pallas import tpu as pltpu
from jax.sharding import PartitionSpec as P

MESH = pl.DeviceIdType.MESH
F32 = jnp.float32
BF16 = jnp.bfloat16
SLOTS = 64


def nn(a, b):
    return jnp.dot(a, b, preferred_element_type=F32)


def nt(a, b):
    return lax.dot_general(a, b, (((1,), (1,)), ((), ())), preferred_element_type=F32)


def exchange(mine, count, dev, src, dst, ss, rs):
    def copy(tgt, frm):
        return pltpu.make_async_remote_copy(
            src_ref=src(tgt), dst_ref=dst(frm), send_sem=ss.at[tgt], recv_sem=rs.at[frm],
            device_id=dev(tgt), device_id_type=MESH,
        )

    def start():
        @pl.loop(1, count)
        def _(off):
            copy(lax.rem(mine + off, count), mine).start()

    def received():
        @pl.loop(1, count)
        def _(off):
            copy(lax.rem(mine + off, count), lax.rem(mine + (count - off), count)).wait_recv()

    def sent():
        @pl.loop(1, count)
        def _(off):
            copy(lax.rem(mine + off, count), mine).wait_send()

    return copy, start, received, sent


def rows(ref, size):
    return lambda k: ref.at[pl.ds(pl.multiple_of(k * size, size), size), :]


def kernel(
    dims,
    x_hbm, g_hbm, adj_hbm, convw_hbm, convb_hbm, mixw_hbm, mixb_hbm, send_hbm, cols_ref, counts_ref,
    out_hbm, gin_hbm, fin_hbm,
    out_ref, gin_ref, fin,
    xall, g_ref, adj_ref, convw_ref, convb_ref, mixw_ref, mixb_ref, send_ref, bpb, xt, gt, wt, wtt, mcat, mcatv, gm, gmt, dm, dmt, dlo, dlot,
    qg, qqg, filt, gate, hid, hidn, hop1, hop2, bp, part,
    sq1, sq2, sf1, sf2, rq1, rq2, rf1, rf2,
    pay, ra, rc, sum_b, sum_c,
    meta, metax, gx, gxt, far, pick, rx1, rx2, tsend, tback,
    ssem, rsem, assem, arsem, nsem, lsem, fsem, psem, xsem, osem,
):
    n_space, n_dp, n_tm, scale = dims
    me = lax.axis_index("space")
    tm = lax.axis_index("tm")
    dp = lax.axis_index("dp")
    x_ref = xall.at[pl.ds(128, 512), :]
    xb = xall.at[pl.ds(0, 128), :]
    z = lax.div(me, 4)
    y = lax.rem(me, 4)
    z_hi = lax.div(tm, 2)
    core = lax.rem(tm, 2)
    e = dp * 2 + core
    n_e = n_dp * 2
    q = z_hi * 4 + z
    side = lax.div(z, 2)
    end_z = 3 * side
    far_z = 3 - end_z
    is_end = z == end_z
    far_me = far_z * 4 + y
    row_in_side = lax.rem(z, 2) * 4 + y

    def space_dev(k):
        return {"space": k}

    w = e * 4 + y
    n_w = n_e * 4

    def w_dev(k):
        ek = lax.div(k, 4)
        return {"dp": lax.div(ek, 2), "space": z * 4 + lax.rem(k, 4), "tm": z_hi * 2 + lax.rem(ek, 2)}

    def q_dev(k):
        return {"space": lax.rem(k, 4) * 4 + y, "tm": lax.div(k, 4) * 2 + core}

    def signal(dev):
        pl.semaphore_signal(barrier, inc=1, device_id=dev, device_id_type=MESH)

    loads = [
        pltpu.make_async_copy(src, dst, lsem.at[i])
        for i, (src, dst) in enumerate(
            (
                (g_hbm, g_ref), (adj_hbm, adj_ref), (x_hbm, x_ref), (send_hbm, send_ref),
                (convw_hbm, convw_ref), (convb_hbm, convb_ref), (mixw_hbm, mixw_ref), (mixb_hbm, mixb_ref),
            )
        )
    ]
    for load in loads:
        load.start()

    parts = [(gin_ref, gin_hbm)]
    parts += [(ref.at[pl.ds(256 * h, 256), :], dst.at[pl.ds(256 * h, 256), :]) for h in range(2) for ref, dst in ((out_ref, out_hbm),)]
    parts += [(fin, fin_hbm)]
    stores = [pltpu.make_async_copy(src, dst, osem.at[i]) for i, (src, dst) in enumerate(parts)]

    barrier = pltpu.get_barrier_semaphore()

    @pl.loop(1, n_space)
    def _(off):
        signal(space_dev(lax.rem(me + off, n_space)))

    @pl.loop(1, n_w)
    def _(off):
        signal(w_dev(lax.rem(w + off, n_w)))

    @pl.loop(0, 4)
    def _(k):
        signal(q_dev((1 - z_hi) * 4 + k))

    signal({"tm": 3 - tm})

    def halo(i, send, recv):
        return [
            exchange(
                me, n_space, space_dev, rows(send.at[h], SLOTS), rows(recv.at[h], SLOTS),
                ssem.at[2 * i + h], rsem.at[2 * i + h],
            )
            for h in range(2)
        ]

    q1 = halo(0, sq1, rq1)
    q2 = halo(1, sq2, rq2)
    f1 = halo(2, sf1, rf1)
    f2 = halo(3, sf2, rf2)

    def part_of(step, k):
        sd = lax.rem(side + 1 + step, 2)
        first = jnp.where(step == 0, 1 - side, 1 - lax.rem(z, 2))
        return sd * 8 + lax.rem(first + lax.div(k, 4), 2) * 4 + lax.rem(y + k, 4)

    def side_rows(step):
        return pl.ds(pl.multiple_of(lax.rem(side + 1 + step, 2) * 512, 512), 512)

    def slot_block(ref, h, k):
        return ref.at[h, pl.ds(pl.multiple_of(k * SLOTS, SLOTS), SLOTS), :]

    def across(part):
        return is_end & (part // 8 != side)

    def f_spread(ex, field, buf, h):
        copy = ex[h][0]
        lanes = slice(256 * h, 256 * (h + 1))

        @pl.loop(0, 2)
        def _(step):
            @pl.when(jnp.logical_not(is_end & (step == 0)))
            def _():
                at = side_rows(step)
                buf[h, at, :] = nn(gmt[at, :], field[:, lanes]).astype(BF16)

                @pl.loop(0, 8)
                def _(k):
                    tgt = part_of(step, k)

                    @pl.when(tgt != me)
                    def _():
                        copy(tgt, me).start()

    def swap(i, h, field):
        return pltpu.make_async_remote_copy(
            src_ref=field.at[:, pl.ds(256 * h, 256)], dst_ref=far.at[2 * i + h],
            send_sem=fsem.at[0, 2 * i + h], recv_sem=fsem.at[1, 2 * i + h],
            device_id=space_dev(far_me), device_id_type=MESH,
        )

    def f_swap(i, h, field):
        @pl.when(is_end)
        def _():
            swap(i, h, field).start()

    def proxy_copy(i, h, recv, k, tgt):
        return pltpu.make_async_remote_copy(
            src_ref=slot_block(pick, 2 * i + h, k), dst_ref=slot_block(recv, h, far_me),
            send_sem=psem.at[2 * i + h, k], recv_sem=rsem.at[4 + 2 * i + h, far_me],
            device_id=space_dev(tgt), device_id_type=MESH,
        )

    def f_proxy(i, h, field, recv):
        @pl.when(is_end)
        def _():
            swap(i, h, field).wait_recv()

            pick[2 * i + h] = nn(gxt[...], far[2 * i + h]).astype(BF16)

            @pl.loop(0, 8)
            def _(j):
                tgt = part_of(1, j)

                @pl.when(tgt != me)
                def _():
                    proxy_copy(i, h, recv, tgt - side * 8, tgt).start()

            slot_block(recv, h, far_me)[...] = slot_block(pick, 2 * i + h, row_in_side)[...]

    def f_received(i, h, ex, recv, total):
        copy = ex[h][0]
        for half in range(2):
            for k in range(8):
                frm = 8 * half + k

                @pl.when((frm != me) & jnp.logical_not(is_end & (frm == far_me)))
                def _():
                    copy(lax.rem(me + 1, n_space), frm).wait_recv()

            at = slice(512 * half, 512 * (half + 1))
            total = total + nn(dm[:, 256 + 512 * half : 768 + 512 * half], recv[h, at, :])
        return total

    def f_sent(i, h, ex, field, recv):
        copy = ex[h][0]

        @pl.loop(1, n_space)
        def _(off):
            tgt = lax.rem(me + off, n_space)

            @pl.when(jnp.logical_not(across(tgt)))
            def _():
                copy(tgt, me).wait_send()

        @pl.when(is_end)
        def _():
            swap(i, h, field).wait_send()

            @pl.loop(0, 8)
            def _(k):
                @pl.when(k != row_in_side)
                def _():
                    proxy_copy(i, h, recv, k, side * 8 + k).wait_send()

    def collect_copy(i, h, send, rx, s, k):
        return pltpu.make_async_remote_copy(
            src_ref=slot_block(send, h, s), dst_ref=slot_block(rx, h, k),
            send_sem=ssem.at[2 * i + h, s], recv_sem=xsem.at[2 * i + h, k],
            device_id=space_dev(end_z * 4 + lax.rem(s, 4)), device_id_type=MESH,
        )

    def q_spread(i, ex, field, buf, rx, h, build=None):
        copy = ex[h][0]
        lanes = slice(256 * h, 256 * (h + 1))

        @pl.loop(0, 2)
        def _(step):
            if build is not None:
                build(lax.rem(side + 1 + step, 2))
            at = side_rows(step)
            buf[h, at, :] = nn(dmt[at, :], field[:, lanes]).astype(BF16)

            @pl.loop(0, 8)
            def _(k):
                tgt = part_of(step, k)
                to_far = lax.div(tgt, 4) == far_z

                @pl.when(jnp.logical_not(to_far) & (tgt != me))
                def _():
                    copy(tgt, me).start()

                @pl.when(to_far & (jnp.logical_not(is_end) | (tgt != far_me)))
                def _():
                    collect_copy(i, h, buf, rx, tgt, row_in_side).start()

        @pl.when(is_end)
        def _():
            slot_block(rx, h, row_in_side)[...] = slot_block(buf, h, far_me)[...]

    def back_field(i, h):
        return pltpu.make_async_remote_copy(
            src_ref=tsend.at[2 * i + h], dst_ref=tback.at[2 * i + h],
            send_sem=fsem.at[2, 2 * i + h], recv_sem=fsem.at[3, 2 * i + h],
            device_id=space_dev(far_me), device_id_type=MESH,
        )

    def q_collect(i, h, buf, rx):
        @pl.when(is_end)
        def _():
            @pl.loop(0, 8)
            def _(k):
                @pl.when(k != row_in_side)
                def _():
                    collect_copy(i, h, buf, rx, far_me, k).wait_recv()

            tsend[2 * i + h] = nn(gx[...], rx[h]).astype(BF16)
            back_field(i, h).start()

    def q_received(i, h, ex, recv, total):
        copy = ex[h][0]
        for half in range(2):
            for k in range(8):
                frm = 8 * half + k

                @pl.when((frm != me) & jnp.logical_not(across(frm)))
                def _():
                    copy(lax.rem(me + 1, n_space), frm).wait_recv()

            at = slice(512 * half, 512 * (half + 1))
            total = total + nn(gm[:, at], recv[h, at, :])

        @pl.when(is_end)
        def _():
            back_field(i, h).wait_recv()

        return total + tback[2 * i + h].astype(F32)

    def q_sent(i, h, ex, buf, rx):
        copy = ex[h][0]

        @pl.loop(1, n_space)
        def _(off):
            tgt = lax.rem(me + off, n_space)
            zz = lax.div(tgt, 4)

            @pl.when(zz != far_z)
            def _():
                copy(tgt, me).wait_send()

            @pl.when((zz == far_z) & (jnp.logical_not(is_end) | (tgt != far_me)))
            def _():
                collect_copy(i, h, buf, rx, tgt, row_in_side).wait_send()

        @pl.when(is_end)
        def _():
            back_field(i, h).wait_send()

    def meta_copy():
        return pltpu.make_async_remote_copy(
            src_ref=meta, dst_ref=metax, send_sem=nsem.at[4], recv_sem=nsem.at[5],
            device_id=space_dev(far_me), device_id_type=MESH,
        )

    def next_copy():
        return pltpu.make_async_remote_copy(
            src_ref=xall.at[pl.ds(512, 128), :], dst_ref=xb, send_sem=nsem.at[0], recv_sem=nsem.at[1],
            device_id={"tm": lax.rem(tm + 1, n_tm)}, device_id_type=MESH,
        )

    def back_copy():
        return pltpu.make_async_remote_copy(
            src_ref=bp.at[:, pl.ds(0, 256)], dst_ref=bpb, send_sem=nsem.at[2], recv_sem=nsem.at[3],
            device_id={"tm": lax.rem(tm + n_tm - 1, n_tm)}, device_id_type=MESH,
        )

    def tile_sum(r, b, own=False):
        total = None
        for k in range(4):
            slot = k if own else 4 + k
            hit = (cols_ref[r, slot] == b).astype(F32)
            term = adj_ref[r, slot].astype(F32) * hit
            total = term if total is None else total + term
        return total

    loads[0].wait()
    for p in range(4):
        gt[:, 128 * p : 128 * (p + 1)] = g_ref[128 * p : 128 * (p + 1), :].T
    loads[1].wait()

    def build(sd):
        for k in range(4):
            b = 4 * sd + k
            at = pl.ds(pl.multiple_of(b * 128, 128), 128)
            for r in range(2):
                tile = tile_sum(r, b + 2).astype(BF16)
                dm[128 * r : 128 * (r + 1), pl.ds(pl.multiple_of(256 + b * 128, 128), 128)] = tile
                dmt[at, 128 * r : 128 * (r + 1)] = tile.T

    loads[2].wait()
    pl.semaphore_wait(barrier, n_space - 1 + n_w - 1 + 4 + 1)

    @pl.when(tm < n_tm - 1)
    def _():
        next_copy().start()

    q_spread(0, q1, gt, sq1, rx1, 0, build)

    own_slots = pl.ds(pl.multiple_of(me * SLOTS, SLOTS), SLOTS)
    for ref in (rq1, rq2, rf1, rf2):
        for h in range(2):
            ref[h, own_slots, :] = jnp.zeros((SLOTS, 256), BF16)
    @pl.when(is_end)
    def _():
        for ref in (rq1, rq2):
            for h in range(2):
                ref[h, pl.ds(pl.multiple_of((1 - side) * 512, 512), 512), :] = jnp.zeros((512, 256), BF16)

    @pl.when(jnp.logical_not(is_end))
    def _():
        tback[...] = jnp.zeros_like(tback)

    for load in loads[3:]:
        load.wait()

    @pl.when(tm == 0)
    def _():
        xb[...] = jnp.zeros((128, 256), BF16)

    @pl.when(tm == n_tm - 1)
    def _():
        bpb[...] = jnp.zeros_like(bpb)

    zero = jnp.zeros((64, 64), F32)

    def pair(w):
        w = w.astype(F32)
        return jnp.concatenate([jnp.concatenate([w, zero], 1), jnp.concatenate([zero, w], 1)], 0)

    for k in range(3):
        block = pair(mixw_ref[k]).astype(BF16)
        mcat[:, 128 * k : 128 * (k + 1)] = block
        mcatv[128 * k : 128 * (k + 1), :] = block
    for half in range(2):
        for tap in range(2):
            block = pair(convw_ref[tap].astype(F32)[:, 64 * half : 64 * (half + 1)]).astype(BF16)
            wtt[128 * tap : 128 * (tap + 1), 128 * half : 128 * (half + 1)] = block
            wt[128 * half : 128 * (half + 1), 128 * tap : 128 * (tap + 1)] = block.T

    for p in range(4):
        xt[:, 128 * (p + 1) : 128 * (p + 2)] = x_ref[128 * p : 128 * (p + 1), :].T

    b = convb_ref[...]
    bias = jnp.concatenate([b[:, :64], b[:, :64], b[:, 64:], b[:, 64:]], 1)

    def conv(p):
        lanes = slice(128 * p, 128 * (p + 1))
        pre = nt(xt[:, 128 * p : 128 * p + 256], wt[...]) + bias
        f = jnp.tanh(pre[:, :128])
        s = jax.nn.sigmoid(pre[:, 128:])
        filt[:, lanes] = f
        gate[:, lanes] = s
        hid[:, lanes] = (f * s).astype(BF16)

    for p in (2, 3):
        conv(p)
    f_swap(0, 1, hid)
    slot = lax.broadcasted_iota(jnp.int32, (1, SLOTS), 1)
    for d in range(16):
        picks = jnp.where(slot < counts_ref[0, d], send_ref[d : d + 1, :], -1)
        meta[d : d + 1, :] = jnp.concatenate([picks, picks], 1)

    @pl.when(is_end)
    def _():
        meta_copy().start()

    q_spread(0, q1, gt, sq1, rx1, 1)
    conv(1)

    sensor = lax.broadcasted_iota(jnp.int32, (256, 128), 0)
    low_row = lax.broadcasted_iota(jnp.int32, (1, 128), 1) < 64

    def select(first, second):
        return (sensor == jnp.where(low_row, first, second)).astype(F32).astype(BF16)

    for m in range(8):
        sel = select(meta[2 * m : 2 * m + 1, :], meta[2 * m + 1 : 2 * m + 2, :])
        gm[:, 128 * m : 128 * (m + 1)] = sel
        gmt[128 * m : 128 * (m + 1), :] = sel.T

    f_spread(f1, hid, sf1, 1)

    @pl.when(tm > 0)
    def _():
        next_copy().wait_recv()

    xt[:, 0:128] = xb[...].T
    conv(0)
    f_swap(0, 0, hid)

    for b in range(2):
        for r in range(2):
            total = tile_sum(r, b, True)
            high = total.astype(BF16)
            low = (total - high.astype(F32)).astype(BF16)
            here = slice(128 * r, 128 * (r + 1)), slice(128 * b, 128 * (b + 1))
            dm[here] = high
            dlo[here] = low
            dlot[128 * b : 128 * (b + 1), 128 * r : 128 * (r + 1)] = high.T
            dlot[128 * b : 128 * (b + 1), 256 + 128 * r : 256 + 128 * (r + 1)] = low.T

    @pl.when(is_end)
    def _():
        meta_copy().wait_recv()
        for m in range(4):
            d = side * 8 + 2 * m
            sel = select(metax[pl.ds(d, 1), :], metax[pl.ds(d + 1, 1), :])
            gx[:, 128 * m : 128 * (m + 1)] = sel
            gxt[128 * m : 128 * (m + 1), :] = sel.T

    def own_back(field, h):
        grad = field[:, 256 * h : 256 * (h + 1)]
        return nn(dlot[:, :256], grad) + nn(dlot[:, 256:], grad)

    q_collect(0, 0, sq1, rx1)
    f_proxy(0, 1, hid, rf1)
    q_collect(0, 1, sq1, rx1)
    for h in range(2):
        own = own_back(gt, h)
        qg[:, 256 * h : 256 * (h + 1)] = q_received(0, h, q1, rq1, own).astype(BF16)
        q_spread(1, q2, qg, sq2, rx2, h)

    def hop(i, h, ex, src, dst, recv):
        lanes = slice(256 * h, 256 * (h + 1))
        field = src[:, lanes]
        own = nn(dm[:, :256], field) + nn(dlo[...], field)
        dst[:, lanes] = f_received(i, h, ex, recv, own).astype(BF16)

    f_spread(f1, hid, sf1, 0)
    f_proxy(0, 0, hid, rf1)
    for p in range(4):
        lanes = slice(128 * p, 128 * (p + 1))
        hidn[lanes, :] = hid[:, lanes].T
    gsum = jnp.zeros((1, 128), F32)
    for p in range(4):
        gsum = gsum + jnp.sum(gt[:, 128 * p : 128 * (p + 1)].astype(F32), axis=0, keepdims=True)
    hop(0, 1, f1, hid, hop1, rf1)
    f_swap(1, 1, hop1)
    f_spread(f2, hop1, sf2, 1)
    for h in range(2):
        q_collect(1, h, sq2, rx2)

    low_lanes = lax.broadcasted_iota(jnp.int32, (64, 128), 1) < 64

    def diag_low(a):
        return a[:64] + pltpu.roll(a[64:], 64, 1)

    def diag_high(a):
        return pltpu.roll(a[:64], 64, 1) + a[64:]

    bsum = jnp.zeros((1, 256), F32)
    accs = [None] * 2

    def add(i, term):
        accs[i] = term if accs[i] is None else accs[i] + term

    for h in range(2):
        own = own_back(qg, h)
        qqg[:, 256 * h : 256 * (h + 1)] = q_received(1, h, q2, rq2, own).astype(BF16)
        for p in (2 * h, 2 * h + 1):
            lanes = slice(128 * p, 128 * (p + 1))
            three = jnp.concatenate([gt[:, lanes], qg[:, lanes], qqg[:, lanes]], 1)
            bh = nn(three, mcatv[...])
            f = filt[:, lanes]
            s = gate[:, lanes]
            gf = (bh * (1.0 - f * f) * s).astype(BF16)
            gg = (bh * f * s * (1.0 - s)).astype(BF16)
            bp[:, 256 * p : 256 * p + 128] = gf
            bp[:, 256 * p + 128 : 256 * (p + 1)] = gg
            if p == 0:
                @pl.when(tm > 0)
                def _():
                    back_copy().start()
            bsum = bsum + jnp.concatenate(
                [
                    jnp.sum(gf.astype(F32), axis=0, keepdims=True),
                    jnp.sum(gg.astype(F32), axis=0, keepdims=True),
                ],
                1,
            )
            add(0, nn(hidn[lanes, :], three))
            add(1, nn(xall[128 * p : 128 * p + 256, :], bp[:, 256 * p : 256 * (p + 1)]))
        if h == 0:
            f_proxy(1, 1, hop1, rf2)
    row = lax.broadcasted_iota(jnp.int32, (64, 128), 0)
    f_sum = bsum[:, :128]
    g_sum = bsum[:, 128:]
    f_sum = f_sum + pltpu.roll(f_sum, 64, 1)
    g_sum = g_sum + pltpu.roll(g_sum, 64, 1)
    o_sum = gsum + pltpu.roll(gsum, 64, 1)
    extra = jnp.where(row == 0, f_sum, jnp.where(row == 1, g_sum, jnp.where(row == 2, o_sum, 0.0)))
    pay[0:64, :] = jnp.where(low_lanes, diag_low(accs[0][:, :128]), diag_high(accs[0][:, 128:256]))
    pay[64:128, :] = jnp.where(low_lanes, diag_low(accs[0][:, 256:]), extra)
    for tap in range(2):
        acc = accs[1][128 * tap : 128 * (tap + 1)]
        pay[128 + 64 * tap : 192 + 64 * tap, :] = jnp.where(
            low_lanes, diag_low(acc[:, :128]), diag_high(acc[:, 128:])
        )

    s1 = exchange(w, n_w, w_dev, rows(pay, 8), rows(ra, 8), assem.at[0], arsem.at[0])
    s2 = exchange(q, 8, q_dev, lambda k: sum_b, rows(rc, 8), assem.at[1], arsem.at[1])
    s3 = exchange(w, n_w, w_dev, lambda k: sum_c, rows(fin, 8), assem.at[2], arsem.at[2])

    def total_of(ref, count, size):
        total = ref[0:size, :]
        for k in range(1, count):
            total = total + ref[size * k : size * (k + 1), :]
        return total

    def place(k, size):
        return pl.ds(pl.multiple_of(k * size, size), size)

    ra[place(w, 8), :] = pay[place(w, 8), :]
    s1[1]()

    def grad_in(p):
        lanes = slice(128 * p, 128 * (p + 1))
        if p < 3:
            here = nt(jnp.concatenate([wtt[128:, :], wtt[:128, :]], 1), bp[:, 256 * p : 256 * p + 512])
        else:
            here = nt(wtt[128:, :], bp[:, 768:]) + nt(wtt[:128, :], bpb[...])
        gin_ref[lanes, :] = (g_ref[lanes, :].astype(F32) + here).astype(BF16)

    mb = mixb_ref[...]
    mb = jnp.broadcast_to(jnp.concatenate([mb, mb], 1), (128, 128)).T
    mb = jnp.concatenate([mb, mb], 1)

    def mixed(p, last):
        lanes = slice(128 * p, 128 * (p + 1))
        if last:
            here = nt(mcat[:, 256:], hop2[:, lanes])
            out_ref[lanes, :] = (part[lanes, :] + here).astype(BF16)
        else:
            here = nt(mcat[:, :256], jnp.concatenate([hid[:, lanes], hop1[:, lanes]], 1))
            part[lanes, :] = x_ref[lanes, :].astype(F32) + mb + here

    hop(0, 0, f1, hid, hop1, rf1)
    f_swap(1, 0, hop1)
    s1[2]()
    total = total_of(ra, n_w, 8)
    sum_b[...] = total
    rc[place(q, 8), :] = total
    s2[1]()
    f_spread(f2, hop1, sf2, 0)
    for p in range(3):
        grad_in(p)
    s2[2]()
    total = total_of(rc, 8, 8) * scale
    sum_c[...] = total
    fin[place(w, 8), :] = total
    s3[1]()
    f_proxy(1, 0, hop1, rf2)
    for p in range(4):
        mixed(p, False)

    @pl.when(tm < n_tm - 1)
    def _():
        back_copy().wait_recv()

    grad_in(3)
    stores[0].start()
    for h in range(2):
        q_sent(0, h, q1, sq1, rx1)
        q_sent(1, h, q2, sq2, rx2)
        f_sent(0, h, f1, hid, rf1)
    s1[3]()
    s2[3]()

    @pl.when(is_end)
    def _():
        meta_copy().wait_send()

    @pl.when(tm < n_tm - 1)
    def _():
        next_copy().wait_send()

    @pl.when(tm > 0)
    def _():
        back_copy().wait_send()

    for h in (1, 0):
        hop(1, h, f2, hop1, hop2, rf2)
        mixed(2 * h, True)
        mixed(2 * h + 1, True)
        stores[1 + h].start()
    s3[2]()
    stores[3].start()
    s3[3]()
    for h in range(2):
        f_sent(1, h, f2, hop1, rf2)
    for store in stores:
        store.wait()


def finish(out_in, gin_in, fin, out_ref, gin_ref, gcw_ref, gcb_ref, gmw_ref, gmb_ref):
    out_ref[...] = out_in[...]
    gin_ref[...] = gin_in[...]
    two = fin[0:64, :].T
    gmw_ref[0] = two[0:64]
    gmw_ref[1] = two[64:128]
    gmw_ref[2] = fin[64:128, :].T[0:64]
    for tap in range(2):
        gcw_ref[tap] = fin[128 + 64 * tap : 192 + 64 * tap, :]
    tail = fin[64:72, :]
    low = lax.broadcasted_iota(jnp.int32, (1, 128), 1) < 64
    gcb_ref[...] = jnp.where(low, pltpu.roll(tail[0:1], 64, 1), tail[1:2])
    gmb_ref[...] = pltpu.roll(tail[2:3], 64, 1)[:, 0:64]


def body(dims, inputs, grad_out, conv_w, conv_b, mix_w, mix_b, adj_tiles, tile_cols, send_rows, counts):
    x = inputs.reshape(512, 256)
    g = grad_out.reshape(512, 256)
    vmem = pl.BlockSpec(memory_space=pltpu.VMEM)
    smem = pl.BlockSpec(memory_space=pltpu.SMEM)
    hbm = pl.BlockSpec(memory_space=pltpu.HBM)
    n_space = dims[0]
    n_e = dims[1] * 2

    def bf(*shape):
        return pltpu.VMEM(shape, BF16)

    def fl(*shape):
        return pltpu.VMEM(shape, F32)

    def dma(*shape):
        return pltpu.SemaphoreType.DMA(shape)

    scratch = [
        bf(512, 256), bf(512, 256), fl(256, 128),
        bf(640, 256), bf(512, 256), bf(2, 8, 128, 128), bf(2, 64, 128), fl(1, 128), bf(3, 64, 64), fl(1, 64),
        pltpu.VMEM((16, SLOTS), jnp.int32), bf(256, 256), bf(256, 640), bf(256, 512),
        bf(256, 256), bf(256, 256), bf(128, 384), bf(384, 128),
        bf(256, 1024), bf(1024, 256), bf(256, 1280), bf(1024, 256), bf(256, 256), bf(256, 512),
        bf(256, 512), bf(256, 512), fl(256, 512), fl(256, 512), bf(256, 512), bf(512, 256),
        bf(256, 512), bf(256, 512), bf(256, 1024), fl(512, 256),
    ]
    scratch += [bf(2, 1024, 256)] * 8
    scratch += [fl(256, 128), fl(256, 128), fl(64, 128), fl(8, 128), fl(8, 128)]
    ints = pltpu.VMEM((16, 128), jnp.int32)
    scratch += [ints, ints, bf(256, 512), bf(512, 256), bf(4, 256, 256), bf(4, 512, 256), bf(2, 512, 256), bf(2, 512, 256)]
    scratch += [bf(4, 256, 256), bf(4, 256, 256)]
    scratch += [dma(8, n_space), dma(8, n_space), dma(3, 4 * n_e), dma(3, 4 * n_e), dma(6), dma(8)]
    scratch += [dma(4, 4), dma(4, 8), dma(4, 8), dma(4)]
    out, gin, fin = pl.pallas_call(
        functools.partial(kernel, dims),
        out_shape=(
            jax.ShapeDtypeStruct((512, 256), BF16),
            jax.ShapeDtypeStruct((512, 256), BF16),
            jax.ShapeDtypeStruct((256, 128), F32),
        ),
        in_specs=[hbm] * 8 + [smem] * 2,
        out_specs=(hbm,) * 3,
        scratch_shapes=scratch,
        compiler_params=pltpu.CompilerParams(
            collective_id=0, has_side_effects=True, vmem_limit_bytes=60 * 2**20
        ),
    )(
        x, g, adj_tiles, jnp.swapaxes(conv_w, 1, 2), conv_b.reshape(1, 128), mix_w, mix_b.reshape(1, 64),
        send_rows[0], tile_cols, counts,
    )
    out, gin, gcw, gcb, gmw, gmb = pl.pallas_call(
        finish,
        out_shape=(
            jax.ShapeDtypeStruct((512, 256), BF16),
            jax.ShapeDtypeStruct((512, 256), BF16),
            jax.ShapeDtypeStruct((2, 64, 128), F32),
            jax.ShapeDtypeStruct((1, 128), F32),
            jax.ShapeDtypeStruct((3, 64, 64), F32),
            jax.ShapeDtypeStruct((1, 64), F32),
        ),
        in_specs=[vmem] * 3,
        out_specs=(vmem,) * 6,
    )(out, gin, fin)
    return (
        out.reshape(inputs.shape),
        gin.reshape(inputs.shape),
        jnp.swapaxes(gcw, 1, 2),
        gcb.reshape(128),
        gmw,
        gmb.reshape(64),
    )


def solution(mesh):
    in_specs = (
        P("dp", "tm", None, "space"),
        P("dp", "tm", None, "space"),
        P(),
        P(),
        P(),
        P(),
        P("space", None, None, None),
        P("space", None),
        P("space", None, None),
        P("space", None),
    )
    out_specs = (P("dp", "tm", None, "space"), P("dp", "tm", None, "space"), P(), P(), P(), P())
    cells = 8 * 256 * mesh.shape["dp"] * mesh.shape["space"] * mesh.shape["tm"]
    dims = (mesh.shape["space"], mesh.shape["dp"], mesh.shape["tm"], 1.0 / math.sqrt(cells))
    return jax.shard_map(
        functools.partial(body, dims), mesh=mesh, in_specs=in_specs, out_specs=out_specs, check_vma=False
    )
```

```python
import functools
import math

import jax
import jax.numpy as jnp
from jax import lax
from jax.experimental import pallas as pl
from jax.experimental.pallas import tpu as pltpu
from jax.sharding import PartitionSpec as P

MESH = pl.DeviceIdType.MESH
F32 = jnp.float32
BF16 = jnp.bfloat16
SLOTS = 64


def nn(a, b):
    return jnp.dot(a, b, preferred_element_type=F32)


def nt(a, b):
    return lax.dot_general(a, b, (((1,), (1,)), ((), ())), preferred_element_type=F32)


def exchange(mine, count, dev, src, dst, ss, rs):
    def copy(tgt, frm):
        return pltpu.make_async_remote_copy(
            src_ref=src(tgt), dst_ref=dst(frm), send_sem=ss.at[tgt], recv_sem=rs.at[frm],
            device_id=dev(tgt), device_id_type=MESH,
        )

    def start():
        @pl.loop(1, count)
        def _(off):
            copy(lax.rem(mine + off, count), mine).start()

    def received():
        @pl.loop(1, count)
        def _(off):
            copy(lax.rem(mine + off, count), lax.rem(mine + (count - off), count)).wait_recv()

    def sent():
        @pl.loop(1, count)
        def _(off):
            copy(lax.rem(mine + off, count), mine).wait_send()

    return copy, start, received, sent


def rows(ref, size):
    return lambda k: ref.at[pl.ds(pl.multiple_of(k * size, size), size), :]


def kernel(
    dims,
    x_hbm, g_hbm, adj_hbm, convw_hbm, convb_hbm, mixw_hbm, mixb_hbm, send_hbm, cols_ref, counts_ref,
    out_hbm, gin_hbm, fin_hbm,
    out_ref, gin_ref, fin,
    xall, g_ref, adj_ref, convw_ref, convb_ref, mixw_ref, mixb_ref, send_ref, bps, bpb, xt, gt, wt, wtt, mcat, mcatv, gm, gmt, dm, dmt, dlo, dlot,
    qg, qqg, filt, gate, hid, hidn, hop1, hop2, bp, part,
    sq1, sq2, sf1, sf2, rq1, rq2, rf1, rf2,
    pay, ra, rc, sum_b, sum_c,
    meta, metax, gx, gxt, far, pick, rx1, rx2, tsend, tback,
    ssem, rsem, assem, arsem, nsem, lsem, fsem, psem, xsem, osem,
):
    n_space, n_dp, n_tm, scale = dims
    me = lax.axis_index("space")
    tm = lax.axis_index("tm")
    dp = lax.axis_index("dp")
    x_ref = xall.at[pl.ds(128, 512), :]
    xb = xall.at[pl.ds(0, 128), :]
    z = lax.div(me, 4)
    y = lax.rem(me, 4)
    z_hi = lax.div(tm, 2)
    core = lax.rem(tm, 2)
    e = dp * 2 + core
    n_e = n_dp * 2
    q = z_hi * 4 + z
    side = lax.div(z, 2)
    end_z = 3 * side
    far_z = 3 - end_z
    is_end = z == end_z
    far_me = far_z * 4 + y
    row_in_side = lax.rem(z, 2) * 4 + y

    def space_dev(k):
        return {"space": k}

    w = e * 4 + y
    n_w = n_e * 4

    def w_dev(k):
        ek = lax.div(k, 4)
        return {"dp": lax.div(ek, 2), "space": z * 4 + lax.rem(k, 4), "tm": z_hi * 2 + lax.rem(ek, 2)}

    def q_dev(k):
        return {"space": lax.rem(k, 4) * 4 + y, "tm": lax.div(k, 4) * 2 + core}

    def signal(dev):
        pl.semaphore_signal(barrier, inc=1, device_id=dev, device_id_type=MESH)

    loads = [
        pltpu.make_async_copy(src, dst, lsem.at[i])
        for i, (src, dst) in enumerate(
            (
                (g_hbm, g_ref), (adj_hbm, adj_ref), (x_hbm, x_ref), (send_hbm, send_ref),
                (convw_hbm, convw_ref), (convb_hbm, convb_ref), (mixw_hbm, mixw_ref), (mixb_hbm, mixb_ref),
            )
        )
    ]
    for load in loads:
        load.start()

    parts = [(gin_ref, gin_hbm)]
    parts += [(ref.at[pl.ds(256 * h, 256), :], dst.at[pl.ds(256 * h, 256), :]) for h in range(2) for ref, dst in ((out_ref, out_hbm),)]
    parts += [(fin, fin_hbm)]
    stores = [pltpu.make_async_copy(src, dst, osem.at[i]) for i, (src, dst) in enumerate(parts)]

    barrier = pltpu.get_barrier_semaphore()

    @pl.loop(1, n_space)
    def _(off):
        signal(space_dev(lax.rem(me + off, n_space)))

    @pl.loop(1, n_w)
    def _(off):
        signal(w_dev(lax.rem(w + off, n_w)))

    @pl.loop(0, 4)
    def _(k):
        signal(q_dev((1 - z_hi) * 4 + k))

    signal({"tm": 3 - tm})

    def halo(i, send, recv):
        return [
            exchange(
                me, n_space, space_dev, rows(send.at[h], SLOTS), rows(recv.at[h], SLOTS),
                ssem.at[2 * i + h], rsem.at[2 * i + h],
            )
            for h in range(2)
        ]

    q1 = halo(0, sq1, rq1)
    q2 = halo(1, sq2, rq2)
    f1 = halo(2, sf1, rf1)
    f2 = halo(3, sf2, rf2)

    def part_of(step, k):
        sd = lax.rem(side + 1 + step, 2)
        first = jnp.where(step == 0, 1 - side, 1 - lax.rem(z, 2))
        return sd * 8 + lax.rem(first + lax.div(k, 4), 2) * 4 + lax.rem(y + k, 4)

    def side_rows(step):
        return pl.ds(pl.multiple_of(lax.rem(side + 1 + step, 2) * 512, 512), 512)

    def slot_block(ref, h, k):
        return ref.at[h, pl.ds(pl.multiple_of(k * SLOTS, SLOTS), SLOTS), :]

    def across(part):
        return is_end & (part // 8 != side)

    def f_spread(ex, field, buf, h):
        copy = ex[h][0]
        lanes = slice(256 * h, 256 * (h + 1))

        @pl.loop(0, 2)
        def _(step):
            @pl.when(jnp.logical_not(is_end & (step == 0)))
            def _():
                at = side_rows(step)
                buf[h, at, :] = nn(gmt[at, :], field[:, lanes]).astype(BF16)

                @pl.loop(0, 8)
                def _(k):
                    tgt = part_of(step, k)

                    @pl.when(tgt != me)
                    def _():
                        copy(tgt, me).start()

    def swap(i, h, field):
        return pltpu.make_async_remote_copy(
            src_ref=field.at[:, pl.ds(256 * h, 256)], dst_ref=far.at[2 * i + h],
            send_sem=fsem.at[0, 2 * i + h], recv_sem=fsem.at[1, 2 * i + h],
            device_id=space_dev(far_me), device_id_type=MESH,
        )

    def f_swap(i, h, field):
        @pl.when(is_end)
        def _():
            swap(i, h, field).start()

    def proxy_copy(i, h, recv, k, tgt):
        return pltpu.make_async_remote_copy(
            src_ref=slot_block(pick, 2 * i + h, k), dst_ref=slot_block(recv, h, far_me),
            send_sem=psem.at[2 * i + h, k], recv_sem=rsem.at[4 + 2 * i + h, far_me],
            device_id=space_dev(tgt), device_id_type=MESH,
        )

    def f_proxy(i, h, field, recv):
        @pl.when(is_end)
        def _():
            swap(i, h, field).wait_recv()

            pick[2 * i + h] = nn(gxt[...], far[2 * i + h]).astype(BF16)

            @pl.loop(0, 8)
            def _(j):
                tgt = part_of(1, j)

                @pl.when(tgt != me)
                def _():
                    proxy_copy(i, h, recv, tgt - side * 8, tgt).start()

            slot_block(recv, h, far_me)[...] = slot_block(pick, 2 * i + h, row_in_side)[...]

    def f_received(i, h, ex, recv, total):
        copy = ex[h][0]
        for half in range(2):
            for k in range(8):
                frm = 8 * half + k

                @pl.when((frm != me) & jnp.logical_not(is_end & (frm == far_me)))
                def _():
                    copy(lax.rem(me + 1, n_space), frm).wait_recv()

            at = slice(512 * half, 512 * (half + 1))
            total = total + nn(dm[:, 256 + 512 * half : 768 + 512 * half], recv[h, at, :])
        return total

    def f_sent(i, h, ex, field, recv):
        copy = ex[h][0]

        @pl.loop(1, n_space)
        def _(off):
            tgt = lax.rem(me + off, n_space)

            @pl.when(jnp.logical_not(across(tgt)))
            def _():
                copy(tgt, me).wait_send()

        @pl.when(is_end)
        def _():
            swap(i, h, field).wait_send()

            @pl.loop(0, 8)
            def _(k):
                @pl.when(k != row_in_side)
                def _():
                    proxy_copy(i, h, recv, k, side * 8 + k).wait_send()

    def collect_copy(i, h, send, rx, s, k):
        return pltpu.make_async_remote_copy(
            src_ref=slot_block(send, h, s), dst_ref=slot_block(rx, h, k),
            send_sem=ssem.at[2 * i + h, s], recv_sem=xsem.at[2 * i + h, k],
            device_id=space_dev(end_z * 4 + lax.rem(s, 4)), device_id_type=MESH,
        )

    def q_spread(i, ex, field, buf, rx, h, build=None):
        copy = ex[h][0]
        lanes = slice(256 * h, 256 * (h + 1))

        @pl.loop(0, 2)
        def _(step):
            if build is not None:
                build(lax.rem(side + 1 + step, 2))
            at = side_rows(step)
            buf[h, at, :] = nn(dmt[at, :], field[:, lanes]).astype(BF16)

            @pl.loop(0, 8)
            def _(k):
                tgt = part_of(step, k)
                to_far = lax.div(tgt, 4) == far_z

                @pl.when(jnp.logical_not(to_far) & (tgt != me))
                def _():
                    copy(tgt, me).start()

                @pl.when(to_far & (jnp.logical_not(is_end) | (tgt != far_me)))
                def _():
                    collect_copy(i, h, buf, rx, tgt, row_in_side).start()

        @pl.when(is_end)
        def _():
            slot_block(rx, h, row_in_side)[...] = slot_block(buf, h, far_me)[...]

    def back_field(i, h):
        return pltpu.make_async_remote_copy(
            src_ref=tsend.at[2 * i + h], dst_ref=tback.at[2 * i + h],
            send_sem=fsem.at[2, 2 * i + h], recv_sem=fsem.at[3, 2 * i + h],
            device_id=space_dev(far_me), device_id_type=MESH,
        )

    def q_collect(i, h, buf, rx):
        @pl.when(is_end)
        def _():
            @pl.loop(0, 8)
            def _(k):
                @pl.when(k != row_in_side)
                def _():
                    collect_copy(i, h, buf, rx, far_me, k).wait_recv()

            tsend[2 * i + h] = nn(gx[...], rx[h]).astype(BF16)
            back_field(i, h).start()

    def q_received(i, h, ex, recv, total):
        copy = ex[h][0]
        for half in range(2):
            for k in range(8):
                frm = 8 * half + k

                @pl.when((frm != me) & jnp.logical_not(across(frm)))
                def _():
                    copy(lax.rem(me + 1, n_space), frm).wait_recv()

            at = slice(512 * half, 512 * (half + 1))
            total = total + nn(gm[:, at], recv[h, at, :])

        @pl.when(is_end)
        def _():
            back_field(i, h).wait_recv()

        return total + tback[2 * i + h].astype(F32)

    def q_sent(i, h, ex, buf, rx):
        copy = ex[h][0]

        @pl.loop(1, n_space)
        def _(off):
            tgt = lax.rem(me + off, n_space)
            zz = lax.div(tgt, 4)

            @pl.when(zz != far_z)
            def _():
                copy(tgt, me).wait_send()

            @pl.when((zz == far_z) & (jnp.logical_not(is_end) | (tgt != far_me)))
            def _():
                collect_copy(i, h, buf, rx, tgt, row_in_side).wait_send()

        @pl.when(is_end)
        def _():
            back_field(i, h).wait_send()

    def meta_copy():
        return pltpu.make_async_remote_copy(
            src_ref=meta, dst_ref=metax, send_sem=nsem.at[4], recv_sem=nsem.at[5],
            device_id=space_dev(far_me), device_id_type=MESH,
        )

    def next_copy():
        return pltpu.make_async_remote_copy(
            src_ref=xall.at[pl.ds(512, 128), :], dst_ref=xb, send_sem=nsem.at[0], recv_sem=nsem.at[1],
            device_id={"tm": lax.rem(tm + 1, n_tm)}, device_id_type=MESH,
        )

    def back_copy():
        return pltpu.make_async_remote_copy(
            src_ref=bps, dst_ref=bpb, send_sem=nsem.at[2], recv_sem=nsem.at[3],
            device_id={"tm": lax.rem(tm + n_tm - 1, n_tm)}, device_id_type=MESH,
        )

    def tile_sum(r, b, own=False):
        total = None
        for k in range(4):
            slot = k if own else 4 + k
            hit = (cols_ref[r, slot] == b).astype(F32)
            term = adj_ref[r, slot].astype(F32) * hit
            total = term if total is None else total + term
        return total

    loads[0].wait()
    for p in range(4):
        gt[:, 128 * p : 128 * (p + 1)] = g_ref[128 * p : 128 * (p + 1), :].T
    loads[1].wait()

    def build(sd):
        for k in range(4):
            b = 4 * sd + k
            at = pl.ds(pl.multiple_of(b * 128, 128), 128)
            for r in range(2):
                tile = tile_sum(r, b + 2).astype(BF16)
                dm[128 * r : 128 * (r + 1), pl.ds(pl.multiple_of(256 + b * 128, 128), 128)] = tile
                dmt[at, 128 * r : 128 * (r + 1)] = tile.T

    loads[2].wait()
    pl.semaphore_wait(barrier, n_space - 1 + n_w - 1 + 4 + 1)

    @pl.when(tm < n_tm - 1)
    def _():
        next_copy().start()

    q_spread(0, q1, gt, sq1, rx1, 0, build)

    own_slots = pl.ds(pl.multiple_of(me * SLOTS, SLOTS), SLOTS)
    for ref in (rq1, rq2, rf1, rf2):
        for h in range(2):
            ref[h, own_slots, :] = jnp.zeros((SLOTS, 256), BF16)
    @pl.when(is_end)
    def _():
        for ref in (rq1, rq2):
            for h in range(2):
                ref[h, pl.ds(pl.multiple_of((1 - side) * 512, 512), 512), :] = jnp.zeros((512, 256), BF16)

    @pl.when(jnp.logical_not(is_end))
    def _():
        tback[...] = jnp.zeros_like(tback)

    for load in loads[3:]:
        load.wait()

    @pl.when(tm == 0)
    def _():
        xb[...] = jnp.zeros((128, 256), BF16)

    @pl.when(tm == n_tm - 1)
    def _():
        bpb[...] = jnp.zeros_like(bpb)

    zero = jnp.zeros((64, 64), F32)

    def pair(w):
        w = w.astype(F32)
        return jnp.concatenate([jnp.concatenate([w, zero], 1), jnp.concatenate([zero, w], 1)], 0)

    for k in range(3):
        block = pair(mixw_ref[k]).astype(BF16)
        mcat[:, 128 * k : 128 * (k + 1)] = block
        mcatv[128 * k : 128 * (k + 1), :] = block
    for half in range(2):
        for tap in range(2):
            block = pair(convw_ref[tap].astype(F32)[:, 64 * half : 64 * (half + 1)]).astype(BF16)
            wtt[128 * tap : 128 * (tap + 1), 128 * half : 128 * (half + 1)] = block
            wt[128 * half : 128 * (half + 1), 128 * tap : 128 * (tap + 1)] = block.T

    for p in range(4):
        xt[:, 128 * (p + 1) : 128 * (p + 2)] = x_ref[128 * p : 128 * (p + 1), :].T

    b = convb_ref[...]
    bias = jnp.concatenate([b[:, :64], b[:, :64], b[:, 64:], b[:, 64:]], 1)

    def conv(p):
        lanes = slice(128 * p, 128 * (p + 1))
        pre = nt(xt[:, 128 * p : 128 * p + 256], wt[...]) + bias
        f = jnp.tanh(pre[:, :128])
        s = jax.nn.sigmoid(pre[:, 128:])
        filt[:, lanes] = f
        gate[:, lanes] = s
        hid[:, lanes] = (f * s).astype(BF16)

    for p in (2, 3):
        conv(p)
    f_swap(0, 1, hid)
    slot = lax.broadcasted_iota(jnp.int32, (1, SLOTS), 1)
    for d in range(16):
        picks = jnp.where(slot < counts_ref[0, d], send_ref[d : d + 1, :], -1)
        meta[d : d + 1, :] = jnp.concatenate([picks, picks], 1)

    @pl.when(is_end)
    def _():
        meta_copy().start()

    q_spread(0, q1, gt, sq1, rx1, 1)
    conv(1)

    sensor = lax.broadcasted_iota(jnp.int32, (256, 128), 0)
    low_row = lax.broadcasted_iota(jnp.int32, (1, 128), 1) < 64

    def select(first, second):
        return (sensor == jnp.where(low_row, first, second)).astype(F32).astype(BF16)

    for m in range(8):
        sel = select(meta[2 * m : 2 * m + 1, :], meta[2 * m + 1 : 2 * m + 2, :])
        gm[:, 128 * m : 128 * (m + 1)] = sel
        gmt[128 * m : 128 * (m + 1), :] = sel.T

    f_spread(f1, hid, sf1, 1)

    @pl.when(tm > 0)
    def _():
        next_copy().wait_recv()

    xt[:, 0:128] = xb[...].T
    conv(0)
    f_swap(0, 0, hid)

    for b in range(2):
        for r in range(2):
            total = tile_sum(r, b, True)
            high = total.astype(BF16)
            low = (total - high.astype(F32)).astype(BF16)
            here = slice(128 * r, 128 * (r + 1)), slice(128 * b, 128 * (b + 1))
            dm[here] = high
            dlo[here] = low
            dlot[128 * b : 128 * (b + 1), 128 * r : 128 * (r + 1)] = high.T
            dlot[128 * b : 128 * (b + 1), 256 + 128 * r : 256 + 128 * (r + 1)] = low.T

    @pl.when(is_end)
    def _():
        meta_copy().wait_recv()
        for m in range(4):
            d = side * 8 + 2 * m
            sel = select(metax[pl.ds(d, 1), :], metax[pl.ds(d + 1, 1), :])
            gx[:, 128 * m : 128 * (m + 1)] = sel
            gxt[128 * m : 128 * (m + 1), :] = sel.T

    def own_back(field, h):
        grad = field[:, 256 * h : 256 * (h + 1)]
        return nn(dlot[:, :256], grad) + nn(dlot[:, 256:], grad)

    q_collect(0, 0, sq1, rx1)
    f_proxy(0, 1, hid, rf1)
    q_collect(0, 1, sq1, rx1)
    for h in range(2):
        own = own_back(gt, h)
        qg[:, 256 * h : 256 * (h + 1)] = q_received(0, h, q1, rq1, own).astype(BF16)
        q_spread(1, q2, qg, sq2, rx2, h)
        if h == 0:
            f_spread(f1, hid, sf1, 0)

    def hop(i, h, ex, src, dst, recv):
        lanes = slice(256 * h, 256 * (h + 1))
        field = src[:, lanes]
        own = nn(dm[:, :256], field) + nn(dlo[...], field)
        dst[:, lanes] = f_received(i, h, ex, recv, own).astype(BF16)

    f_proxy(0, 0, hid, rf1)
    for p in range(4):
        lanes = slice(128 * p, 128 * (p + 1))
        hidn[lanes, :] = hid[:, lanes].T
    gsum = jnp.zeros((1, 128), F32)
    for p in range(4):
        gsum = gsum + jnp.sum(gt[:, 128 * p : 128 * (p + 1)].astype(F32), axis=0, keepdims=True)
    hop(0, 1, f1, hid, hop1, rf1)
    f_swap(1, 1, hop1)
    f_spread(f2, hop1, sf2, 1)
    for h in range(2):
        q_collect(1, h, sq2, rx2)

    low_lanes = lax.broadcasted_iota(jnp.int32, (64, 128), 1) < 64

    def diag_low(a):
        return a[:64] + pltpu.roll(a[64:], 64, 1)

    def diag_high(a):
        return pltpu.roll(a[:64], 64, 1) + a[64:]

    bsum = jnp.zeros((1, 256), F32)
    accs = [None] * 2

    def add(i, term):
        accs[i] = term if accs[i] is None else accs[i] + term

    for h in range(2):
        own = own_back(qg, h)
        qqg[:, 256 * h : 256 * (h + 1)] = q_received(1, h, q2, rq2, own).astype(BF16)
        for p in (2 * h, 2 * h + 1):
            lanes = slice(128 * p, 128 * (p + 1))
            three = jnp.concatenate([gt[:, lanes], qg[:, lanes], qqg[:, lanes]], 1)
            bh = nn(three, mcatv[...])
            f = filt[:, lanes]
            s = gate[:, lanes]
            gf = (bh * (1.0 - f * f) * s).astype(BF16)
            gg = (bh * f * s * (1.0 - s)).astype(BF16)
            bp[:, 256 * p : 256 * p + 128] = gf
            bp[:, 256 * p + 128 : 256 * (p + 1)] = gg
            if p == 0:
                bps[...] = nt(wtt[:128, :], bp[:, :256]).astype(BF16)

                @pl.when(tm > 0)
                def _():
                    back_copy().start()
            bsum = bsum + jnp.concatenate(
                [
                    jnp.sum(gf.astype(F32), axis=0, keepdims=True),
                    jnp.sum(gg.astype(F32), axis=0, keepdims=True),
                ],
                1,
            )
            add(0, nn(hidn[lanes, :], three))
            add(1, nn(xall[128 * p : 128 * p + 256, :], bp[:, 256 * p : 256 * (p + 1)]))
        if h == 0:
            f_proxy(1, 1, hop1, rf2)
    row = lax.broadcasted_iota(jnp.int32, (64, 128), 0)
    f_sum = bsum[:, :128]
    g_sum = bsum[:, 128:]
    f_sum = f_sum + pltpu.roll(f_sum, 64, 1)
    g_sum = g_sum + pltpu.roll(g_sum, 64, 1)
    o_sum = gsum + pltpu.roll(gsum, 64, 1)
    extra = jnp.where(row == 0, f_sum, jnp.where(row == 1, g_sum, jnp.where(row == 2, o_sum, 0.0)))
    pay[0:64, :] = jnp.where(low_lanes, diag_low(accs[0][:, :128]), diag_high(accs[0][:, 128:256]))
    pay[64:128, :] = jnp.where(low_lanes, diag_low(accs[0][:, 256:]), extra)
    for tap in range(2):
        acc = accs[1][128 * tap : 128 * (tap + 1)]
        pay[128 + 64 * tap : 192 + 64 * tap, :] = jnp.where(
            low_lanes, diag_low(acc[:, :128]), diag_high(acc[:, 128:])
        )

    s1 = exchange(w, n_w, w_dev, rows(pay, 8), rows(ra, 8), assem.at[0], arsem.at[0])
    s2 = exchange(q, 8, q_dev, lambda k: sum_b, rows(rc, 8), assem.at[1], arsem.at[1])
    s3 = exchange(w, n_w, w_dev, lambda k: sum_c, rows(fin, 8), assem.at[2], arsem.at[2])

    def total_of(ref, count, size):
        total = ref[0:size, :]
        for k in range(1, count):
            total = total + ref[size * k : size * (k + 1), :]
        return total

    def place(k, size):
        return pl.ds(pl.multiple_of(k * size, size), size)

    ra[place(w, 8), :] = pay[place(w, 8), :]
    s1[1]()

    def grad_in(p):
        lanes = slice(128 * p, 128 * (p + 1))
        if p < 3:
            here = nt(jnp.concatenate([wtt[128:, :], wtt[:128, :]], 1), bp[:, 256 * p : 256 * p + 512])
        else:
            here = nt(wtt[128:, :], bp[:, 768:]) + bpb[...].astype(F32)
        gin_ref[lanes, :] = (g_ref[lanes, :].astype(F32) + here).astype(BF16)

    mb = mixb_ref[...]
    mb = jnp.broadcast_to(jnp.concatenate([mb, mb], 1), (128, 128)).T
    mb = jnp.concatenate([mb, mb], 1)

    def mixed(p, last):
        lanes = slice(128 * p, 128 * (p + 1))
        if last:
            here = nt(mcat[:, 256:], hop2[:, lanes])
            out_ref[lanes, :] = (part[lanes, :] + here).astype(BF16)
        else:
            here = nt(mcat[:, :256], jnp.concatenate([hid[:, lanes], hop1[:, lanes]], 1))
            part[lanes, :] = x_ref[lanes, :].astype(F32) + mb + here

    hop(0, 0, f1, hid, hop1, rf1)
    f_swap(1, 0, hop1)
    s1[2]()
    total = total_of(ra, n_w, 8)
    sum_b[...] = total
    rc[place(q, 8), :] = total
    s2[1]()
    f_spread(f2, hop1, sf2, 0)
    for p in range(3):
        grad_in(p)
    s2[2]()
    total = total_of(rc, 8, 8) * scale
    sum_c[...] = total
    fin[place(w, 8), :] = total
    s3[1]()
    f_proxy(1, 0, hop1, rf2)
    for p in range(4):
        mixed(p, False)

    @pl.when(tm < n_tm - 1)
    def _():
        back_copy().wait_recv()

    grad_in(3)
    stores[0].start()
    for h in range(2):
        q_sent(0, h, q1, sq1, rx1)
        q_sent(1, h, q2, sq2, rx2)
        f_sent(0, h, f1, hid, rf1)
    s1[3]()
    s2[3]()

    @pl.when(is_end)
    def _():
        meta_copy().wait_send()

    @pl.when(tm < n_tm - 1)
    def _():
        next_copy().wait_send()

    @pl.when(tm > 0)
    def _():
        back_copy().wait_send()

    for h in (1, 0):
        hop(1, h, f2, hop1, hop2, rf2)
        mixed(2 * h, True)
        mixed(2 * h + 1, True)
        stores[1 + h].start()
    s3[2]()
    stores[3].start()
    s3[3]()
    for h in range(2):
        f_sent(1, h, f2, hop1, rf2)
    for store in stores:
        store.wait()


def finish(out_in, gin_in, fin, out_ref, gin_ref, gcw_ref, gcb_ref, gmw_ref, gmb_ref):
    out_ref[...] = out_in[...]
    gin_ref[...] = gin_in[...]
    two = fin[0:64, :].T
    gmw_ref[0] = two[0:64]
    gmw_ref[1] = two[64:128]
    gmw_ref[2] = fin[64:128, :].T[0:64]
    for tap in range(2):
        gcw_ref[tap] = fin[128 + 64 * tap : 192 + 64 * tap, :]
    tail = fin[64:72, :]
    low = lax.broadcasted_iota(jnp.int32, (1, 128), 1) < 64
    gcb_ref[...] = jnp.where(low, pltpu.roll(tail[0:1], 64, 1), tail[1:2])
    gmb_ref[...] = pltpu.roll(tail[2:3], 64, 1)[:, 0:64]


def body(dims, inputs, grad_out, conv_w, conv_b, mix_w, mix_b, adj_tiles, tile_cols, send_rows, counts):
    x = inputs.reshape(512, 256)
    g = grad_out.reshape(512, 256)
    vmem = pl.BlockSpec(memory_space=pltpu.VMEM)
    smem = pl.BlockSpec(memory_space=pltpu.SMEM)
    hbm = pl.BlockSpec(memory_space=pltpu.HBM)
    n_space = dims[0]
    n_e = dims[1] * 2

    def bf(*shape):
        return pltpu.VMEM(shape, BF16)

    def fl(*shape):
        return pltpu.VMEM(shape, F32)

    def dma(*shape):
        return pltpu.SemaphoreType.DMA(shape)

    scratch = [
        bf(512, 256), bf(512, 256), fl(256, 128),
        bf(640, 256), bf(512, 256), bf(2, 8, 128, 128), bf(2, 64, 128), fl(1, 128), bf(3, 64, 64), fl(1, 64),
        pltpu.VMEM((16, SLOTS), jnp.int32), bf(128, 256), bf(128, 256), bf(256, 640), bf(256, 512),
        bf(256, 256), bf(256, 256), bf(128, 384), bf(384, 128),
        bf(256, 1024), bf(1024, 256), bf(256, 1280), bf(1024, 256), bf(256, 256), bf(256, 512),
        bf(256, 512), bf(256, 512), fl(256, 512), fl(256, 512), bf(256, 512), bf(512, 256),
        bf(256, 512), bf(256, 512), bf(256, 1024), fl(512, 256),
    ]
    scratch += [bf(2, 1024, 256)] * 8
    scratch += [fl(256, 128), fl(256, 128), fl(64, 128), fl(8, 128), fl(8, 128)]
    ints = pltpu.VMEM((16, 128), jnp.int32)
    scratch += [ints, ints, bf(256, 512), bf(512, 256), bf(4, 256, 256), bf(4, 512, 256), bf(2, 512, 256), bf(2, 512, 256)]
    scratch += [bf(4, 256, 256), bf(4, 256, 256)]
    scratch += [dma(8, n_space), dma(8, n_space), dma(3, 4 * n_e), dma(3, 4 * n_e), dma(6), dma(8)]
    scratch += [dma(4, 4), dma(4, 8), dma(4, 8), dma(4)]
    out, gin, fin = pl.pallas_call(
        functools.partial(kernel, dims),
        out_shape=(
            jax.ShapeDtypeStruct((512, 256), BF16),
            jax.ShapeDtypeStruct((512, 256), BF16),
            jax.ShapeDtypeStruct((256, 128), F32),
        ),
        in_specs=[hbm] * 8 + [smem] * 2,
        out_specs=(hbm,) * 3,
        scratch_shapes=scratch,
        compiler_params=pltpu.CompilerParams(
            collective_id=0, has_side_effects=True, vmem_limit_bytes=60 * 2**20
        ),
    )(
        x, g, adj_tiles, jnp.swapaxes(conv_w, 1, 2), conv_b.reshape(1, 128), mix_w, mix_b.reshape(1, 64),
        send_rows[0], tile_cols, counts,
    )
    out, gin, gcw, gcb, gmw, gmb = pl.pallas_call(
        finish,
        out_shape=(
            jax.ShapeDtypeStruct((512, 256), BF16),
            jax.ShapeDtypeStruct((512, 256), BF16),
            jax.ShapeDtypeStruct((2, 64, 128), F32),
            jax.ShapeDtypeStruct((1, 128), F32),
            jax.ShapeDtypeStruct((3, 64, 64), F32),
            jax.ShapeDtypeStruct((1, 64), F32),
        ),
        in_specs=[vmem] * 3,
        out_specs=(vmem,) * 6,
    )(out, gin, fin)
    return (
        out.reshape(inputs.shape),
        gin.reshape(inputs.shape),
        jnp.swapaxes(gcw, 1, 2),
        gcb.reshape(128),
        gmw,
        gmb.reshape(64),
    )


def solution(mesh):
    in_specs = (
        P("dp", "tm", None, "space"),
        P("dp", "tm", None, "space"),
        P(),
        P(),
        P(),
        P(),
        P("space", None, None, None),
        P("space", None),
        P("space", None, None),
        P("space", None),
    )
    out_specs = (P("dp", "tm", None, "space"), P("dp", "tm", None, "space"), P(), P(), P(), P())
    cells = 8 * 256 * mesh.shape["dp"] * mesh.shape["space"] * mesh.shape["tm"]
    dims = (mesh.shape["space"], mesh.shape["dp"], mesh.shape["tm"], 1.0 / math.sqrt(cells))
    return jax.shard_map(
        functools.partial(body, dims), mesh=mesh, in_specs=in_specs, out_specs=out_specs, check_vma=False
    )
```
